32 devices in a mesh: dp: 4 (over y, x), fsdp: 8 (over z, core).
Axes of the slice: x: 2, y: 2, z: 4, core: 2. Of those that a mesh axis runs over, the one named last changes fastest.
Arguments:
- tokens: bfloat16 [16384, 768], P(('dp', 'fsdp')), may hold values from -6 to 6
- in_weight: bfloat16 [768, 2304], P('fsdp'), may hold values from -0.21875 to 0.21875
- in_bias: bfloat16 [1536], P('fsdp'), may hold values from -1.75 to 1.75
- mix_weight: bfloat16 [768, 768], P('fsdp'), may hold values from -2.5 to 2.5
- mix_bias: bfloat16 [768], P('fsdp'), may hold values from -1.75 to 1.75
- first_gain: bfloat16 [768], P('fsdp'), may hold values from 0.5 to 1.5
- first_shift: bfloat16 [768], P('fsdp'), may hold values from -1.75 to 1.75
- up_weight: bfloat16 [768, 3072], P('fsdp'), may hold values from -0.21875 to 0.21875
- up_bias: bfloat16 [3072], P('fsdp'), may hold values from -3 to 3
- down_weight: bfloat16 [3072, 768], P('fsdp'), may hold values from -0.109375 to 0.109375
- down_bias: bfloat16 [768], P('fsdp'), may hold values from -1.75 to 1.75
- second_gain: bfloat16 [768], P('fsdp'), may hold values from 0.5 to 1.5
- second_shift: bfloat16 [768], P('fsdp'), may hold values from -1.75 to 1.75
- pool_weight: bfloat16 [768, 768], P('fsdp'), may hold values from -0.21875 to 0.21875
- pool_bias: bfloat16 [768], P('fsdp'), may hold values from -3 to 3
- class_weight: bfloat16 [768, 3], P('fsdp'), may hold values from -0.625 to 0.625
- class_bias: bfloat16 [3], replicated, may hold values from -3 to 3
- lengths: int32 [32], P(('dp', 'fsdp')), may hold values from 1 to 512, 10240 in all
- labels: int32 [32], P(('dp', 'fsdp')), may hold values from 0 to 2
- cotangent: bfloat16 [16384, 768], P(('dp', 'fsdp')), may hold values from -6 to 6
Outputs:
- layer_out: bfloat16 [16384, 768], P(('dp', 'fsdp'))
- input_grad: float32 [16384, 768], P(('dp', 'fsdp'))
- grad_in_weight: float32 [768, 2304], P('fsdp')
- grad_in_bias: float32 [1536], P('fsdp')
- grad_mix_weight: float32 [768, 768], P('fsdp')
- grad_mix_bias: float32 [768], P('fsdp')
- grad_first_gain: float32 [768], P('fsdp')
- grad_first_shift: float32 [768], P('fsdp')
- grad_up_weight: float32 [768, 3072], P('fsdp')
- grad_up_bias: float32 [3072], P('fsdp')
- grad_down_weight: float32 [3072, 768], P('fsdp')
- grad_down_bias: float32 [768], P('fsdp')
- grad_second_gain: float32 [768], P('fsdp')
- grad_second_shift: float32 [768], P('fsdp')
- grad_pool_weight: float32 [768, 768], P('fsdp')
- grad_pool_bias: float32 [768], P('fsdp')
- grad_class_weight: float32 [768, 3], P('fsdp')
- grad_class_bias: float32 [3], replicated
The draws below stay inside these ranges and needn't reach their ends.
Inputs may be any that keep to these rules, and one draw needn't show every extreme that they name: `lengths`: tokens of a sequence at positions at or past its length are padding; some sequence has exactly 512.
All inputs are finite; a program needn't handle non-finite values. No bound on the sum of `lengths` on one device may be relied on, other than what follows from the above.
Results may differ from the reference program's by a relative error of at most 0.017.
Values may be sent and summed in bfloat16 or wider, within the bound.
A program may use at most 128 MiB of HBM per device.

```python
import math
import jax
import jax.numpy as jnp
import numpy as np
from jax import lax

D = 768
H = 12
DH = 64
FF = 3072
CLASSES = 3
SEQ = 512
SEQS = 32
TOKENS = 16384


def set_ends(array, rng, smallest, largest):
    longest = array.shape.index(max(array.shape))
    spots = []
    for shift in (0, 1):
        where = [jax.random.randint(jax.random.fold_in(rng, axis), (), 0, length) for axis, length in enumerate(array.shape)]
        where[longest] = (where[longest] + shift) % array.shape[longest]
        spots.append(tuple(where))
    return array.at[spots[0]].set(smallest).at[spots[1]].set(largest)


def block_scale(own_key, shape, split, least, top_value):
    factor_of = 1.0
    for dim, blocks in split:
        heights = jax.random.uniform(jax.random.fold_in(jax.random.fold_in(own_key, 6), dim), (blocks,), jnp.float32, least / len(split), top_value / len(split))
        factor_of = factor_of * jnp.repeat(jnp.exp(heights), shape[dim] // blocks).reshape((-1,) + (1,) * (len(shape) - 1 - dim))
    return factor_of


def profile(count, total, limit, slope):
    weights = [(1 << 20) // math.isqrt(rank ** slope) + 1 for rank in range(2, count + 1)]
    surplus, given = total - limit - (count - 1), [1] * (count - 1)
    while surplus > 0:
        free = [i for i in range(count - 1) if given[i] < limit]
        mass, remaining = sum([weights[i] for i in free]), surplus
        for i in free:
            more = min(limit - given[i], max(1, remaining * weights[i] // mass), surplus)
            given[i] = given[i] + more
            surplus = surplus - more
    return np.array([limit] + given)


def uneven(own_key, count, total, reach, slope):
    if count == 2:
        one = jax.random.randint(own_key, (), max(1, total - reach), min(reach, total - 1) + 1)
        return jnp.stack([one, total - one])
    sizes = jnp.asarray(profile(count, total, reach, slope), jnp.int32)
    couples = (count - 1) // 2
    source_of, sink = sizes[1:1 + 2 * couples:2], sizes[2:2 + 2 * couples:2]
    room = jnp.minimum(source_of - 1, reach - sink)
    shifted = jax.random.randint(jax.random.fold_in(own_key, 1), (couples,), 0, 1 << 20) % (room + 1)
    sizes = sizes.at[1:1 + 2 * couples:2].set(source_of - shifted).at[2:2 + 2 * couples:2].set(sink + shifted)
    return sizes[jax.random.permutation(jax.random.fold_in(own_key, 2), count)]


def normal_values(own_key, shape, scale, reach, cuts=(), held_as=jnp.bfloat16):
    entries = scale * jax.random.normal(own_key, shape, jnp.float32)
    if cuts:
        entries = entries * block_scale(own_key, shape, cuts, -0.22, 0.18)
    return jnp.clip(entries, -reach, reach).astype(held_as)


def setup_inputs(seed: int = 0) -> dict:
    seeds = jax.random.split(jax.random.key(seed), 21)
    return {
        "tokens": normal_values(seeds[0], (TOKENS, D), 1.0, 6.0, ((0, 32),)),
        "in_weight": normal_values(seeds[1], (D, 3 * D), D ** -0.5, 0.21875, ((0, 8),)),
        "in_bias": normal_values(seeds[2], (2 * D,), 0.3, 1.75, ((0, 8),)),
        "mix_weight": normal_values(seeds[3], (D, D), (max(D // 128, 1)) ** -0.5, 2.5, ((0, 8),)),
        "mix_bias": normal_values(seeds[4], (D,), 0.3, 1.75, ((0, 8),)),
        "first_gain": jnp.clip(1.0 + 0.1 * jax.random.normal(seeds[5], (D,), jnp.float32), 0.5, 1.5).astype(jnp.bfloat16),
        "first_shift": normal_values(seeds[6], (D,), 0.3, 1.75, ((0, 8),)),
        "up_weight": normal_values(seeds[7], (D, FF), D ** -0.5, 0.21875, ((0, 8),)),
        "up_bias": normal_values(seeds[8], (FF,), 0.5, 3.0, ((0, 8),)),
        "down_weight": normal_values(seeds[9], (FF, D), FF ** -0.5, 0.109375, ((0, 8),)),
        "down_bias": normal_values(seeds[10], (D,), 0.3, 1.75, ((0, 8),)),
        "second_gain": jnp.clip(1.0 + 0.1 * jax.random.normal(seeds[11], (D,), jnp.float32), 0.5, 1.5).astype(jnp.bfloat16),
        "second_shift": normal_values(seeds[12], (D,), 0.3, 1.75, ((0, 8),)),
        "pool_weight": normal_values(seeds[13], (D, D), D ** -0.5, 0.21875, ((0, 8),)),
        "pool_bias": normal_values(seeds[14], (D,), 0.5, 3.0, ((0, 8),)),
        "class_weight": normal_values(seeds[15], (D, CLASSES), (max(D // 8, 1)) ** -0.5, 0.625, ((0, 8),)),
        "class_bias": normal_values(seeds[16], (CLASSES,), 0.5, 3.0),
        "lengths": uneven(seeds[17], SEQS, SEQS * SEQ * 5 // 8, SEQ, 2).astype(jnp.int32),
        "labels": set_ends(jax.random.randint(seeds[18], (SEQS,), 0, CLASSES), jax.random.fold_in(seeds[18], 1), 0, CLASSES - 1).astype(jnp.int32),
        "cotangent": normal_values(seeds[19], (TOKENS, D), 1.0, 6.0, ((0, 32),)),
    }


@jax.custom_vjp
def low(v):
    return lax.optimization_barrier(v.astype(jnp.bfloat16)).astype(jnp.float32)

@jax.custom_vjp
def low_back(v):
    return v

def low_keep(v):
    return (low(v), None)

def low_pass(kept, grad):
    return (grad,)

def back_keep(v):
    return (v, None)

def back_low(kept, grad):
    return (low(grad),)
low.defvjp(low_keep, low_pass)
low_back.defvjp(back_keep, back_low)
EPSILON = 1e-06

def product(left_side, right_side):
    return jnp.dot(left_side, right_side, precision=lax.Precision.HIGHEST)

def layer_norm(vector, norm_gain, norm_shift):
    average = lax.optimization_barrier(jnp.mean(vector, axis=-1, keepdims=True))
    centered = vector - average
    inverse = lax.rsqrt(lax.optimization_barrier(jnp.mean(centered * centered, axis=-1, keepdims=True)) + EPSILON)
    return centered * inverse * norm_gain + norm_shift

def group_terms(params, block_tokens, block_cot, block_lengths, block_labels):
    in_weight, in_bias, mix_weight, mix_bias, first_gain, first_shift, up_weight, up_bias, down_weight, down_bias, second_gain, second_shift, pool_weight, pool_bias, class_weight, class_bias = params
    seq_count = block_lengths.shape[0]
    token_rows = block_tokens.shape[0]
    score_scale = 1.0 / math.sqrt(DH)
    projected = product(low(block_tokens), in_weight)
    queries = low(low_back(projected[:, :D] + in_bias[:D]))
    keys_all = low(low_back(projected[:, D:2 * D]))
    values_all = low(low_back(projected[:, 2 * D:] + in_bias[D:]))
    positions = jnp.arange(SEQ)

    def attend(block_items):
        query_blk, key_blk, value_blk, length = block_items
        scores = low_back(jnp.einsum('qhd,khd->hqk', query_blk, key_blk, precision=lax.Precision.HIGHEST) * score_scale)
        scores = jnp.where(positions[None, None, :] < length, scores, -1e+30)
        softmaxed = low(jax.nn.softmax(scores, axis=-1))
        return jnp.einsum('hqk,khd->qhd', softmaxed, value_blk, precision=lax.Precision.HIGHEST)
    attended = lax.map(jax.checkpoint(attend), (queries.reshape(seq_count, SEQ, H, DH), keys_all.reshape(seq_count, SEQ, H, DH), values_all.reshape(seq_count, SEQ, H, DH), block_lengths))
    attn_low = low(low_back(attended.reshape(token_rows, D)))
    branch = low_back(product(attn_low, mix_weight) + mix_bias)
    first_norm = layer_norm(block_tokens + branch, first_gain, first_shift)
    pre_act = low_back(product(low(first_norm), up_weight) + up_bias)
    ffn_out = low_back(product(low(jax.nn.gelu(pre_act, approximate=False)), down_weight) + down_bias)
    result = layer_norm(first_norm + ffn_out, second_gain, second_shift)
    first_rows = result.reshape(seq_count, SEQ, D)[:, 0, :]
    pooled = jnp.tanh(low_back(product(low(first_rows), pool_weight) + pool_bias))
    logits = low_back(product(low(pooled), class_weight) + class_bias)
    live_mask = (positions[None, :] < block_lengths[:, None]).reshape(token_rows).astype(jnp.float32)
    onehot = jax.nn.one_hot(block_labels, CLASSES, dtype=jnp.float32)
    losses = jax.nn.logsumexp(logits, axis=-1) - lax.optimization_barrier(jnp.sum(logits * onehot, axis=-1))
    total_sum = jnp.sum(result * block_cot * live_mask[:, None]) + jnp.sum(losses)
    return (total_sum, result)

def reference(tokens, in_weight, in_bias, mix_weight, mix_bias, first_gain, first_shift, up_weight, up_bias, down_weight, down_bias, second_gain, second_shift, pool_weight, pool_bias, class_weight, class_bias, lengths, labels, cotangent):
    params = (in_weight.astype(jnp.float32), in_bias.astype(jnp.float32), mix_weight.astype(jnp.float32), mix_bias.astype(jnp.float32), first_gain.astype(jnp.float32), first_shift.astype(jnp.float32), up_weight.astype(jnp.float32), up_bias.astype(jnp.float32), down_weight.astype(jnp.float32), down_bias.astype(jnp.float32), second_gain.astype(jnp.float32), second_shift.astype(jnp.float32), pool_weight.astype(jnp.float32), pool_bias.astype(jnp.float32), class_weight.astype(jnp.float32), class_bias.astype(jnp.float32))
    per_group = math.gcd(SEQS, max(1, 4096 // SEQ))
    groups = SEQS // per_group
    block_rows = per_group * SEQ
    cot_all = cotangent.astype(jnp.float32).reshape(groups, block_rows, D)
    length_all = lengths.reshape(groups, per_group)
    label_all = labels.reshape(groups, per_group)

    def objective(weights, token_values):

        def scan_step(running, block_items):
            part_tokens, part_cot, part_lengths, part_labels = block_items
            term, part_result = jax.checkpoint(group_terms)(weights, part_tokens, part_cot, part_lengths, part_labels)
            return (running + term, part_result)
        total_sum, results = lax.scan(scan_step, jnp.zeros((), jnp.float32), (token_values.reshape(groups, block_rows, D), cot_all, length_all, label_all))
        return (total_sum, results.reshape(TOKENS, D))
    total_sum, pullback, result = jax.vjp(objective, params, tokens.astype(jnp.float32), has_aux=True)
    weight_grads, token_grad = pullback(jnp.ones_like(total_sum))
    return (result.astype(jnp.bfloat16), token_grad, weight_grads[0], weight_grads[1], weight_grads[2], weight_grads[3], weight_grads[4], weight_grads[5], weight_grads[6], weight_grads[7], weight_grads[8], weight_grads[9], weight_grads[10], weight_grads[11], weight_grads[12], weight_grads[13], weight_grads[14], weight_grads[15])
```

```python
import functools
from functools import partial
import math

import jax
import jax.numpy as jnp
from jax import lax
from jax.experimental import pallas as pl
from jax.experimental.pallas import tpu as pltpu
from jax.sharding import PartitionSpec as P

H = 12
DH = 64


EPSILON = 1e-06


def norm_fore(vector, norm_gain, norm_shift):
    average = jnp.mean(vector, axis=-1, keepdims=True)
    centered = vector - average
    inverse = lax.rsqrt(jnp.mean(centered * centered, axis=-1, keepdims=True) + EPSILON)
    normed = centered * inverse
    return (normed * norm_gain + norm_shift, normed, inverse)


def norm_back(gradient, normed, inverse, norm_gain):
    scaled = gradient * norm_gain
    inner_mean = jnp.mean(scaled, axis=-1, keepdims=True)
    cross_mean = jnp.mean(scaled * normed, axis=-1, keepdims=True)
    input_part = inverse * (scaled - inner_mean - normed * cross_mean)
    return (input_part, jnp.sum(gradient * normed, axis=0), jnp.sum(gradient, axis=0))


def column_sums(matrix):
    return jnp.sum(matrix.astype(jnp.float32), axis=0)


MESH = pl.DeviceIdType.MESH


def remote(src, dst, send_sem, recv_sem, target):
    return pltpu.make_async_remote_copy(
        src_ref=src, dst_ref=dst, send_sem=send_sem, recv_sem=recv_sem, device_id=target, device_id_type=MESH
    )


class Place:
    def __init__(self, fsdp_size):
        self.dp = lax.axis_index("dp")
        self.shard = lax.axis_index("fsdp")
        self.line = fsdp_size // 2
        self.row_half, self.col_half = self.dp // 2, lax.rem(self.dp, 2)
        self.spot, self.core = self.shard // 2, lax.rem(self.shard, 2)
        across = 2 * self.row_half + (1 - self.col_half)
        along = 2 * (1 - self.row_half) + self.col_half
        self.first = jnp.where(self.core == 0, across, along)
        self.second = jnp.where(self.core == 0, along, across)

    def partner(self):
        return {"dp": self.dp, "fsdp": 2 * self.spot + 1 - self.core}

    def on_line(self, hop):
        return {"dp": self.dp, "fsdp": 2 * lax.rem(self.spot + hop, self.line) + self.core}

    def in_plane(self, dp):
        return {"dp": dp, "fsdp": self.shard}

    def source_spot(self, hop):
        return lax.rem(self.spot + self.line - hop, self.line)

    def peers(self):
        return (
            [self.partner()]
            + [self.on_line(hop) for hop in range(1, self.line)]
            + [self.in_plane(lax.rem(self.dp + step, 4)) for step in range(1, 4)]
        )

    def meet(self):
        barrier = pltpu.get_barrier_semaphore()
        peers = self.peers()
        for peer in peers:
            pl.semaphore_signal(barrier, inc=1, device_id=peer, device_id_type=MESH)
        pl.semaphore_wait(barrier, len(peers))


class Gather:
    def __init__(self, place, shard_ref, whole_ref, send_sems, recv_sems):
        self.place, self.shard_ref, self.whole = place, shard_ref, whole_ref
        self.send_sems, self.recv_sems = send_sems, recv_sems
        self.rows, self.cols = shard_ref.shape
        self.hops = place.line - 1
        self.started = []

    @staticmethod
    def sems(line):
        return 5 * (line - 1) + 2

    def block(self, shard):
        return self.whole.at[shard // 2, lax.rem(shard, 2)]

    def quarter(self, shard, row_half, col_half):
        half_rows, half_cols = self.rows // 2, self.cols // 2
        return self.whole.at[
            shard // 2,
            lax.rem(shard, 2),
            pl.ds(pl.multiple_of(row_half * half_rows, 16), half_rows),
            pl.ds(pl.multiple_of(col_half * half_cols, 128), half_cols),
        ]

    def go(self, index, src, dst, target):
        copy = remote(src, dst, self.send_sems.at[index], self.recv_sems.at[index], target)
        copy.start()
        self.started.append(copy)

    def arrived(self, index, dst):
        remote(dst, dst, self.send_sems.at[index], self.recv_sems.at[index], self.place.partner()).wait_recv()

    def begin(self):
        p = self.place
        half_rows, half_cols = self.rows // 2, self.cols // 2
        piece = self.shard_ref.at[
            pl.ds(pl.multiple_of(p.row_half * half_rows, 16), half_rows),
            pl.ds(pl.multiple_of(p.col_half * half_cols, 128), half_cols),
        ]
        for hop in range(1, p.line):
            self.go(hop - 1, piece, self.quarter(p.shard, p.row_half, p.col_half), p.on_line(hop))
        self.go(4 * self.hops, self.shard_ref, self.block(p.shard), p.partner())
        self.own = pltpu.make_async_copy(self.shard_ref, self.block(p.shard), self.recv_sems.at[5 * self.hops + 1])
        self.own.start()

    def source(self, hop):
        return 2 * self.place.source_spot(hop) + self.place.core

    def spread(self, hop):
        p = self.place
        quarter = self.quarter(self.source(hop), p.row_half, p.col_half)
        self.arrived(hop - 1, quarter)
        self.go(self.hops + hop - 1, quarter, quarter, p.in_plane(p.first))
        self.go(2 * self.hops + hop - 1, quarter, quarter, p.in_plane(p.second))

    def relay(self, hop):
        p = self.place
        quarter = self.quarter(self.source(hop), p.first // 2, lax.rem(p.first, 2))
        self.arrived(self.hops + hop - 1, quarter)
        self.go(3 * self.hops + hop - 1, quarter, quarter, p.in_plane(p.second))

    def hand(self, hop):
        p = self.place
        self.arrived(2 * self.hops + hop - 1, self.quarter(self.source(hop), p.second // 2, lax.rem(p.second, 2)))
        self.arrived(3 * self.hops + hop - 1, self.quarter(self.source(hop), 1 - p.row_half, 1 - p.col_half))
        block = self.block(self.source(hop))
        self.go(4 * self.hops + hop, block, block, p.partner())

    def ready(self):
        p = self.place
        self.own.wait()
        self.arrived(4 * self.hops, self.block(p.shard + 1 - 2 * p.core))
        for hop in range(1, p.line):
            self.arrived(4 * self.hops + hop, self.block(2 * p.source_spot(hop) + 1 - p.core))

    def end(self):
        for copy in self.started:
            copy.wait_send()


class SmallGather:
    def __init__(self, place, own_ref, all_ref, send_sems, recv_sems):
        self.place, self.own_ref, self.all = place, own_ref, all_ref
        self.send_sems, self.recv_sems = send_sems, recv_sems
        self.hops = place.line - 1
        self.started = []

    @staticmethod
    def sems(line):
        return 2 * (line - 1) + 2

    def go(self, index, src, dst, target):
        copy = remote(src, dst, self.send_sems.at[index], self.recv_sems.at[index], target)
        copy.start()
        self.started.append(copy)

    def arrived(self, index, dst):
        remote(dst, dst, self.send_sems.at[index], self.recv_sems.at[index], self.place.partner()).wait_recv()

    def begin(self):
        p = self.place
        for hop in range(1, p.line):
            self.go(hop - 1, self.own_ref, self.all.at[p.shard], p.on_line(hop))
        self.go(2 * self.hops, self.own_ref, self.all.at[p.shard], p.partner())
        self.own = pltpu.make_async_copy(self.own_ref, self.all.at[p.shard], self.recv_sems.at[2 * self.hops + 1])
        self.own.start()

    def hand(self):
        p = self.place
        for hop in range(1, p.line):
            block = self.all.at[2 * p.source_spot(hop) + p.core]
            self.arrived(hop - 1, block)
            self.go(self.hops + hop - 1, block, block, p.partner())

    def ready(self):
        p = self.place
        self.own.wait()
        self.arrived(2 * self.hops, self.all.at[p.shard + 1 - 2 * p.core])
        for hop in range(1, p.line):
            self.arrived(self.hops + hop - 1, self.all.at[2 * p.source_spot(hop) + 1 - p.core])

    def end(self):
        for copy in self.started:
            copy.wait_send()


class Scatter:
    def __init__(self, place, grad, from_core, from_first, from_second, from_line, done, send_sems, recv_sems):
        self.place, self.grad = place, grad
        self.from_core, self.from_first, self.from_second = from_core, from_first, from_second
        self.from_line, self.done = from_line, done
        self.send_sems, self.recv_sems = send_sems, recv_sems
        self.line, _, self.rows, self.cols = grad.shape
        self.started = []

    @staticmethod
    def sems(line):
        return 1 + 2 + 1 + (line - 1) + 3

    @staticmethod
    def scratch(line, rows, cols):
        half = (rows // 2, cols // 2)
        return [
            pltpu.VMEM((line, rows, cols), jnp.bfloat16),
            pltpu.VMEM((2, line) + half, jnp.bfloat16),
            pltpu.VMEM((line,) + half, jnp.bfloat16),
            pltpu.VMEM((line - 1,) + half, jnp.bfloat16),
            pltpu.VMEM((2, 2) + half, jnp.bfloat16),
        ]

    def go(self, index, src, dst, target):
        copy = remote(src, dst, self.send_sems.at[index], self.recv_sems.at[index], target)
        copy.start()
        self.started.append(copy)

    def arrived(self, index, dst):
        remote(dst, dst, self.send_sems.at[index], self.recv_sems.at[index], self.place.partner()).wait_recv()

    def slices(self, row_half, col_half):
        half_rows, half_cols = self.rows // 2, self.cols // 2
        return (
            pl.ds(pl.multiple_of(row_half * half_rows, 16), half_rows),
            pl.ds(pl.multiple_of(col_half * half_cols, 128), half_cols),
        )

    def halves(self, side, which):
        p = self.place
        row_half = jnp.where(p.core == 0, which, side)
        col_half = jnp.where(p.core == 0, side, which)
        return self.slices(row_half, col_half)

    def swap(self):
        p = self.place
        self.go(0, self.grad.at[:, 1 - p.core], self.from_core, p.partner())

    def add(self, rows, cols, others, targets_spot=None):
        p = self.place
        half_rows, half_cols = self.rows // 2, self.cols // 2
        step = 48 if half_rows % 48 == 0 else 16
        steps = half_rows // step

        def one(index, carry):
            spot, part = index // steps, lax.rem(index, steps)
            at = pl.ds(pl.multiple_of(rows.start + part * step, 16), step)
            inner = pl.ds(pl.multiple_of(part * step, 16), step)
            total = self.grad[spot, p.core, at, cols].astype(jnp.float32) + self.from_core[spot, at, cols].astype(
                jnp.float32
            )
            for other in others:
                total = total + other[spot, inner, :].astype(jnp.float32)
            self.grad[spot, p.core, at, cols] = total.astype(jnp.bfloat16)
            return carry

        lax.fori_loop(0, self.line * steps, one, 0)

    def to_first(self):
        p = self.place
        self.arrived(0, self.from_core)
        keep = jnp.where(p.core == 0, p.col_half, p.row_half)
        for which in (0, 1):
            rows, cols = self.halves(1 - keep, which)
            self.add(rows, cols, [])
            self.go(1 + which, self.grad.at[:, p.core, rows, cols], self.from_first.at[which], p.in_plane(p.first))

    def to_second(self):
        p = self.place
        for which in (0, 1):
            self.arrived(1 + which, self.from_first.at[which])
        keep = jnp.where(p.core == 0, p.col_half, p.row_half)
        mine = jnp.where(p.core == 0, p.row_half, p.col_half)
        rows, cols = self.halves(keep, 1 - mine)
        self.add(rows, cols, [self.from_first.at[1 - mine]])
        self.go(3, self.grad.at[:, p.core, rows, cols], self.from_second, p.in_plane(p.second))

    def to_line(self):
        p = self.place
        self.arrived(3, self.from_second)
        mine = jnp.where(p.core == 0, p.row_half, p.col_half)
        rows, cols = self.slices(p.row_half, p.col_half)
        self.add(rows, cols, [self.from_first.at[mine], self.from_second])
        for hop in range(1, self.line):
            spot = lax.rem(p.spot + hop, self.line)
            self.go(3 + hop, self.grad.at[spot, p.core, rows, cols], self.from_line.at[hop - 1], p.on_line(hop))

    def to_plane(self):
        p = self.place
        for hop in range(1, self.line):
            self.arrived(3 + hop, self.from_line.at[hop - 1])
        half_rows = self.rows // 2
        rows, cols = self.slices(p.row_half, p.col_half)
        step = 16

        def one(part, carry):
            at = pl.ds(pl.multiple_of(rows.start + part * step, 16), step)
            inner = pl.ds(pl.multiple_of(part * step, 16), step)
            total = self.grad[p.spot, p.core, at, cols].astype(jnp.float32)
            for hop in range(1, self.line):
                total = total + self.from_line[hop - 1, inner, :].astype(jnp.float32)
            self.done[p.row_half, p.col_half, inner, :] = total.astype(jnp.bfloat16)
            return carry

        lax.fori_loop(0, half_rows // step, one, 0)
        own = self.done.at[p.row_half, p.col_half]
        for step in range(1, 4):
            self.go(2 + self.line + step, own, own, p.in_plane(lax.rem(p.dp + step, 4)))

    def finish(self):
        p = self.place
        for step in range(1, 4):
            other = lax.rem(p.dp + 4 - step, 4)
            self.arrived(2 + self.line + step, self.done.at[other // 2, lax.rem(other, 2)])

    def end(self):
        for copy in self.started:
            copy.wait_send()


class SmallSum:
    def __init__(self, place, own, from_core, on_line, in_plane, send_sems, recv_sems):
        self.place, self.own, self.from_core, self.on_line, self.in_plane = place, own, from_core, on_line, in_plane
        self.send_sems, self.recv_sems = send_sems, recv_sems
        self.started = []

    @staticmethod
    def sems(line):
        return 1 + (line - 1) + 3

    @staticmethod
    def scratch(line, rows, cols):
        return [
            pltpu.VMEM((rows, cols), jnp.float32),
            pltpu.VMEM((rows, cols), jnp.float32),
            pltpu.VMEM((line, rows, cols), jnp.float32),
            pltpu.VMEM((4, rows, cols), jnp.float32),
        ]

    def go(self, index, src, dst, target):
        copy = remote(src, dst, self.send_sems.at[index], self.recv_sems.at[index], target)
        copy.start()
        self.started.append(copy)

    def arrived(self, index, dst):
        remote(dst, dst, self.send_sems.at[index], self.recv_sems.at[index], self.place.partner()).wait_recv()

    def swap(self):
        self.go(0, self.own, self.from_core, self.place.partner())

    def to_line(self):
        p = self.place
        self.arrived(0, self.from_core)
        self.on_line[p.spot] = self.own[...] + self.from_core[...]
        slot = self.on_line.at[p.spot]
        for hop in range(1, p.line):
            self.go(hop, slot, slot, p.on_line(hop))

    def to_plane(self):
        p = self.place
        for hop in range(1, p.line):
            self.arrived(hop, self.on_line.at[p.source_spot(hop)])
        total = self.on_line[0]
        for spot in range(1, p.line):
            total = total + self.on_line[spot]
        self.in_plane[p.dp] = total
        slot = self.in_plane.at[p.dp]
        for step in range(1, 4):
            self.go(p.line - 1 + step, slot, slot, p.in_plane(lax.rem(p.dp + step, 4)))

    def finish(self, out_ref):
        p = self.place
        for step in range(1, 4):
            self.arrived(p.line - 1 + step, self.in_plane.at[lax.rem(p.dp + 4 - step, 4)])
        out_ref[...] = (self.in_plane[0] + self.in_plane[1]) + (self.in_plane[2] + self.in_plane[3])

    def end(self):
        for copy in self.started:
            copy.wait_send()


class SequenceGather:
    def __init__(self, place, blocks, send_sems, recv_sems):
        self.place, self.blocks = place, blocks
        self.send_sems, self.recv_sems = send_sems, recv_sems
        self.started = []

    @staticmethod
    def sems(line):
        return 3 + (line - 1) + line

    def go(self, index, ref, target):
        copy = remote(ref, ref, self.send_sems.at[index], self.recv_sems.at[index], target)
        copy.start()
        self.started.append(copy)

    def arrived(self, index, dst):
        remote(dst, dst, self.send_sems.at[index], self.recv_sems.at[index], self.place.partner()).wait_recv()

    def begin(self):
        p = self.place
        for step in range(1, 4):
            self.go(step - 1, self.blocks.at[p.shard, p.dp], p.in_plane(lax.rem(p.dp + step, 4)))

    def to_line(self):
        p = self.place
        for step in range(1, 4):
            self.arrived(step - 1, self.blocks.at[p.shard, lax.rem(p.dp + 4 - step, 4)])
        own = self.blocks.at[p.shard]
        for hop in range(1, p.line):
            self.go(2 + hop, own, p.on_line(hop))
        self.go(2 + p.line, own, p.partner())

    def hand(self):
        p = self.place
        for hop in range(1, p.line):
            block = self.blocks.at[2 * p.source_spot(hop) + p.core]
            self.arrived(2 + hop, block)
            self.go(2 + p.line + hop, block, p.partner())

    def ready(self):
        p = self.place
        self.arrived(2 + p.line, self.blocks.at[p.shard + 1 - 2 * p.core])
        for hop in range(1, p.line):
            self.arrived(2 + p.line + hop, self.blocks.at[2 * p.source_spot(hop) + 1 - p.core])

    def end(self):
        for copy in self.started:
            copy.wait_send()
ANY = pl.BlockSpec(memory_space=pl.ANY)
WHOLE = pl.BlockSpec(memory_space=pltpu.VMEM)
SCALARS = pl.BlockSpec(memory_space=pltpu.SMEM)
VMEM_BYTES = 67_000_000
BF16, F32 = jnp.bfloat16, jnp.float32


def nn(left, right):
    return lax.dot_general(left, right, (((1,), (0,)), ((), ())), preferred_element_type=F32)


def nt(left, right):
    return lax.dot_general(left, right, (((1,), (1,)), ((), ())), preferred_element_type=F32)


def tn(left, right):
    return lax.dot_general(left, right, (((0,), (0,)), ((), ())), preferred_element_type=F32)


def lanes(start, size):
    return pl.ds(pl.multiple_of(start, 128), size)


def loop(count, step):
    def one(index, carry):
        step(index)
        return carry

    lax.fori_loop(0, count, one, 0)


def gelu_parts(v):
    spread = 0.5 * (1.0 + lax.erf(v * (1.0 / math.sqrt(2.0))))
    bell = jnp.exp(-0.5 * v * v) * (1.0 / math.sqrt(2.0 * math.pi))
    return v * spread, spread + v * bell


def place_vectors(shard, vectors, class_rows, short, out):
    in_bias, mix_bias, gain_one, shift_one, up_bias, down_bias, gain_two, shift_two, pool_bias = vectors
    short[...] = jnp.zeros(short.shape, F32)
    rows = [in_bias, in_bias, mix_bias, gain_one, shift_one, up_bias, up_bias, up_bias, up_bias]
    rows += [down_bias, gain_two, shift_two, pool_bias]
    for row, vector in enumerate(rows):
        size = vector.shape[0]
        short[row : row + 1, 0:size] = vector[...].astype(F32).reshape(1, size)
    size = class_rows.shape[1]
    short[13 : 13 + class_rows.shape[0], 0:size] = class_rows[...].astype(F32)
    values = short[...].astype(BF16)
    span, width = short.shape[1], out.shape[1]
    lane = lax.broadcasted_iota(jnp.int32, (span, width), 0)
    column = lax.broadcasted_iota(jnp.int32, (span, width), 1)
    row_at = lax.broadcasted_iota(jnp.int32, (16, 1), 0)

    def placed(size):
        per_row = width // size
        spread = jnp.where((column - lax.rem(shard, per_row) * size == lane) & (lane < size), 1.0, 0.0)
        return nn(values, spread.astype(BF16)), shard // per_row

    one_row, _ = placed(mix_bias.shape[0])
    of_in, in_row = placed(in_bias.shape[0])
    of_up, up_row = placed(up_bias.shape[0])
    is_in, is_up = row_at < 2, (row_at >= 5) & (row_at < 9)
    result = jnp.where(is_in, jnp.where(row_at == in_row, of_in, 0.0), one_row)
    result = jnp.where(is_up, jnp.where(row_at == 5 + up_row, of_up, 0.0), result)
    out[...] = result.astype(BF16)


def own_sums(shard, parts, total_ref, out, classes):
    total = total_ref[...]
    width = total.shape[1]
    size = width // parts
    own, own_in, own_up = (jnp.zeros(shape, F32) for shape in ((24, size), (1, 2 * size), (1, 4 * size)))
    for place in range(parts):
        here = shard == place
        own = jnp.where(here, total[:, place * size : (place + 1) * size], own)
        row, at = divmod(2 * size * place, width)
        own_in = jnp.where(here, total[row : row + 1, at : at + 2 * size], own_in)
        row, at = divmod(4 * size * place, width)
        own_up = jnp.where(here, total[5 + row : 6 + row, at : at + 4 * size], own_up)
    out[...] = jnp.zeros(out.shape, F32)
    out[0:24, 0:size] = own
    out[24:25, 0 : 2 * size] = own_in
    out[25:26, 0 : 4 * size] = own_up
    out[26:27, 0:classes] = total[16:17, 13 : 13 + classes]


def layer_kernel(fsdp_size, *refs):
    refs = list(refs)

    def take(count):
        out = refs[:count]
        del refs[:count]
        return out

    lengths, labels, class_bias, tokens_in, cot_in = take(5)
    shards = take(5)
    vectors, class_rows = take(9), take(1)[0]
    layer_out, input_grad, down_out, up_out, mix_out, in_out, pool_out, sums_out = take(8)
    w_in, w_mix, w_up, w_down, w_pool, small_all = take(6)
    g_down, g_up = take(2)
    recv = [take(5) for _ in range(4)]
    sum_refs = take(4)
    (blocks,) = take(1)
    tok, tok_t, cot, att, att_t, first, first_t = take(7)
    qkv, act, slope = take(3)
    unit_one, unit_two, grad = take(3)
    inv_one, inv_two, key_mask, lse, vec = take(5)
    short, small_in, bias_row, sums_all = take(4)
    g_send, g_recv, s_send, s_recv, q_send, q_recv, v_send, v_recv, b_send, b_recv, local = take(11)
    seq, width = tok.shape
    hidden = act.shape[1]
    pairs = width // 128
    parts = hidden // width
    line = fsdp_size // 2
    rows_of = pl.ds

    loads = [
        pltpu.make_async_copy(tokens_in, tok, local.at[0]),
        pltpu.make_async_copy(cot_in, cot, local.at[1]),
    ]
    for load in loads:
        load.start()
    place = Place(fsdp_size)
    place_vectors(place.shard, vectors, class_rows, short, small_in)
    bias_row[...] = jnp.zeros(bias_row.shape, F32)
    classes = class_bias.shape[0]
    bias_row[0:1, 13 : 13 + classes] = class_bias[...].astype(F32).reshape(1, classes)
    place.meet()
    gathers = [
        Gather(place, shard, whole, g_send.at[i], g_recv.at[i])
        for i, (shard, whole) in enumerate(zip(shards, (w_in, w_mix, w_up, w_down, w_pool)))
    ]
    for_in, for_mix, for_up, for_down, for_pool = gathers
    little = SmallGather(place, small_in, small_all, v_send, v_recv)
    for_in.begin()
    little.begin()
    for one in gathers[1:]:
        one.begin()
    hops = range(1, line)
    length = lengths[0]
    label = labels[0]

    for load in loads:
        load.wait()
    tok_t[...] = tok[...].T
    key_at = lax.broadcasted_iota(jnp.int32, (seq, 128), 0)
    key_mask[...] = jnp.where(key_at < length, 0.0, -1e30).astype(F32)

    def mask_cot(index):
        rows = rows_of(pl.multiple_of(index * 128, 128), 128)
        live = (key_mask[rows, :] == 0.0).astype(F32)
        grad[rows, :] = cot[rows, :].astype(F32) * jnp.concatenate([live] * (width // 128), axis=1)

    loop(seq // 128, mask_cot)
    grad_low = cot

    for hop in hops:
        for_in.spread(hop)
    little.hand()
    for hop in hops:
        for_in.relay(hop)
    for hop in hops:
        for_mix.spread(hop)
    little.ready()
    vec[...] = jnp.sum(small_all[...].astype(F32), axis=0)
    for hop in hops:
        for_in.hand(hop)
    for hop in hops:
        for_mix.relay(hop)
    for_in.ready()

    score_scale = 1.0 / math.sqrt(DH)
    for part in range(3):

        def project(index, part=part):
            inner = lanes(index * 256, 256)
            cols = lanes(part * width + index * 256, 256)
            out = nn(tok[...], w_in[:, :, :, cols].reshape(width, 256))
            if part != 1:
                row = 0 if part == 0 else 1
                out = out + vec[row : row + 1, inner]
            out = out.astype(BF16)
            if part == 0:
                out = out * jnp.asarray(score_scale, BF16)
            qkv[:, cols] = out

        loop(width // 256, project)
    for hop in hops:
        for_mix.hand(hop)

    low_lanes = lax.broadcasted_iota(jnp.int32, (1, 128), 1) < 64
    zero_low = jnp.zeros((), BF16)

    def head_lanes(value, half):
        return jnp.where(low_lanes if half == 0 else jnp.logical_not(low_lanes), value, zero_low)

    def masked_scores(keys, queries):
        mask = key_mask[...]
        return nt(keys, queries) + jnp.concatenate([mask] * (seq // 128), axis=1)

    def attend(pair):
        queries, keys, values = (qkv[:, lanes(part * width + pair * 128, 128)] for part in range(3))
        values_t = values.T
        mixed = []
        for half in (0, 1):
            scores = masked_scores(keys, head_lanes(queries, half))
            highest = jnp.max(scores, axis=0, keepdims=True)
            raw = jnp.exp(scores - highest)
            total = jnp.sum(raw, axis=0, keepdims=True)
            lse[pair, half : half + 1, :] = highest + jnp.log(total)
            soft = (raw * (1.0 / total)).astype(BF16)
            mixed.append(nn(values_t, soft)[64 * half : 64 * half + 64, :])
        both = jnp.concatenate(mixed, axis=0)
        att_t[rows_of(pl.multiple_of(pair * 128, 128), 128), :] = both.astype(BF16)
        att[:, lanes(pair * 128, 128)] = both.T.astype(BF16)

    def attend_some(first_pair, last_pair):
        lax.fori_loop(first_pair, last_pair, lambda pair, carry: (attend(pair), carry)[1], 0)

    attend_some(0, 2)
    for hop in hops:
        for_up.spread(hop)
    attend_some(2, 4)
    for hop in hops:
        for_up.relay(hop)
    attend_some(4, pairs)
    for hop in hops:
        for_down.spread(hop)
    for hop in hops:
        for_up.hand(hop)
    for_mix.ready()

    gain_one, shift_one = vec[3:4, :], vec[4:5, :]

    def mean_of(value):
        return jnp.sum(value, axis=1, keepdims=True) * (1.0 / width)

    def norm_one(index):
        rows = rows_of(pl.multiple_of(index * 256, 256), 256)
        total = nn(att[rows, :], w_mix[...].reshape(width, width)) + vec[2:3, :] + tok[rows, :].astype(F32)
        centered = total - mean_of(total)
        inverse = lax.rsqrt(mean_of(centered * centered) + EPSILON)
        unit = centered * inverse
        unit_one[rows, :] = unit
        inv_one[rows, :] = jnp.broadcast_to(inverse, (256, 128))
        first[rows, :] = (unit * gain_one + shift_one).astype(BF16)

    loop(seq // 256, norm_one)
    first_t[...] = first[...].T
    for hop in hops:
        for_down.relay(hop)
    for hop in hops:
        for_pool.spread(hop)
    for_up.ready()

    for part in range(parts):

        def raise_up(index, part=part):
            inner = lanes(index * 384, 384)
            cols = lanes(part * width + index * 384, 384)
            pre = nn(first[...], w_up[:, :, :, cols].reshape(width, 384)) + vec[5 + part : 6 + part, inner]
            value, derivative = gelu_parts(pre)
            act[:, cols] = value.astype(BF16)
            slope[:, cols] = derivative.astype(BF16)

        loop(width // 384, raise_up)
        if part == 0:
            for hop in hops:
                for_down.hand(hop)
        if part == 1:
            for hop in hops:
                for_pool.relay(hop)
    for hop in hops:
        for_pool.hand(hop)
    for_down.ready()
    gain_two, shift_two = vec[10:11, :], vec[11:12, :]

    def norm_two(index):
        rows = rows_of(pl.multiple_of(index * 256, 256), 256)
        total = nn(act[rows, :], w_down[...].reshape(hidden, width)) + vec[9:10, :]
        total = total + (unit_one[rows, :] * gain_one + shift_one)
        centered = total - mean_of(total)
        inverse = lax.rsqrt(mean_of(centered * centered) + EPSILON)
        unit = centered * inverse
        unit_two[rows, :] = unit
        inv_two[rows, :] = jnp.broadcast_to(inverse, (256, 128))
        att[rows, :] = (unit * gain_two + shift_two).astype(BF16)

    loop(seq // 256, norm_two)
    stores = [pltpu.make_async_copy(att, layer_out, local.at[2])]
    stores[0].start()

    for_pool.ready()
    top = lax.broadcasted_iota(jnp.int32, (16, 1), 0) == 0
    head = att[0:16, :]
    vec_low = vec[...].astype(BF16)
    pooled = jnp.tanh(nn(head, w_pool[...].reshape(width, width)) + vec[12:13, :])
    pooled_low = pooled.astype(BF16)
    logits = nt(pooled_low, vec_low) + bias_row[0:1, 0:16]
    class_at = lax.broadcasted_iota(jnp.int32, (16, 16), 1) - 13
    logits = jnp.where(class_at >= 0, logits, -1e30)
    raised = jnp.exp(logits - jnp.max(logits, axis=1, keepdims=True))
    soft_logits = raised / jnp.sum(raised, axis=1, keepdims=True)
    onehot = (class_at == label).astype(F32)
    grad_logits = jnp.where(top, soft_logits - onehot, 0.0).astype(BF16)
    sums = sum_refs[0]
    sums[0:16, :] = tn(grad_logits, pooled_low)
    sums[16:24, :] = jnp.zeros((8, width), F32)
    sums[16:17, 0:16] = grad_logits[0:1, :].astype(F32)
    grad_pool_pre = (nn(grad_logits, vec_low) * (1.0 - pooled * pooled)).astype(BF16)
    sums[12:13, :] = grad_pool_pre[0:1, :].astype(F32)
    block = jnp.where(top, head.astype(F32), 0.0)
    second_row = lax.broadcasted_iota(jnp.int32, (16, 1), 0) == 1
    block = jnp.where(second_row, jnp.broadcast_to(grad_pool_pre[0:1, :].astype(F32), (16, width)), block)
    blocks[place.shard, place.dp] = block.astype(BF16)
    sequences = SequenceGather(place, blocks, q_send, q_recv)
    sequences.begin()
    grad[0:16, :] += nt(grad_pool_pre, w_pool[...].reshape(width, width))

    for one in gathers:
        one.end()

    def norm_back(unit_ref, inv_ref, gain, gain_row, shift_row, bias_row, size):
        def one(index, carry):
            by_gain, by_shift, by_bias = carry
            rows = rows_of(pl.multiple_of(index * size, size), size)
            incoming = grad[rows, :]
            unit = unit_ref[rows, :]
            scaled = incoming * gain
            inverse = jnp.concatenate([inv_ref[rows, :]] * (width // 128), axis=1)
            back = inverse * (scaled - mean_of(scaled) - unit * mean_of(scaled * unit))
            low = back.astype(BF16)
            grad[rows, :] = back
            grad_low[rows, :] = low
            return (
                by_gain + jnp.sum(incoming * unit, axis=0, keepdims=True),
                by_shift + jnp.sum(incoming, axis=0, keepdims=True),
                by_bias + jnp.sum(low.astype(F32), axis=0, keepdims=True),
            )

        zero = jnp.zeros((1, width), F32)
        by_gain, by_shift, by_bias = lax.fori_loop(0, seq // size, one, (zero, zero, zero))
        sums[gain_row : gain_row + 1, :] = by_gain
        sums[shift_row : shift_row + 1, :] = by_shift
        sums[bias_row : bias_row + 1, :] = by_bias

    norm_back(unit_two, inv_two, gain_two, 10, 11, 9, 128)

    scatters = [
        Scatter(place, ref, *recv[i], s_send.at[i], s_recv.at[i])
        for i, ref in enumerate((g_down, g_up, w_up.at[:, :, :, pl.ds(3 * width, width)], w_up.at[:, :, :, pl.ds(0, 3 * width)]))
    ]
    of_down, of_up, of_mix, of_in = scatters
    rows_down = hidden // fsdp_size

    def down_gradient(index):
        cols = lanes(index * rows_down, rows_down)
        g_down[index // 2, lax.rem(index, 2)] = tn(act[:, cols], grad_low[...]).astype(BF16)

    loop(fsdp_size, down_gradient)
    of_down.swap()
    sequences.to_line()

    for part in range(parts):

        def through_down(index, part=part):
            owner = part * 2 + index
            inner = lanes(index * rows_down, rows_down)
            cols = lanes(owner * rows_down, rows_down)
            low = (nt(grad_low[...], w_down[part, index]) * slope[:, cols].astype(F32)).astype(BF16)
            slope[:, cols] = low
            sums[5 + part : 6 + part, inner] = jnp.sum(low.astype(F32), axis=0, keepdims=True)

        loop(2, through_down)
        if part == 1:
            of_down.to_first()

    def up_gradient(index):
        cols = lanes(index * 256, 256)
        out = nn(first_t[...], slope[:, cols]).astype(BF16)
        g_up[:, :, :, cols] = out.reshape(line, 2, width // fsdp_size, 256)

    loop(hidden // 256, up_gradient)
    of_up.swap()
    of_down.to_second()
    sequences.hand()

    half_line = line // 2
    half_width = width // 2

    def through_up(index):
        cols = lanes(index * half_width, half_width)
        weight = w_up[rows_of(index * half_line, half_line)].reshape(half_width, hidden)
        grad[:, cols] += nt(slope[...], weight)

    loop(2, through_up)
    of_up.to_first()
    of_down.to_line()
    norm_back(unit_one, inv_one, gain_one, 3, 4, 2, 128)

    def mix_gradient(index):
        out = nn(att_t[...], grad_low[:, lanes(index * 256, 256)]).astype(BF16)
        w_up[:, :, :, lanes(3 * width + index * 256, 256)] = out.reshape(line, 2, width // fsdp_size, 256)

    loop(width // 256, mix_gradient)
    of_mix.swap()

    def through_mix(index):
        cols = lanes(index * half_width, half_width)
        weight = w_mix[rows_of(index * half_line, half_line)].reshape(half_width, width)
        first[:, cols] = nt(grad_low[...], weight).astype(BF16)

    loop(2, through_mix)
    of_up.to_second()

    def attend_back(pair):
        at = [lanes(part * width + pair * 128, 128) for part in range(3)]
        queries, keys, values = (qkv[:, cols] for cols in at)
        rows = rows_of(pl.multiple_of(pair * 128, 128), 128)
        out_grad = first[:, lanes(pair * 128, 128)]
        keys_t = keys.T
        products = out_grad.astype(F32).T * att_t[rows, :].astype(F32)
        by_query, by_key, by_value = [], None, None
        for half in (0, 1):
            own_queries, own_grad = head_lanes(queries, half), head_lanes(out_grad, half)
            soft = jnp.exp(masked_scores(keys, own_queries) - lse[pair, half : half + 1, :])
            row_sum = jnp.sum(products[64 * half : 64 * half + 64, :], axis=0, keepdims=True)
            score_grad = (soft * (nt(values, own_grad) - row_sum)).astype(BF16)
            value_part = nn(soft.astype(BF16), own_grad)
            key_part = nn(score_grad, own_queries)
            by_value = value_part if by_value is None else by_value + value_part
            by_key = key_part if by_key is None else by_key + key_part
            by_query.append(nn(keys_t, score_grad)[64 * half : 64 * half + 64, :])
        qkv[:, at[0]] = (jnp.concatenate(by_query, axis=0).T * score_scale).astype(BF16)
        qkv[:, at[1]] = by_key.astype(BF16)
        qkv[:, at[2]] = by_value.astype(BF16)

    def attend_back_some(first_pair, last_pair):
        lax.fori_loop(first_pair, last_pair, lambda pair, carry: (attend_back(pair), carry)[1], 0)

    attend_back_some(0, 1)
    of_mix.to_first()
    of_down.to_plane()
    attend_back_some(1, 2)
    of_up.to_line()
    attend_back_some(2, 3)
    of_mix.to_second()
    attend_back_some(3, 4)
    sequences.ready()
    attend_back_some(4, 5)
    of_up.to_plane()
    of_mix.to_line()
    attend_back_some(5, pairs)

    for part in range(3):

        def in_gradient(index, part=part):
            inner = lanes(index * 256, 256)
            cols = lanes(part * width + index * 256, 256)
            incoming = qkv[:, cols]
            w_up[:, :, :, cols] = nn(tok_t[...], incoming).astype(BF16).reshape(line, 2, width // fsdp_size, 256)
            if part != 1:
                row = 0 if part == 0 else 1
                sums[row : row + 1, inner] = jnp.sum(incoming.astype(F32), axis=0, keepdims=True)

        loop(width // 256, in_gradient)
    of_in.swap()
    total = SmallSum(place, *sum_refs, b_send, b_recv)
    total.swap()
    of_mix.to_plane()

    def through_in(index):
        cols = lanes(index * half_width, half_width)
        weight = w_in[rows_of(index * half_line, half_line)].reshape(half_width, 3 * width)
        grad[:, cols] += nt(qkv[...], weight)

    loop(1, through_in)
    of_in.to_first()
    total.to_line()
    loop_from_one = lambda step: lax.fori_loop(1, 2, lambda index, carry: (step(index), carry)[1], 0)
    loop_from_one(through_in)
    store = pltpu.make_async_copy(grad, input_grad, local.at[3])
    store.start()
    stores.append(store)
    of_in.to_second()
    total.to_plane()

    every = blocks[...].reshape(fsdp_size * 4 * 16, width)
    count = fsdp_size * 4 * 16
    row_at = lax.broadcasted_iota(jnp.int32, (count, count), 0)
    col_at = lax.broadcasted_iota(jnp.int32, (count, count), 1)
    shift = jnp.where((lax.rem(row_at, 16) == 0) & (col_at == row_at + 1), 1.0, 0.0).astype(BF16)
    paired = nn(shift, every).astype(BF16)
    own_rows_at = lax.broadcasted_iota(jnp.int32, (128, width), 0) + place.shard * (width // fsdp_size)
    pick = jnp.where(own_rows_at == lax.broadcasted_iota(jnp.int32, (128, width), 1), 1.0, 0.0).astype(BF16)
    own_part = nt(pick, every).astype(BF16)
    pool_out[...] = nn(own_part, paired)[0 : width // fsdp_size, :]

    of_in.to_line()
    total.finish(sums_all)
    own_sums(place.shard, fsdp_size, sums_all, sums_out, classes)
    of_in.to_plane()
    for index, (one, out) in enumerate(zip(scatters, (down_out, up_out, mix_out, in_out))):
        one.finish()
        half_rows, half_cols = one.rows // 2, one.cols // 2
        for quarter in range(4):
            row_half, col_half = quarter // 2, quarter % 2
            target = out.at[
                pl.ds(row_half * half_rows, half_rows), pl.ds(col_half * half_cols, half_cols)
            ]
            store = pltpu.make_async_copy(one.done.at[row_half, col_half], target, local.at[4 + 4 * index + quarter])
            store.start()
            stores.append(store)
    for store in stores:
        store.wait()
    for one in scatters + [little, sequences, total]:
        one.end()


def run_layer(fsdp_size, lengths, labels, class_bias, tokens, cotangent, shards, vectors, class_rows):
    line = fsdp_size // 2
    seq, width = tokens.shape
    in_shard, mix_shard, up_shard, down_shard, pool_shard = shards
    hidden = up_shard.shape[1]
    vmem, dma = pltpu.VMEM, pltpu.SemaphoreType.DMA
    reduced = (down_shard, up_shard, mix_shard, in_shard)
    scratch = [vmem((line, 2) + s.shape, BF16) for s in shards] + [vmem((fsdp_size, 16, width), BF16)]
    scratch += [vmem((line, 2) + s.shape, BF16) for s in (down_shard, up_shard)]
    for s in reduced:
        scratch += Scatter.scratch(line, *s.shape)
    scratch += SmallSum.scratch(line, 24, width)
    scratch += [vmem((fsdp_size, 4, 16, width), BF16)]
    rows, turned = vmem((seq, width), BF16), vmem((width, seq), BF16)
    scratch += [rows, turned, rows, rows, turned, rows, turned]
    scratch += [vmem((seq, 3 * width), BF16), vmem((seq, hidden), BF16), vmem((seq, hidden), BF16)]
    scratch += [vmem((seq, width), F32)] * 3
    scratch += [vmem((seq, 128), F32)] * 3 + [vmem((width // 128, 8, seq), F32), vmem((16, width), F32)]
    span = hidden // fsdp_size
    scratch += [vmem((16, span), F32), vmem((16, width), BF16), vmem((8, 128), F32), vmem((24, width), F32)]
    for count in (
        (5, Gather.sems(line)),
        (4, Scatter.sems(line)),
        (SequenceGather.sems(line),),
        (SmallGather.sems(line),),
        (SmallSum.sems(line),),
    ):
        scratch += [dma(count), dma(count)]
    scratch += [dma((20,))]
    out_shape = [jax.ShapeDtypeStruct((seq, width), BF16), jax.ShapeDtypeStruct((seq, width), F32)]
    out_shape += [jax.ShapeDtypeStruct(s.shape, BF16) for s in reduced]
    out_shape += [jax.ShapeDtypeStruct((width // fsdp_size, width), F32), jax.ShapeDtypeStruct((32, span), F32)]
    return pl.pallas_call(
        functools.partial(layer_kernel, fsdp_size),
        out_shape=out_shape,
        in_specs=[SCALARS, SCALARS, WHOLE] + [ANY] * 7 + [WHOLE] * 10,
        out_specs=[ANY] * 6 + [WHOLE] * 2,
        scratch_shapes=scratch,
        compiler_params=pltpu.CompilerParams(collective_id=0, has_side_effects=True, vmem_limit_bytes=VMEM_BYTES),
        name="layer",
    )(lengths, labels, class_bias, tokens, cotangent, *shards, *vectors, class_rows)


def outputs_kernel(as_is, rounded, sizes, classes, size, *refs):
    count = as_is + rounded
    inputs, sums = refs[:count], refs[count]
    refs = refs[count + 1 :]
    outs, small = refs[:count], refs[count : count + len(sizes) + 2]
    refs = refs[count + len(sizes) + 2 :]
    held, wide, (load_sems, store_sems) = refs[:count], refs[count : count + rounded], refs[count + rounded :]
    order = list(range(as_is, count)) + list(range(as_is))
    loads = {i: pltpu.make_async_copy(inputs[i], held[i], load_sems.at[i]) for i in order}
    for load in loads.values():
        load.start()
    for (row, length), out in zip(sizes.items(), small):
        out[...] = sums[row : row + 1, 0:length].reshape(length)
    small[-2][...] = sums[13 : 13 + classes, 0:size]
    small[-1][...] = sums[26:27, 0:classes].reshape(classes)
    stores = []
    for i in order:
        loads[i].wait()
        source = held[i]
        if i >= as_is:
            source = wide[i - as_is]
            step = 32

            def widen(index, narrow=held[i], source=source):
                rows = pl.ds(pl.multiple_of(index * step, step), step)
                source[rows, :] = narrow[rows, :].astype(F32)

            loop(source.shape[0] // step, widen)
        stores.append(pltpu.make_async_copy(source, outs[i], store_sems.at[i]))
        stores[-1].start()
    for store in stores:
        store.wait()


def run_outputs(as_is, rounded, sums, sizes, classes, size):
    arrays = as_is + rounded
    out_shape = [jax.ShapeDtypeStruct(a.shape, a.dtype) for a in as_is]
    out_shape += [jax.ShapeDtypeStruct(a.shape, F32) for a in rounded]
    out_shape += [jax.ShapeDtypeStruct((length,), F32) for length in sizes.values()]
    out_shape += [jax.ShapeDtypeStruct((classes, size), F32), jax.ShapeDtypeStruct((classes,), F32)]
    scratch = [pltpu.VMEM(a.shape, a.dtype) for a in arrays] + [pltpu.VMEM(a.shape, F32) for a in rounded]
    scratch += [pltpu.SemaphoreType.DMA((len(arrays),))] * 2
    return pl.pallas_call(
        functools.partial(outputs_kernel, len(as_is), len(rounded), sizes, classes, size),
        out_shape=out_shape,
        in_specs=[ANY] * len(arrays) + [WHOLE],
        out_specs=[ANY] * len(arrays) + [WHOLE] * (len(sizes) + 2),
        scratch_shapes=scratch,
        compiler_params=pltpu.CompilerParams(vmem_limit_bytes=VMEM_BYTES),
        name="outputs",
    )(*arrays, sums)


def kernel_body(
    fsdp_size,
    tokens,
    in_weight,
    in_bias,
    mix_weight,
    mix_bias,
    first_gain,
    first_shift,
    up_weight,
    up_bias,
    down_weight,
    down_bias,
    second_gain,
    second_shift,
    pool_weight,
    pool_bias,
    class_weight,
    class_bias,
    lengths,
    labels,
    cotangent,
):
    layer_out, input_grad, down_grad, up_grad, mix_grad, in_grad, pool_grad, sums = run_layer(
        fsdp_size,
        lengths,
        labels,
        class_bias,
        tokens,
        cotangent,
        (in_weight, mix_weight, up_weight, down_weight, pool_weight),
        (in_bias, mix_bias, first_gain, first_shift, up_bias, down_bias, second_gain, second_shift, pool_bias),
        class_weight.T,
    )
    size = mix_bias.shape[0]
    sizes = {24: 2 * size, 2: size, 3: size, 4: size, 25: 4 * size, 9: size, 10: size, 11: size, 12: size}
    outs = run_outputs(
        (layer_out, input_grad, pool_grad),
        (in_grad, mix_grad, up_grad, down_grad),
        sums,
        sizes,
        class_bias.shape[0],
        size,
    )
    layer_out, input_grad, pool_grad, in_grad, mix_grad, up_grad, down_grad = outs[:7]
    of_in, of_mix, of_gain_one, of_shift_one, of_up, of_down, of_gain_two, of_shift_two, of_pool = outs[7:16]
    class_grad, class_bias_grad = outs[16:]
    return (
        layer_out,
        input_grad,
        in_grad,
        of_in,
        mix_grad,
        of_mix,
        of_gain_one,
        of_shift_one,
        up_grad,
        of_up,
        down_grad,
        of_down,
        of_gain_two,
        of_shift_two,
        pool_grad,
        of_pool,
        class_grad.T,
        class_bias_grad,
    )


def plain_body(
    tokens,
    in_weight,
    in_bias,
    mix_weight,
    mix_bias,
    first_gain,
    first_shift,
    up_weight,
    up_bias,
    down_weight,
    down_bias,
    second_gain,
    second_shift,
    pool_weight,
    pool_bias,
    class_weight,
    class_bias,
    lengths,
    labels,
    cotangent,
):
    gathered = (
        lax.all_gather(in_weight, "fsdp", axis=0, tiled=True),
        lax.all_gather(in_bias, "fsdp", axis=0, tiled=True),
        lax.all_gather(mix_weight, "fsdp", axis=0, tiled=True),
        lax.all_gather(mix_bias, "fsdp", axis=0, tiled=True),
        lax.all_gather(first_gain, "fsdp", axis=0, tiled=True),
        lax.all_gather(first_shift, "fsdp", axis=0, tiled=True),
        lax.all_gather(up_weight, "fsdp", axis=0, tiled=True),
        lax.all_gather(up_bias, "fsdp", axis=0, tiled=True),
        lax.all_gather(down_weight, "fsdp", axis=0, tiled=True),
        lax.all_gather(down_bias, "fsdp", axis=0, tiled=True),
        lax.all_gather(second_gain, "fsdp", axis=0, tiled=True),
        lax.all_gather(second_shift, "fsdp", axis=0, tiled=True),
        lax.all_gather(pool_weight, "fsdp", axis=0, tiled=True),
        lax.all_gather(pool_bias, "fsdp", axis=0, tiled=True),
        lax.all_gather(class_weight, "fsdp", axis=0, tiled=True),
    )
    (
        whole_in,
        bias_in,
        whole_mix,
        bias_mix,
        gain_one,
        shift_one,
        whole_up,
        bias_up,
        whole_down,
        bias_down,
        gain_two,
        shift_two,
        whole_pool,
        bias_pool,
        whole_class,
    ) = gathered
    token_rows = tokens.shape[0]
    seq_count = lengths.shape[0]
    seq_len = token_rows // seq_count
    model_width = whole_mix.shape[0]
    score_scale = 1.0 / math.sqrt(DH)
    positions = jnp.arange(seq_len)
    projected = jnp.dot(tokens, whole_in, preferred_element_type=jnp.float32)
    in_bias_f = bias_in.astype(jnp.float32)
    head_shape = (seq_count, seq_len, H, DH)
    queries = (
        (projected[:, :model_width] + in_bias_f[:model_width])
        .astype(jnp.bfloat16)
        .reshape(head_shape)
    )
    keys_all = projected[:, model_width : 2 * model_width].astype(jnp.bfloat16).reshape(head_shape)
    values_all = (
        (projected[:, 2 * model_width :] + in_bias_f[model_width:])
        .astype(jnp.bfloat16)
        .reshape(head_shape)
    )

    def scores_of(query_blk, key_blk, length):
        raw_scores = (
            jnp.einsum("qhd,khd->hqk", query_blk, key_blk, preferred_element_type=jnp.float32)
            * score_scale
        )
        return jnp.where(positions[None, None, :] < length, raw_scores, -1e30)

    def attend_fore(block_items):
        query_blk, key_blk, value_blk, length = block_items
        scores = scores_of(query_blk, key_blk, length)
        highest = jnp.max(scores, axis=-1, keepdims=True)
        raw_weights = jnp.exp(scores - highest)
        totals = jnp.sum(raw_weights, axis=-1, keepdims=True)
        softmaxed = (raw_weights / totals).astype(jnp.bfloat16)
        mixed_values = jnp.einsum(
            "hqk,khd->qhd", softmaxed, value_blk, preferred_element_type=jnp.float32
        )
        return (mixed_values, (highest + jnp.log(totals))[..., 0])

    attended, logsum = lax.map(attend_fore, (queries, keys_all, values_all, lengths))
    attn_low = attended.reshape(token_rows, model_width).astype(jnp.bfloat16)
    branch = jnp.dot(attn_low, whole_mix, preferred_element_type=jnp.float32) + bias_mix.astype(
        jnp.float32
    )
    first_norm, unit_one, inverse_one = norm_fore(
        tokens.astype(jnp.float32) + branch,
        gain_one.astype(jnp.float32),
        shift_one.astype(jnp.float32),
    )
    first_low = first_norm.astype(jnp.bfloat16)
    pre_act = jnp.dot(first_low, whole_up, preferred_element_type=jnp.float32) + bias_up.astype(
        jnp.float32
    )
    activated, gelu_pull = jax.vjp(partial(jax.nn.gelu, approximate=False), pre_act)
    act_low = activated.astype(jnp.bfloat16)
    ffn_out = jnp.dot(act_low, whole_down, preferred_element_type=jnp.float32) + bias_down.astype(
        jnp.float32
    )
    result, unit_two, inverse_two = norm_fore(
        first_norm + ffn_out, gain_two.astype(jnp.float32), shift_two.astype(jnp.float32)
    )
    head_rows = result.reshape(seq_count, seq_len, model_width)[:, 0, :].astype(jnp.bfloat16)
    pooled = jnp.tanh(
        jnp.dot(head_rows, whole_pool, preferred_element_type=jnp.float32)
        + bias_pool.astype(jnp.float32)
    )
    pooled_low = pooled.astype(jnp.bfloat16)
    logits = jnp.dot(
        pooled_low, whole_class, preferred_element_type=jnp.float32
    ) + class_bias.astype(jnp.float32)
    back_in, back_mix, back_gain_one, back_up, back_down, back_gain_two, back_pool, back_class = (
        lax.all_gather(in_weight, "fsdp", axis=0, tiled=True),
        lax.all_gather(mix_weight, "fsdp", axis=0, tiled=True),
        lax.all_gather(first_gain, "fsdp", axis=0, tiled=True),
        lax.all_gather(up_weight, "fsdp", axis=0, tiled=True),
        lax.all_gather(down_weight, "fsdp", axis=0, tiled=True),
        lax.all_gather(second_gain, "fsdp", axis=0, tiled=True),
        lax.all_gather(pool_weight, "fsdp", axis=0, tiled=True),
        lax.all_gather(class_weight, "fsdp", axis=0, tiled=True),
    )
    onehot = (labels[:, None] == jnp.arange(logits.shape[1])[None, :]).astype(jnp.float32)
    grad_logits = (jax.nn.softmax(logits, axis=-1) - onehot).astype(jnp.bfloat16)
    grad_class_weight = jnp.dot(pooled_low.T, grad_logits, preferred_element_type=jnp.float32)
    grad_class_bias = column_sums(grad_logits)
    grad_pool_pre = (
        jnp.dot(grad_logits, back_class.T, preferred_element_type=jnp.float32)
        * (1.0 - pooled * pooled)
    ).astype(jnp.bfloat16)
    grad_pool_weight = jnp.dot(head_rows.T, grad_pool_pre, preferred_element_type=jnp.float32)
    grad_pool_bias = column_sums(grad_pool_pre)
    grad_head_rows = jnp.dot(grad_pool_pre, back_pool.T, preferred_element_type=jnp.float32)
    live_mask = (positions[None, :] < lengths[:, None]).astype(jnp.float32)
    grad_result = (
        cotangent.astype(jnp.float32).reshape(seq_count, seq_len, model_width)
        * live_mask[:, :, None]
    )
    grad_result = grad_result.at[:, 0, :].add(grad_head_rows).reshape(token_rows, model_width)
    grad_sum_two, grad_second_gain, grad_second_shift = norm_back(
        grad_result, unit_two, inverse_two, back_gain_two.astype(jnp.float32)
    )
    grad_ffn = grad_sum_two.astype(jnp.bfloat16)
    grad_down_weight = jnp.dot(act_low.T, grad_ffn, preferred_element_type=jnp.float32)
    grad_down_bias = column_sums(grad_ffn)
    grad_pre = gelu_pull(jnp.dot(grad_ffn, back_down.T, preferred_element_type=jnp.float32))[
        0
    ].astype(jnp.bfloat16)
    grad_up_weight = jnp.dot(first_low.T, grad_pre, preferred_element_type=jnp.float32)
    grad_up_bias = column_sums(grad_pre)
    grad_first_norm = grad_sum_two + jnp.dot(
        grad_pre, back_up.T, preferred_element_type=jnp.float32
    )
    grad_sum_one, grad_first_gain, grad_first_shift = norm_back(
        grad_first_norm, unit_one, inverse_one, back_gain_one.astype(jnp.float32)
    )
    grad_branch = grad_sum_one.astype(jnp.bfloat16)
    grad_mix_weight = jnp.dot(attn_low.T, grad_branch, preferred_element_type=jnp.float32)
    grad_mix_bias = column_sums(grad_branch)
    grad_attended = (
        jnp.dot(grad_branch, back_mix.T, preferred_element_type=jnp.float32)
        .astype(jnp.bfloat16)
        .reshape(head_shape)
    )

    def attend_back(block_items):
        query_blk, key_blk, value_blk, length, lse_blk, grad_blk = block_items
        softmaxed = jnp.exp(scores_of(query_blk, key_blk, length) - lse_blk[..., None])
        grad_value = jnp.einsum(
            "hqk,qhd->khd",
            softmaxed.astype(jnp.bfloat16),
            grad_blk,
            preferred_element_type=jnp.float32,
        )
        grad_soft = jnp.einsum(
            "qhd,khd->hqk", grad_blk, value_blk, preferred_element_type=jnp.float32
        )
        grad_scores = (
            softmaxed * (grad_soft - jnp.sum(softmaxed * grad_soft, axis=-1, keepdims=True))
        ).astype(jnp.bfloat16)
        grad_query = (
            jnp.einsum("hqk,khd->qhd", grad_scores, key_blk, preferred_element_type=jnp.float32)
            * score_scale
        )
        grad_key = (
            jnp.einsum("hqk,qhd->khd", grad_scores, query_blk, preferred_element_type=jnp.float32)
            * score_scale
        )
        return (grad_query, grad_key, grad_value)

    grad_queries, grad_keys, grad_values = lax.map(
        attend_back, (queries, keys_all, values_all, lengths, logsum, grad_attended)
    )
    grad_proj = jnp.concatenate(
        [
            grad_queries.reshape(token_rows, model_width),
            grad_keys.reshape(token_rows, model_width),
            grad_values.reshape(token_rows, model_width),
        ],
        axis=1,
    ).astype(jnp.bfloat16)
    grad_in_weight = jnp.dot(tokens.T, grad_proj, preferred_element_type=jnp.float32)
    proj_sums = column_sums(grad_proj)
    grad_in_bias = jnp.concatenate([proj_sums[:model_width], proj_sums[2 * model_width :]])
    input_grad = grad_sum_one + jnp.dot(grad_proj, back_in.T, preferred_element_type=jnp.float32)
    gradients = (
        grad_in_weight,
        grad_in_bias,
        grad_mix_weight,
        grad_mix_bias,
        grad_first_gain,
        grad_first_shift,
        grad_up_weight,
        grad_up_bias,
        grad_down_weight,
        grad_down_bias,
        grad_second_gain,
        grad_second_shift,
        grad_pool_weight,
        grad_pool_bias,
        grad_class_weight,
    )
    shard_sums = (
        lax.psum_scatter(gradients[0], "fsdp", scatter_dimension=0, tiled=True),
        lax.psum_scatter(gradients[1], "fsdp", scatter_dimension=0, tiled=True),
        lax.psum_scatter(gradients[2], "fsdp", scatter_dimension=0, tiled=True),
        lax.psum_scatter(gradients[3], "fsdp", scatter_dimension=0, tiled=True),
        lax.psum_scatter(gradients[4], "fsdp", scatter_dimension=0, tiled=True),
        lax.psum_scatter(gradients[5], "fsdp", scatter_dimension=0, tiled=True),
        lax.psum_scatter(gradients[6], "fsdp", scatter_dimension=0, tiled=True),
        lax.psum_scatter(gradients[7], "fsdp", scatter_dimension=0, tiled=True),
        lax.psum_scatter(gradients[8], "fsdp", scatter_dimension=0, tiled=True),
        lax.psum_scatter(gradients[9], "fsdp", scatter_dimension=0, tiled=True),
        lax.psum_scatter(gradients[10], "fsdp", scatter_dimension=0, tiled=True),
        lax.psum_scatter(gradients[11], "fsdp", scatter_dimension=0, tiled=True),
        lax.psum_scatter(gradients[12], "fsdp", scatter_dimension=0, tiled=True),
        lax.psum_scatter(gradients[13], "fsdp", scatter_dimension=0, tiled=True),
        lax.psum_scatter(gradients[14], "fsdp", scatter_dimension=0, tiled=True),
    )
    summed = (
        lax.psum(shard_sums[0].astype(jnp.bfloat16), "dp").astype(jnp.float32),
        lax.psum(shard_sums[1].astype(jnp.bfloat16), "dp").astype(jnp.float32),
        lax.psum(shard_sums[2].astype(jnp.bfloat16), "dp").astype(jnp.float32),
        lax.psum(shard_sums[3].astype(jnp.bfloat16), "dp").astype(jnp.float32),
        lax.psum(shard_sums[4].astype(jnp.bfloat16), "dp").astype(jnp.float32),
        lax.psum(shard_sums[5].astype(jnp.bfloat16), "dp").astype(jnp.float32),
        lax.psum(shard_sums[6].astype(jnp.bfloat16), "dp").astype(jnp.float32),
        lax.psum(shard_sums[7].astype(jnp.bfloat16), "dp").astype(jnp.float32),
        lax.psum(shard_sums[8].astype(jnp.bfloat16), "dp").astype(jnp.float32),
        lax.psum(shard_sums[9].astype(jnp.bfloat16), "dp").astype(jnp.float32),
        lax.psum(shard_sums[10].astype(jnp.bfloat16), "dp").astype(jnp.float32),
        lax.psum(shard_sums[11].astype(jnp.bfloat16), "dp").astype(jnp.float32),
        lax.psum(shard_sums[12].astype(jnp.bfloat16), "dp").astype(jnp.float32),
        lax.psum(shard_sums[13].astype(jnp.bfloat16), "dp").astype(jnp.float32),
        lax.psum(shard_sums[14].astype(jnp.bfloat16), "dp").astype(jnp.float32),
    )
    bias_total = lax.psum(grad_class_bias, ("dp", "fsdp"))
    return (
        result.astype(jnp.bfloat16),
        input_grad,
        summed[0],
        summed[1],
        summed[2],
        summed[3],
        summed[4],
        summed[5],
        summed[6],
        summed[7],
        summed[8],
        summed[9],
        summed[10],
        summed[11],
        summed[12],
        summed[13],
        summed[14],
        bias_total,
    )


def solution(mesh):
    in_specs = (
        P(("dp", "fsdp"), None),
        P("fsdp", None),
        P("fsdp"),
        P("fsdp", None),
        P("fsdp"),
        P("fsdp"),
        P("fsdp"),
        P("fsdp", None),
        P("fsdp"),
        P("fsdp", None),
        P("fsdp"),
        P("fsdp"),
        P("fsdp"),
        P("fsdp", None),
        P("fsdp"),
        P("fsdp", None),
        P(),
        P(("dp", "fsdp")),
        P(("dp", "fsdp")),
        P(("dp", "fsdp"), None),
    )
    out_specs = (
        P(("dp", "fsdp"), None),
        P(("dp", "fsdp"), None),
        P("fsdp", None),
        P("fsdp"),
        P("fsdp", None),
        P("fsdp"),
        P("fsdp"),
        P("fsdp"),
        P("fsdp", None),
        P("fsdp"),
        P("fsdp", None),
        P("fsdp"),
        P("fsdp"),
        P("fsdp"),
        P("fsdp", None),
        P("fsdp"),
        P("fsdp", None),
        P(),
    )
    dp_size, fsdp_size = mesh.shape["dp"], mesh.shape["fsdp"]
    body = partial(kernel_body, fsdp_size) if (dp_size, fsdp_size) == (4, 8) else plain_body
    return jax.shard_map(body, mesh=mesh, in_specs=in_specs, out_specs=out_specs, check_vma=False)
```

```python
import functools
from functools import partial
import math

import jax
import jax.numpy as jnp
from jax import lax
from jax.experimental import pallas as pl
from jax.experimental.pallas import tpu as pltpu
from jax.sharding import PartitionSpec as P

H = 12
DH = 64


EPSILON = 1e-06


def norm_fore(vector, norm_gain, norm_shift):
    average = jnp.mean(vector, axis=-1, keepdims=True)
    centered = vector - average
    inverse = lax.rsqrt(jnp.mean(centered * centered, axis=-1, keepdims=True) + EPSILON)
    normed = centered * inverse
    return (normed * norm_gain + norm_shift, normed, inverse)


def norm_back(gradient, normed, inverse, norm_gain):
    scaled = gradient * norm_gain
    inner_mean = jnp.mean(scaled, axis=-1, keepdims=True)
    cross_mean = jnp.mean(scaled * normed, axis=-1, keepdims=True)
    input_part = inverse * (scaled - inner_mean - normed * cross_mean)
    return (input_part, jnp.sum(gradient * normed, axis=0), jnp.sum(gradient, axis=0))


def column_sums(matrix):
    return jnp.sum(matrix.astype(jnp.float32), axis=0)


MESH = pl.DeviceIdType.MESH


def remote(src, dst, send_sem, recv_sem, target):
    return pltpu.make_async_remote_copy(
        src_ref=src, dst_ref=dst, send_sem=send_sem, recv_sem=recv_sem, device_id=target, device_id_type=MESH
    )


class Place:
    def __init__(self, fsdp_size):
        self.dp = lax.axis_index("dp")
        self.shard = lax.axis_index("fsdp")
        self.line = fsdp_size // 2
        self.row_half, self.col_half = self.dp // 2, lax.rem(self.dp, 2)
        self.spot, self.core = self.shard // 2, lax.rem(self.shard, 2)
        across = 2 * self.row_half + (1 - self.col_half)
        along = 2 * (1 - self.row_half) + self.col_half
        self.first = jnp.where(self.core == 0, across, along)
        self.second = jnp.where(self.core == 0, along, across)

    def partner(self):
        return {"dp": self.dp, "fsdp": 2 * self.spot + 1 - self.core}

    def on_line(self, hop):
        return {"dp": self.dp, "fsdp": 2 * lax.rem(self.spot + hop, self.line) + self.core}

    def in_plane(self, dp):
        return {"dp": dp, "fsdp": self.shard}

    def source_spot(self, hop):
        return lax.rem(self.spot + self.line - hop, self.line)

    def peers(self):
        return (
            [self.partner()]
            + [self.on_line(hop) for hop in range(1, self.line)]
            + [self.in_plane(lax.rem(self.dp + step, 4)) for step in range(1, 4)]
        )

    def meet(self):
        barrier = pltpu.get_barrier_semaphore()
        peers = self.peers()
        for peer in peers:
            pl.semaphore_signal(barrier, inc=1, device_id=peer, device_id_type=MESH)
        pl.semaphore_wait(barrier, len(peers))


class Gather:
    def __init__(self, place, shard_ref, whole_ref, send_sems, recv_sems):
        self.place, self.shard_ref, self.whole = place, shard_ref, whole_ref
        self.send_sems, self.recv_sems = send_sems, recv_sems
        self.rows, self.cols = shard_ref.shape
        self.hops = place.line - 1
        self.started = []

    @staticmethod
    def sems(line):
        return 5 * (line - 1) + 2

    def block(self, shard):
        return self.whole.at[shard // 2, lax.rem(shard, 2)]

    def quarter(self, shard, row_half, col_half):
        half_rows, half_cols = self.rows // 2, self.cols // 2
        return self.whole.at[
            shard // 2,
            lax.rem(shard, 2),
            pl.ds(pl.multiple_of(row_half * half_rows, 16), half_rows),
            pl.ds(pl.multiple_of(col_half * half_cols, 128), half_cols),
        ]

    def go(self, index, src, dst, target):
        remote(src, dst, self.send_sems.at[index], self.recv_sems.at[index], target).start()
        self.started.append((index, dst.shape[-2:]))

    def arrived(self, index, dst):
        remote(dst, dst, self.send_sems.at[index], self.recv_sems.at[index], self.place.partner()).wait_recv()

    def begin(self):
        p = self.place
        half_rows, half_cols = self.rows // 2, self.cols // 2
        piece = self.shard_ref.at[
            pl.ds(pl.multiple_of(p.row_half * half_rows, 16), half_rows),
            pl.ds(pl.multiple_of(p.col_half * half_cols, 128), half_cols),
        ]
        for hop in range(1, p.line):
            self.go(hop - 1, piece, self.quarter(p.shard, p.row_half, p.col_half), p.on_line(hop))
        self.go(4 * self.hops, self.shard_ref, self.block(p.shard), p.partner())
        self.own().start()

    def own(self):
        return pltpu.make_async_copy(
            self.shard_ref, self.block(self.place.shard), self.recv_sems.at[5 * self.hops + 1]
        )

    def source(self, hop):
        return 2 * self.place.source_spot(hop) + self.place.core

    def spread(self, hop):
        p = self.place
        quarter = self.quarter(self.source(hop), p.row_half, p.col_half)
        self.arrived(hop - 1, quarter)
        self.go(self.hops + hop - 1, quarter, quarter, p.in_plane(p.first))
        self.go(2 * self.hops + hop - 1, quarter, quarter, p.in_plane(p.second))

    def relay(self, hop):
        p = self.place
        quarter = self.quarter(self.source(hop), p.first // 2, lax.rem(p.first, 2))
        self.arrived(self.hops + hop - 1, quarter)
        self.go(3 * self.hops + hop - 1, quarter, quarter, p.in_plane(p.second))

    def hand(self, hop):
        p = self.place
        self.arrived(2 * self.hops + hop - 1, self.quarter(self.source(hop), p.second // 2, lax.rem(p.second, 2)))
        self.arrived(3 * self.hops + hop - 1, self.quarter(self.source(hop), 1 - p.row_half, 1 - p.col_half))
        block = self.block(self.source(hop))
        self.go(4 * self.hops + hop, block, block, p.partner())

    def ready(self):
        p = self.place
        self.own().wait()
        self.arrived(4 * self.hops, self.block(p.shard + 1 - 2 * p.core))
        for hop in range(1, p.line):
            self.arrived(4 * self.hops + hop, self.block(2 * p.source_spot(hop) + 1 - p.core))

    def end(self):
        for index, (rows, cols) in self.started:
            like = self.whole.at[0, 0, pl.ds(0, rows), pl.ds(0, cols)]
            remote(like, like, self.send_sems.at[index], self.recv_sems.at[index], self.place.partner()).wait_send()


class SmallGather:
    def __init__(self, place, own_ref, all_ref, send_sems, recv_sems):
        self.place, self.own_ref, self.all = place, own_ref, all_ref
        self.send_sems, self.recv_sems = send_sems, recv_sems
        self.hops = place.line - 1
        self.started = []

    def at(self, shard):
        rows, cols = self.own_ref.shape
        return self.all.at[pl.ds(pl.multiple_of(shard * rows, rows), rows), pl.ds(0, cols)]

    @staticmethod
    def sems(line):
        return 2 * (line - 1) + 2

    def go(self, index, src, dst, target):
        copy = remote(src, dst, self.send_sems.at[index], self.recv_sems.at[index], target)
        copy.start()
        self.started.append(copy)

    def arrived(self, index, dst):
        remote(dst, dst, self.send_sems.at[index], self.recv_sems.at[index], self.place.partner()).wait_recv()

    def begin(self):
        p = self.place
        for hop in range(1, p.line):
            self.go(hop - 1, self.own_ref, self.at(p.shard), p.on_line(hop))
        self.go(2 * self.hops, self.own_ref, self.at(p.shard), p.partner())
        self.own = pltpu.make_async_copy(self.own_ref, self.at(p.shard), self.recv_sems.at[2 * self.hops + 1])
        self.own.start()

    def hand(self):
        p = self.place
        for hop in range(1, p.line):
            block = self.at(2 * p.source_spot(hop) + p.core)
            self.arrived(hop - 1, block)
            self.go(self.hops + hop - 1, block, block, p.partner())

    def ready(self):
        p = self.place
        self.own.wait()
        self.arrived(2 * self.hops, self.at(p.shard + 1 - 2 * p.core))
        for hop in range(1, p.line):
            self.arrived(self.hops + hop - 1, self.at(2 * p.source_spot(hop) + 1 - p.core))

    def end(self):
        for copy in self.started:
            copy.wait_send()


class Scatter:
    def __init__(self, place, grad, from_core, from_first, from_second, from_line, done, send_sems, recv_sems):
        self.place, self.grad = place, grad
        self.from_core, self.from_first, self.from_second = from_core, from_first, from_second
        self.from_line, self.done = from_line, done
        self.send_sems, self.recv_sems = send_sems, recv_sems
        self.line, _, self.rows, self.cols = grad.shape

    @staticmethod
    def sems(line):
        return 1 + 2 + 1 + (line - 1) + 3

    @staticmethod
    def scratch(line, rows, cols):
        half = (rows // 2, cols // 2)
        return [
            pltpu.VMEM((line, rows, cols), jnp.bfloat16),
            pltpu.VMEM((2, line) + half, jnp.bfloat16),
            pltpu.VMEM((line,) + half, jnp.bfloat16),
            pltpu.VMEM((line - 1,) + half, jnp.bfloat16),
            pltpu.VMEM((2, 2) + half, jnp.bfloat16),
        ]

    def go(self, index, src, dst, target):
        remote(src, dst, self.send_sems.at[index], self.recv_sems.at[index], target).start()

    def arrived(self, index, dst):
        remote(dst, dst, self.send_sems.at[index], self.recv_sems.at[index], self.place.partner()).wait_recv()

    def slices(self, row_half, col_half):
        half_rows, half_cols = self.rows // 2, self.cols // 2
        return (
            pl.ds(pl.multiple_of(row_half * half_rows, 16), half_rows),
            pl.ds(pl.multiple_of(col_half * half_cols, 128), half_cols),
        )

    def halves(self, side, which):
        p = self.place
        row_half = which * (1 - p.core) + side * p.core
        col_half = side * (1 - p.core) + which * p.core
        return self.slices(row_half, col_half)

    def swap(self):
        p = self.place
        self.go(0, self.grad.at[:, 1 - p.core], self.from_core, p.partner())

    def add(self, rows, cols, others, targets_spot=None):
        p = self.place
        half_rows, half_cols = self.rows // 2, self.cols // 2
        step = next(size for size in (64, 48, 32, 16) if half_rows % size == 0)
        steps = half_rows // step

        def one(index, carry):
            spot, part = index // steps, lax.rem(index, steps)
            at = pl.ds(pl.multiple_of(rows.start + part * step, 16), step)
            inner = pl.ds(pl.multiple_of(part * step, 16), step)
            total = self.grad[spot, p.core, at, cols].astype(jnp.float32) + self.from_core[spot, at, cols].astype(
                jnp.float32
            )
            for other in others:
                total = total + other[spot, inner, :].astype(jnp.float32)
            self.grad[spot, p.core, at, cols] = total.astype(jnp.bfloat16)
            return carry

        lax.fori_loop(0, self.line * steps, one, 0)

    def to_first(self):
        p = self.place
        self.arrived(0, self.from_core)
        keep = jnp.where(p.core == 0, p.col_half, p.row_half)
        for which in (0, 1):
            rows, cols = self.halves(1 - keep, which)
            self.add(rows, cols, [])
            self.go(1 + which, self.grad.at[:, p.core, rows, cols], self.from_first.at[which], p.in_plane(p.first))

    def to_second(self):
        p = self.place
        for which in (0, 1):
            self.arrived(1 + which, self.from_first.at[which])
        keep = jnp.where(p.core == 0, p.col_half, p.row_half)
        mine = jnp.where(p.core == 0, p.row_half, p.col_half)
        rows, cols = self.halves(keep, 1 - mine)
        self.add(rows, cols, [self.from_first.at[1 - mine]])
        self.go(3, self.grad.at[:, p.core, rows, cols], self.from_second, p.in_plane(p.second))

    def to_line(self):
        p = self.place
        self.arrived(3, self.from_second)
        mine = jnp.where(p.core == 0, p.row_half, p.col_half)
        rows, cols = self.slices(p.row_half, p.col_half)
        self.add(rows, cols, [self.from_first.at[mine], self.from_second])
        for hop in range(1, self.line):
            spot = lax.rem(p.spot + hop, self.line)
            self.go(3 + hop, self.grad.at[spot, p.core, rows, cols], self.from_line.at[hop - 1], p.on_line(hop))

    def to_plane(self):
        p = self.place
        for hop in range(1, self.line):
            self.arrived(3 + hop, self.from_line.at[hop - 1])
        half_rows = self.rows // 2
        rows, cols = self.slices(p.row_half, p.col_half)
        step = 16

        def one(part, carry):
            at = pl.ds(pl.multiple_of(rows.start + part * step, 16), step)
            inner = pl.ds(pl.multiple_of(part * step, 16), step)
            total = self.grad[p.spot, p.core, at, cols].astype(jnp.float32)
            for hop in range(1, self.line):
                total = total + self.from_line[hop - 1, inner, :].astype(jnp.float32)
            self.done[p.row_half, p.col_half, inner, :] = total.astype(jnp.bfloat16)
            return carry

        lax.fori_loop(0, half_rows // step, one, 0)
        own = self.done.at[p.row_half, p.col_half]
        for step in range(1, 4):
            self.go(2 + self.line + step, own, own, p.in_plane(lax.rem(p.dp + step, 4)))

    def finish(self):
        p = self.place
        for step in range(1, 4):
            other = lax.rem(p.dp + 4 - step, 4)
            self.arrived(2 + self.line + step, self.done.at[other // 2, lax.rem(other, 2)])

    def end(self):
        third = 2 + self.line
        landed = {0: self.from_core, 1: self.from_first.at[0], 2: self.from_first.at[0], 3: self.from_second}
        for hop in range(1, self.line):
            landed[3 + hop] = self.from_line.at[0]
        for step in range(1, 4):
            landed[third + step] = self.done.at[0, 0]
        for index, like in landed.items():
            remote(like, like, self.send_sems.at[index], self.recv_sems.at[index], self.place.partner()).wait_send()


class SmallSum:
    def __init__(self, place, own, from_core, on_line, in_plane, send_sems, recv_sems):
        self.place, self.own, self.from_core, self.on_line, self.in_plane = place, own, from_core, on_line, in_plane
        self.send_sems, self.recv_sems = send_sems, recv_sems
        self.started = []

    @staticmethod
    def sems(line):
        return 1 + (line - 1) + 3

    @staticmethod
    def scratch(line, rows, cols):
        return [
            pltpu.VMEM((rows, cols), jnp.float32),
            pltpu.VMEM((rows, cols), jnp.float32),
            pltpu.VMEM((line, rows, cols), jnp.float32),
            pltpu.VMEM((4, rows, cols), jnp.float32),
        ]

    def go(self, index, src, dst, target):
        copy = remote(src, dst, self.send_sems.at[index], self.recv_sems.at[index], target)
        copy.start()
        self.started.append(copy)

    def arrived(self, index, dst):
        remote(dst, dst, self.send_sems.at[index], self.recv_sems.at[index], self.place.partner()).wait_recv()

    def swap(self):
        self.go(0, self.own, self.from_core, self.place.partner())

    def to_line(self):
        p = self.place
        self.arrived(0, self.from_core)
        self.on_line[p.spot] = self.own[...] + self.from_core[...]
        slot = self.on_line.at[p.spot]
        for hop in range(1, p.line):
            self.go(hop, slot, slot, p.on_line(hop))

    def to_plane(self):
        p = self.place
        for hop in range(1, p.line):
            self.arrived(hop, self.on_line.at[p.source_spot(hop)])
        total = self.on_line[0]
        for spot in range(1, p.line):
            total = total + self.on_line[spot]
        self.in_plane[p.dp] = total
        slot = self.in_plane.at[p.dp]
        for step in range(1, 4):
            self.go(p.line - 1 + step, slot, slot, p.in_plane(lax.rem(p.dp + step, 4)))

    def finish(self, out_ref):
        p = self.place
        for step in range(1, 4):
            self.arrived(p.line - 1 + step, self.in_plane.at[lax.rem(p.dp + 4 - step, 4)])
        out_ref[...] = (self.in_plane[0] + self.in_plane[1]) + (self.in_plane[2] + self.in_plane[3])

    def end(self):
        for copy in self.started:
            copy.wait_send()


class SequenceGather:
    def __init__(self, place, blocks, send_sems, recv_sems):
        self.place, self.blocks = place, blocks
        self.send_sems, self.recv_sems = send_sems, recv_sems
        self.started = []

    @staticmethod
    def sems(line):
        return 3 + (line - 1) + line

    def go(self, index, ref, target):
        remote(ref, ref, self.send_sems.at[index], self.recv_sems.at[index], target).start()
        self.started.append((index, len(ref.shape)))

    def arrived(self, index, dst):
        remote(dst, dst, self.send_sems.at[index], self.recv_sems.at[index], self.place.partner()).wait_recv()

    def begin(self):
        p = self.place
        for step in range(1, 4):
            self.go(step - 1, self.blocks.at[p.shard, p.dp], p.in_plane(lax.rem(p.dp + step, 4)))

    def to_line(self):
        p = self.place
        for step in range(1, 4):
            self.arrived(step - 1, self.blocks.at[p.shard, lax.rem(p.dp + 4 - step, 4)])
        own = self.blocks.at[p.shard]
        for hop in range(1, p.line):
            self.go(2 + hop, own, p.on_line(hop))
        self.go(2 + p.line, own, p.partner())

    def hand(self):
        p = self.place
        for hop in range(1, p.line):
            block = self.blocks.at[2 * p.source_spot(hop) + p.core]
            self.arrived(2 + hop, block)
            self.go(2 + p.line + hop, block, p.partner())

    def ready(self):
        p = self.place
        self.arrived(2 + p.line, self.blocks.at[p.shard + 1 - 2 * p.core])
        for hop in range(1, p.line):
            self.arrived(2 + p.line + hop, self.blocks.at[2 * p.source_spot(hop) + 1 - p.core])

    def end(self):
        for index, rank in self.started:
            like = self.blocks.at[0] if rank == 3 else self.blocks.at[0, 0]
            remote(like, like, self.send_sems.at[index], self.recv_sems.at[index], self.place.partner()).wait_send()
ANY = pl.BlockSpec(memory_space=pl.ANY)
WHOLE = pl.BlockSpec(memory_space=pltpu.VMEM)
SCALARS = pl.BlockSpec(memory_space=pltpu.SMEM)
VMEM_BYTES = 67_043_328
AHEAD = 4
BF16, F32 = jnp.bfloat16, jnp.float32


def nn(left, right):
    return lax.dot_general(left, right, (((1,), (0,)), ((), ())), preferred_element_type=F32)


def nt(left, right):
    return lax.dot_general(left, right, (((1,), (1,)), ((), ())), preferred_element_type=F32)


def tn(left, right):
    return lax.dot_general(left, right, (((0,), (0,)), ((), ())), preferred_element_type=F32)


def lanes(start, size):
    return pl.ds(pl.multiple_of(start, 128), size)


def loop(count, step):
    def one(index, carry):
        step(index)
        return carry

    lax.fori_loop(0, count, one, 0)


def gelu_parts(v):
    spread = 0.5 * (1.0 + lax.erf(v * (1.0 / math.sqrt(2.0))))
    bell = jnp.exp(-0.5 * v * v) * (1.0 / math.sqrt(2.0 * math.pi))
    return v * spread, spread + v * bell


def place_vectors(shard, vectors, class_rows, short, out):
    in_bias, mix_bias, gain_one, shift_one, up_bias, down_bias, gain_two, shift_two, pool_bias = vectors
    short[...] = jnp.zeros(short.shape, F32)
    rows = [in_bias, in_bias, mix_bias, gain_one, shift_one, up_bias, up_bias, up_bias, up_bias]
    rows += [down_bias, gain_two, shift_two, pool_bias]
    for row, vector in enumerate(rows):
        size = vector.shape[0]
        short[row : row + 1, 0:size] = vector[...].astype(F32).reshape(1, size)
    size = class_rows.shape[1]
    short[13 : 13 + class_rows.shape[0], 0:size] = class_rows[...].astype(F32)
    values = short[...].astype(BF16)
    span, width = short.shape[1], out.shape[1]
    lane = lax.broadcasted_iota(jnp.int32, (span, width), 0)
    column = lax.broadcasted_iota(jnp.int32, (span, width), 1)
    row_at = lax.broadcasted_iota(jnp.int32, (16, 1), 0)

    def placed(size):
        per_row = width // size
        spread = jnp.where((column - lax.rem(shard, per_row) * size == lane) & (lane < size), 1.0, 0.0)
        return nn(values, spread.astype(BF16)), shard // per_row

    one_row, _ = placed(mix_bias.shape[0])
    of_in, in_row = placed(in_bias.shape[0])
    of_up, up_row = placed(up_bias.shape[0])
    is_in, is_up = row_at < 2, (row_at >= 5) & (row_at < 9)
    result = jnp.where(is_in, jnp.where(row_at == in_row, of_in, 0.0), one_row)
    result = jnp.where(is_up, jnp.where(row_at == 5 + up_row, of_up, 0.0), result)
    out[...] = result.astype(BF16)


def own_sums(shard, parts, total_ref, out, classes):
    total = total_ref[...]
    width = total.shape[1]
    size = width // parts
    own, own_in, own_up = (jnp.zeros(shape, F32) for shape in ((24, size), (1, 2 * size), (1, 4 * size)))
    for place in range(parts):
        here = shard == place
        own = jnp.where(here, total[:, place * size : (place + 1) * size], own)
        row, at = divmod(2 * size * place, width)
        own_in = jnp.where(here, total[row : row + 1, at : at + 2 * size], own_in)
        row, at = divmod(4 * size * place, width)
        own_up = jnp.where(here, total[5 + row : 6 + row, at : at + 4 * size], own_up)
    out[...] = jnp.zeros(out.shape, F32)
    out[0:24, 0:size] = own
    out[24:25, 0 : 2 * size] = own_in
    out[25:26, 0 : 4 * size] = own_up
    out[26:27, 0:classes] = total[16:17, 13 : 13 + classes]


def layer_kernel(fsdp_size, *refs):
    refs = list(refs)

    def take(count):
        out = refs[:count]
        del refs[:count]
        return out

    lengths, labels, class_bias, tokens_in, cot_in = take(5)
    shards = take(5)
    vectors, class_rows = take(9), take(1)[0]
    layer_out, input_grad, down_out, up_out, mix_out, in_out, pool_out, sums_out = take(8)
    w_in, w_mix, w_up, w_down, w_pool = take(5)
    g_down, g_up = take(2)
    recv = [take(5) for _ in range(7)]
    recv.append([recv[1][0].at[:, pl.ds(0, shards[0].shape[0]), :]] + take(4))
    sum_refs = take(4)
    (blocks,) = take(1)
    tok, tok_t, cot, att, att_t, first, first_t = take(7)
    qkv, act, slope = take(3)
    unit_one, unit_two, grad = take(3)
    inv_one, inv_two, key_mask, lse, vec = take(5)
    short, small_in, bias_row = take(3)
    g_send, g_recv, s_send, s_recv, q_send, q_recv, v_send, v_recv, b_send, b_recv, local = take(11)
    seq, width = tok.shape
    hidden = act.shape[1]
    pairs = width // 128
    parts = hidden // width
    line = fsdp_size // 2
    rows_of = pl.ds

    loads = [
        pltpu.make_async_copy(tokens_in, tok, local.at[0]),
        pltpu.make_async_copy(cot_in, cot, local.at[1]),
    ]
    for load in loads:
        load.start()
    place = Place(fsdp_size)
    place_vectors(place.shard, vectors, class_rows, short, small_in)
    bias_row[...] = jnp.zeros(bias_row.shape, F32)
    classes = class_bias.shape[0]
    bias_row[0:1, 13 : 13 + classes] = class_bias[...].astype(F32).reshape(1, classes)
    place.meet()
    everything, all_rows = [], shards[0].shape[0]
    for shard, whole in zip(shards, (w_in, w_mix, w_up, w_down, w_pool)):
        for row in range(0, shard.shape[0], all_rows):
            for col in range(0, shard.shape[1], width):
                rows, cols = pl.ds(row, all_rows), pl.ds(col, width)
                everything.append((shard.at[rows, cols], whole.at[:, :, rows, cols]))
    gathers = [Gather(place, *pair, g_send.at[i], g_recv.at[i]) for i, pair in enumerate(everything)]
    little = SmallGather(place, small_in, slope, v_send, v_recv)
    hops = range(1, line)
    first_mix, first_up, first_down, first_pool = 3, 4, 4 + parts, 4 + 2 * parts

    def tick(count):
        if count + AHEAD < len(gathers):
            gathers[count + AHEAD].begin()
        if count < len(gathers):
            for hop in hops:
                gathers[count].spread(hop)
        if 0 <= count - 1 < len(gathers):
            for hop in hops:
                gathers[count - 1].relay(hop)
        if 0 <= count - 2 < len(gathers):
            for hop in hops:
                gathers[count - 2].hand(hop)

    gathers[0].begin()
    little.begin()
    for one in gathers[1:AHEAD]:
        one.begin()
    length = lengths[0]
    label = labels[0]

    for load in loads:
        load.wait()
    tok_t[...] = tok[...].T
    key_at = lax.broadcasted_iota(jnp.int32, (seq, 128), 0)
    key_mask[...] = jnp.where(key_at < length, 0.0, -1e30).astype(F32)

    def mask_cot(index):
        rows = rows_of(pl.multiple_of(index * 128, 128), 128)
        live = (key_mask[rows, :] == 0.0).astype(F32)
        grad[rows, :] = cot[rows, :].astype(F32) * jnp.concatenate([live] * (width // 128), axis=1)

    loop(seq // 128, mask_cot)
    grad_low = cot

    tick(0)
    little.hand()
    tick(1)
    little.ready()
    vec[...] = jnp.sum(slope[0 : 16 * fsdp_size, 0:width].reshape(fsdp_size, 16, width).astype(F32), axis=0)

    score_scale = 1.0 / math.sqrt(DH)
    for part in range(3):
        tick(2 + part)
        gathers[part].ready()

        def project(index, part=part):
            inner = lanes(index * 256, 256)
            cols = lanes(part * width + index * 256, 256)
            out = nn(tok[...], w_in[:, :, :, cols].reshape(width, 256))
            if part != 1:
                row = 0 if part == 0 else 1
                out = out + vec[row : row + 1, inner]
            out = out.astype(BF16)
            if part == 0:
                out = out * jnp.asarray(score_scale, BF16)
            qkv[:, cols] = out

        loop(width // 256, project)

    low_lanes = lax.broadcasted_iota(jnp.int32, (1, 128), 1) < 64
    zero_low = jnp.zeros((), BF16)

    def head_lanes(value, half):
        return jnp.where(low_lanes if half == 0 else jnp.logical_not(low_lanes), value, zero_low)

    def masked_scores(keys, queries):
        mask = key_mask[...]
        return nt(keys, queries) + jnp.concatenate([mask] * (seq // 128), axis=1)

    def attend(pair):
        queries, keys, values = (qkv[:, lanes(part * width + pair * 128, 128)] for part in range(3))
        values_t = values.T
        mixed = []
        for half in (0, 1):
            scores = masked_scores(keys, head_lanes(queries, half))
            highest = jnp.max(scores, axis=0, keepdims=True)
            raw = jnp.exp(scores - highest)
            total = jnp.sum(raw, axis=0, keepdims=True)
            lse[pair, half : half + 1, :] = highest + jnp.log(total)
            soft = (raw * (1.0 / total)).astype(BF16)
            mixed.append(nn(values_t, soft)[64 * half : 64 * half + 64, :])
        both = jnp.concatenate(mixed, axis=0)
        att_t[rows_of(pl.multiple_of(pair * 128, 128), 128), :] = both.astype(BF16)
        att[:, lanes(pair * 128, 128)] = both.T.astype(BF16)

    def attend_on(pair):
        attend(pair)
        for one in range(pairs):

            @pl.when(pair == one)
            def _(one=one):
                tick(5 + one)

    loop(pairs, attend_on)
    gathers[first_mix].ready()

    little.end()

    gain_one, shift_one = vec[3:4, :], vec[4:5, :]

    def mean_of(value):
        return jnp.sum(value, axis=1, keepdims=True) * (1.0 / width)

    def norm_one(index):
        rows = rows_of(pl.multiple_of(index * 256, 256), 256)
        total = nn(att[rows, :], w_mix[...].reshape(width, width)) + vec[2:3, :] + tok[rows, :].astype(F32)
        centered = total - mean_of(total)
        inverse = lax.rsqrt(mean_of(centered * centered) + EPSILON)
        unit = centered * inverse
        unit_one[rows, :] = unit
        inv_one[rows, :] = jnp.broadcast_to(inverse, (256, 128))
        first[rows, :] = (unit * gain_one + shift_one).astype(BF16)

    loop(seq // 256, norm_one)
    first_t[...] = first[...].T
    tick(5 + pairs)

    for part in range(parts):
        gathers[first_up + part].ready()

        def raise_up(index, part=part):
            inner = lanes(index * 384, 384)
            cols = lanes(part * width + index * 384, 384)
            pre = nn(first[...], w_up[:, :, :, cols].reshape(width, 384)) + vec[5 + part : 6 + part, inner]
            value, derivative = gelu_parts(pre)
            act[:, cols] = value.astype(BF16)
            slope[:, cols] = derivative.astype(BF16)

        loop(width // 384, raise_up)
        if part < 3:
            tick(6 + pairs + part)
    for one in gathers[first_down:first_pool]:
        one.ready()
    gain_two, shift_two = vec[10:11, :], vec[11:12, :]

    def norm_two(index):
        rows = rows_of(pl.multiple_of(index * 256, 256), 256)
        total = nn(act[rows, :], w_down[...].reshape(hidden, width)) + vec[9:10, :]
        total = total + (unit_one[rows, :] * gain_one + shift_one)
        centered = total - mean_of(total)
        inverse = lax.rsqrt(mean_of(centered * centered) + EPSILON)
        unit = centered * inverse
        unit_two[rows, :] = unit
        inv_two[rows, :] = jnp.broadcast_to(inverse, (256, 128))
        att[rows, :] = (unit * gain_two + shift_two).astype(BF16)

    loop(seq // 256, norm_two)
    stores = [pltpu.make_async_copy(att, layer_out, local.at[2])]
    stores[0].start()

    gathers[first_pool].ready()
    top = lax.broadcasted_iota(jnp.int32, (16, 1), 0) == 0
    head = att[0:16, :]
    vec_low = vec[...].astype(BF16)
    pooled = jnp.tanh(nn(head, w_pool[...].reshape(width, width)) + vec[12:13, :])
    pooled_low = pooled.astype(BF16)
    logits = nt(pooled_low, vec_low) + bias_row[0:1, 0:16]
    class_at = lax.broadcasted_iota(jnp.int32, (16, 16), 1) - 13
    logits = jnp.where(class_at >= 0, logits, -1e30)
    raised = jnp.exp(logits - jnp.max(logits, axis=1, keepdims=True))
    soft_logits = raised / jnp.sum(raised, axis=1, keepdims=True)
    onehot = (class_at == label).astype(F32)
    grad_logits = jnp.where(top, soft_logits - onehot, 0.0).astype(BF16)
    sums = sum_refs[0]
    sums[0:16, :] = tn(grad_logits, pooled_low)
    sums[16:24, :] = jnp.zeros((8, width), F32)
    sums[16:17, 0:16] = grad_logits[0:1, :].astype(F32)
    grad_pool_pre = (nn(grad_logits, vec_low) * (1.0 - pooled * pooled)).astype(BF16)
    sums[12:13, :] = grad_pool_pre[0:1, :].astype(F32)
    block = jnp.where(top, head.astype(F32), 0.0)
    second_row = lax.broadcasted_iota(jnp.int32, (16, 1), 0) == 1
    block = jnp.where(second_row, jnp.broadcast_to(grad_pool_pre[0:1, :].astype(F32), (16, width)), block)
    blocks[place.shard, place.dp] = block.astype(BF16)
    sequences = SequenceGather(place, blocks, q_send, q_recv)
    sequences.begin()
    grad[0:16, :] += nt(grad_pool_pre, w_pool[...].reshape(width, width))

    def norm_back(unit_ref, inv_ref, gain, gain_row, shift_row, bias_row, size):
        def one(index, carry):
            by_gain, by_shift, by_bias = carry
            rows = rows_of(pl.multiple_of(index * size, size), size)
            incoming = grad[rows, :]
            unit = unit_ref[rows, :]
            scaled = incoming * gain
            inverse = jnp.concatenate([inv_ref[rows, :]] * (width // 128), axis=1)
            back = inverse * (scaled - mean_of(scaled) - unit * mean_of(scaled * unit))
            low = back.astype(BF16)
            grad[rows, :] = back
            grad_low[rows, :] = low
            return (
                by_gain + jnp.sum(incoming * unit, axis=0, keepdims=True),
                by_shift + jnp.sum(incoming, axis=0, keepdims=True),
                by_bias + jnp.sum(low.astype(F32), axis=0, keepdims=True),
            )

        zero = jnp.zeros((1, width), F32)
        by_gain, by_shift, by_bias = lax.fori_loop(0, seq // size, one, (zero, zero, zero))
        sums[gain_row : gain_row + 1, :] = by_gain
        sums[shift_row : shift_row + 1, :] = by_shift
        sums[bias_row : bias_row + 1, :] = by_bias

    norm_back(unit_two, inv_two, gain_two, 10, 11, 9, 128)

    rows_down = hidden // fsdp_size
    few = 128
    many = rows_down - few
    pieces = [g_down.at[:, :, pl.ds(many, few), :], g_down.at[:, :, pl.ds(0, many), :]]
    pieces += [g_up.at[:, :, :, pl.ds(half * 2 * width, 2 * width)] for half in (0, 1)]
    pieces += [w_up.at[:, :, :, pl.ds(at * width, width)] for at in (3, 0, 1, 2)]
    scatters = [Scatter(place, ref, *recv[i], s_send.at[i], s_recv.at[i]) for i, ref in enumerate(pieces)]
    down_a, down_b, up_a, up_b, of_mix, in_a, in_b, in_c = scatters

    for first_row, count, one in ((many, few, down_a), (0, many, down_b)):

        def down_gradient(index, first_row=first_row, count=count):
            cols = lanes(index * rows_down + first_row, count)
            out = tn(act[:, cols], grad_low[...]).astype(BF16)
            g_down[index // 2, lax.rem(index, 2), pl.ds(first_row, count), :] = out

        loop(fsdp_size, down_gradient)
        one.swap()
    sequences.to_line()

    for part in range(parts):

        def through_down(index, part=part):
            owner = part * 2 + index
            inner = lanes(index * rows_down, rows_down)
            cols = lanes(owner * rows_down, rows_down)
            low = (nt(grad_low[...], w_down[part, index]) * slope[:, cols].astype(F32)).astype(BF16)
            slope[:, cols] = low
            sums[5 + part : 6 + part, inner] = jnp.sum(low.astype(F32), axis=0, keepdims=True)

        loop(2, through_down)

        def up_gradient(index, part=part):
            cols = lanes(part * width + index * 256, 256)
            out = nn(first_t[...], slope[:, cols]).astype(BF16)
            g_up[:, :, :, cols] = out.reshape(line, 2, width // fsdp_size, 256)

        loop(width // 256, up_gradient)
        if part == 0:
            down_a.to_first()
        if part == 1:
            up_a.swap()
            down_b.to_first()
            down_a.to_second()
        if part == 2:
            up_a.to_first()
            down_a.to_line()
        if part == 3:
            up_b.swap()
            down_b.to_second()
            sequences.hand()

    half_line = line // 2
    half_width = width // 2

    def through_up(index):
        cols = lanes(index * half_width, half_width)
        weight = w_up[rows_of(index * half_line, half_line)].reshape(half_width, hidden)
        grad[:, cols] += nt(slope[...], weight)
        for one in (0, 1):

            @pl.when(index == one)
            def _(one=one):
                if one == 0:
                    up_b.to_first()
                    down_b.to_line()
                else:
                    up_a.to_second()
                    down_a.to_plane()

    loop(2, through_up)
    norm_back(unit_one, inv_one, gain_one, 3, 4, 2, 128)
    for one in gathers:
        one.end()

    def mix_gradient(index):
        out = nn(att_t[...], grad_low[:, lanes(index * 256, 256)]).astype(BF16)
        w_up[:, :, :, lanes(3 * width + index * 256, 256)] = out.reshape(line, 2, width // fsdp_size, 256)

    loop(width // 256, mix_gradient)
    of_mix.swap()
    up_b.to_second()

    def through_mix(index):
        cols = lanes(index * half_width, half_width)
        weight = w_mix[rows_of(index * half_line, half_line)].reshape(half_width, width)
        first[:, cols] = nt(grad_low[...], weight).astype(BF16)

    loop(2, through_mix)
    of_mix.to_first()
    up_a.to_line()

    def attend_back(pair):
        at = [lanes(part * width + pair * 128, 128) for part in range(3)]
        queries, keys, values = (qkv[:, cols] for cols in at)
        rows = rows_of(pl.multiple_of(pair * 128, 128), 128)
        out_grad = first[:, lanes(pair * 128, 128)]
        keys_t = keys.T
        products = out_grad.astype(F32).T * att_t[rows, :].astype(F32)
        by_query, by_key, by_value = [], None, None
        for half in (0, 1):
            own_queries, own_grad = head_lanes(queries, half), head_lanes(out_grad, half)
            soft = jnp.exp(masked_scores(keys, own_queries) - lse[pair, half : half + 1, :])
            row_sum = jnp.sum(products[64 * half : 64 * half + 64, :], axis=0, keepdims=True)
            score_grad = (soft * (nt(values, own_grad) - row_sum)).astype(BF16)
            value_part = nn(soft.astype(BF16), own_grad)
            key_part = nn(score_grad, own_queries)
            by_value = value_part if by_value is None else by_value + value_part
            by_key = key_part if by_key is None else by_key + key_part
            by_query.append(nn(keys_t, score_grad)[64 * half : 64 * half + 64, :])
        qkv[:, at[0]] = (jnp.concatenate(by_query, axis=0).T * score_scale).astype(BF16)
        qkv[:, at[1]] = by_key.astype(BF16)
        qkv[:, at[2]] = by_value.astype(BF16)

    after_pair = {
        0: [down_b.to_plane],
        1: [up_b.to_line, of_mix.to_second],
        2: [in_a.to_first, up_a.to_plane],
        3: [of_mix.to_line, in_a.to_second],
        4: [in_b.to_first, up_b.to_plane],
        5: [in_a.to_line, of_mix.to_plane, in_b.to_second],
    }

    def attend_back_on(pair):
        attend_back(pair)
        for one in range(pairs):

            @pl.when(pair == one)
            def _(one=one):
                for step in after_pair[one]:
                    step()

    def in_gradient(chunk):
        for part in range(3):
            inner = lanes(chunk * 256, 256)
            incoming = qkv[:, lanes(part * width + chunk * 256, 256)]
            out = nn(tok_t[...], incoming).astype(BF16).reshape(line, 2, width // fsdp_size, 256)
            w_up[:, :, :, lanes(chunk * width + part * 256, 256)] = out
            if part != 1:
                row = 0 if part == 0 else 1
                sums[row : row + 1, inner] = jnp.sum(incoming.astype(F32), axis=0, keepdims=True)

    def attend_chunk(chunk):
        lax.fori_loop(2 * chunk, 2 * chunk + 2, lambda pair, carry: (attend_back_on(pair), carry)[1], 0)
        in_gradient(chunk)
        for at, one in enumerate((in_a, in_b, in_c)):

            @pl.when(chunk == at)
            def _(one=one):
                one.swap()

    loop(pairs // 2, attend_chunk)
    sequences.ready()
    total = SmallSum(place, *sum_refs, b_send, b_recv)
    total.swap()

    def through_in(index):
        cols = lanes(index * half_width, half_width)
        weight = w_in[rows_of(index * half_line, half_line)].reshape(half_width, 3 * width)
        grad[:, cols] += nt(qkv[...], weight)
        for one in (0, 1):

            @pl.when(index == one)
            def _(one=one):
                if one == 0:
                    in_c.to_first()
                    in_b.to_line()
                else:
                    in_a.to_plane()

    loop(2, through_in)
    store = pltpu.make_async_copy(grad, input_grad, local.at[3])
    store.start()
    stores.append(store)
    in_c.to_second()
    total.to_line()
    in_b.to_plane()

    every = blocks[...].reshape(fsdp_size * 4 * 16, width)
    count = fsdp_size * 4 * 16
    row_at = lax.broadcasted_iota(jnp.int32, (count, count), 0)
    col_at = lax.broadcasted_iota(jnp.int32, (count, count), 1)
    shift = jnp.where((lax.rem(row_at, 16) == 0) & (col_at == row_at + 1), 1.0, 0.0).astype(BF16)
    paired = nn(shift, every).astype(BF16)
    own_rows_at = lax.broadcasted_iota(jnp.int32, (128, width), 0) + place.shard * (width // fsdp_size)
    pick = jnp.where(own_rows_at == lax.broadcasted_iota(jnp.int32, (128, width), 1), 1.0, 0.0).astype(BF16)
    own_part = nt(pick, every).astype(BF16)
    pool_out[...] = nn(own_part, paired)[0 : width // fsdp_size, :]

    in_c.to_line()
    total.to_plane()

    wide = 256
    kept = [
        (down_a, down_out, many, [(0, 0, width)]),
        (down_b, down_out, 0, [(0, 0, width)]),
        (up_a, up_out, 0, [(0, 0, 2 * width)]),
        (up_b, up_out, 0, [(0, 2 * width, 2 * width)]),
        (of_mix, mix_out, 0, [(0, 0, width)]),
    ]
    for chunk, one in enumerate((in_a, in_b, in_c)):
        kept.append((one, in_out, 0, [(part * wide, part * width + chunk * wide, wide) for part in range(3)]))

    def keep(one, out, first_row, spans):
        one.finish()
        half_rows, half_cols = one.rows // 2, one.cols // 2
        for row_half in (0, 1):
            rows = pl.ds(first_row + row_half * half_rows, half_rows)
            for col_half in (0, 1):
                begin, end = col_half * half_cols, (col_half + 1) * half_cols
                for here, there, count in spans:
                    low, high = max(here, begin), min(here + count, end)
                    if low < high:
                        source = one.done.at[row_half, col_half, :, pl.ds(low - begin, high - low)]
                        target = out.at[rows, pl.ds(there + low - here, high - low)]
                        store = pltpu.make_async_copy(source, target, local.at[len(stores) + 2])
                        store.start()
                        stores.append(store)

    for item in kept[:-1]:
        keep(*item)
    total.finish(total.from_core)
    own_sums(place.shard, fsdp_size, total.from_core, sums_out, classes)
    in_c.to_plane()
    keep(*kept[-1])
    for store in stores:
        store.wait()
    for one in scatters + [sequences, total]:
        one.end()


def run_layer(fsdp_size, lengths, labels, class_bias, tokens, cotangent, shards, vectors, class_rows):
    line = fsdp_size // 2
    seq, width = tokens.shape
    in_shard, mix_shard, up_shard, down_shard, pool_shard = shards
    hidden = up_shard.shape[1]
    vmem, dma = pltpu.VMEM, pltpu.SemaphoreType.DMA
    reduced = (down_shard, up_shard, mix_shard, in_shard)
    block = width // fsdp_size
    few = 128
    sizes = [(few, width), (down_shard.shape[0] - few, width)] + [(block, 2 * width)] * 2 + [(block, width)] * 4
    scratch = [vmem((line, 2) + s.shape, BF16) for s in shards]
    scratch += [vmem((line, 2) + s.shape, BF16) for s in (down_shard, up_shard)]
    for size in sizes:
        scratch += Scatter.scratch(line, *size)
    del scratch[-5]
    scratch += SmallSum.scratch(line, 24, width)
    scratch += [vmem((fsdp_size, 4, 16, width), BF16)]
    rows, turned = vmem((seq, width), BF16), vmem((width, seq), BF16)
    scratch += [rows, turned, rows, rows, turned, rows, turned]
    scratch += [vmem((seq, 3 * width), BF16), vmem((seq, hidden), BF16), vmem((seq, hidden), BF16)]
    scratch += [vmem((seq, width), F32)] * 3
    scratch += [vmem((seq, 128), F32)] * 3 + [vmem((width // 128, 8, seq), F32), vmem((16, width), F32)]
    span = hidden // fsdp_size
    scratch += [vmem((16, span), F32), vmem((16, width), BF16), vmem((8, 128), F32)]
    for count in (
        (sum(s.shape[0] * s.shape[1] for s in shards) // (block * width), Gather.sems(line)),
        (len(sizes), Scatter.sems(line)),
        (SequenceGather.sems(line),),
        (SmallGather.sems(line),),
        (SmallSum.sems(line),),
    ):
        scratch += [dma(count), dma(count)]
    scratch += [dma((64,))]
    out_shape = [jax.ShapeDtypeStruct((seq, width), BF16), jax.ShapeDtypeStruct((seq, width), F32)]
    out_shape += [jax.ShapeDtypeStruct(s.shape, BF16) for s in reduced]
    out_shape += [jax.ShapeDtypeStruct((width // fsdp_size, width), F32), jax.ShapeDtypeStruct((32, span), F32)]
    return pl.pallas_call(
        functools.partial(layer_kernel, fsdp_size),
        out_shape=out_shape,
        in_specs=[SCALARS, SCALARS, WHOLE] + [ANY] * 7 + [WHOLE] * 10,
        out_specs=[ANY] * 6 + [WHOLE] * 2,
        scratch_shapes=scratch,
        compiler_params=pltpu.CompilerParams(collective_id=0, has_side_effects=True, vmem_limit_bytes=VMEM_BYTES),
        name="layer",
    )(lengths, labels, class_bias, tokens, cotangent, *shards, *vectors, class_rows)


def outputs_kernel(as_is, rounded, sizes, classes, size, *refs):
    count = as_is + rounded
    inputs, sums = refs[:count], refs[count]
    refs = refs[count + 1 :]
    outs, small = refs[:count], refs[count : count + len(sizes) + 2]
    refs = refs[count + len(sizes) + 2 :]
    held, wide, (load_sems, store_sems) = refs[:count], refs[count : count + rounded], refs[count + rounded :]
    order = list(range(as_is, count)) + list(range(as_is))
    loads = {i: pltpu.make_async_copy(inputs[i], held[i], load_sems.at[i]) for i in order}
    for load in loads.values():
        load.start()
    for (row, length), out in zip(sizes.items(), small):
        out[...] = sums[row : row + 1, 0:length].reshape(length)
    small[-2][...] = sums[13 : 13 + classes, 0:size]
    small[-1][...] = sums[26:27, 0:classes].reshape(classes)
    stores = []
    for i in order:
        loads[i].wait()
        source = held[i]
        if i >= as_is:
            source = wide[i - as_is]
            step = 32

            def widen(index, narrow=held[i], source=source):
                rows = pl.ds(pl.multiple_of(index * step, step), step)
                source[rows, :] = narrow[rows, :].astype(F32)

            loop(source.shape[0] // step, widen)
        stores.append(pltpu.make_async_copy(source, outs[i], store_sems.at[i]))
        stores[-1].start()
    for store in stores:
        store.wait()


def run_outputs(as_is, rounded, sums, sizes, classes, size):
    arrays = as_is + rounded
    out_shape = [jax.ShapeDtypeStruct(a.shape, a.dtype) for a in as_is]
    out_shape += [jax.ShapeDtypeStruct(a.shape, F32) for a in rounded]
    out_shape += [jax.ShapeDtypeStruct((length,), F32) for length in sizes.values()]
    out_shape += [jax.ShapeDtypeStruct((classes, size), F32), jax.ShapeDtypeStruct((classes,), F32)]
    scratch = [pltpu.VMEM(a.shape, a.dtype) for a in arrays] + [pltpu.VMEM(a.shape, F32) for a in rounded]
    scratch += [pltpu.SemaphoreType.DMA((len(arrays),))] * 2
    return pl.pallas_call(
        functools.partial(outputs_kernel, len(as_is), len(rounded), sizes, classes, size),
        out_shape=out_shape,
        in_specs=[ANY] * len(arrays) + [WHOLE],
        out_specs=[ANY] * len(arrays) + [WHOLE] * (len(sizes) + 2),
        scratch_shapes=scratch,
        compiler_params=pltpu.CompilerParams(vmem_limit_bytes=VMEM_BYTES),
        name="outputs",
    )(*arrays, sums)


def kernel_body(
    fsdp_size,
    tokens,
    in_weight,
    in_bias,
    mix_weight,
    mix_bias,
    first_gain,
    first_shift,
    up_weight,
    up_bias,
    down_weight,
    down_bias,
    second_gain,
    second_shift,
    pool_weight,
    pool_bias,
    class_weight,
    class_bias,
    lengths,
    labels,
    cotangent,
):
    layer_out, input_grad, down_grad, up_grad, mix_grad, in_grad, pool_grad, sums = run_layer(
        fsdp_size,
        lengths,
        labels,
        class_bias,
        tokens,
        cotangent,
        (in_weight, mix_weight, up_weight, down_weight, pool_weight),
        (in_bias, mix_bias, first_gain, first_shift, up_bias, down_bias, second_gain, second_shift, pool_bias),
        class_weight.T,
    )
    size = mix_bias.shape[0]
    sizes = {24: 2 * size, 2: size, 3: size, 4: size, 25: 4 * size, 9: size, 10: size, 11: size, 12: size}
    outs = run_outputs(
        (layer_out, input_grad, pool_grad),
        (in_grad, mix_grad, up_grad, down_grad),
        sums,
        sizes,
        class_bias.shape[0],
        size,
    )
    layer_out, input_grad, pool_grad, in_grad, mix_grad, up_grad, down_grad = outs[:7]
    of_in, of_mix, of_gain_one, of_shift_one, of_up, of_down, of_gain_two, of_shift_two, of_pool = outs[7:16]
    class_grad, class_bias_grad = outs[16:]
    return (
        layer_out,
        input_grad,
        in_grad,
        of_in,
        mix_grad,
        of_mix,
        of_gain_one,
        of_shift_one,
        up_grad,
        of_up,
        down_grad,
        of_down,
        of_gain_two,
        of_shift_two,
        pool_grad,
        of_pool,
        class_grad.T,
        class_bias_grad,
    )


def plain_body(
    tokens,
    in_weight,
    in_bias,
    mix_weight,
    mix_bias,
    first_gain,
    first_shift,
    up_weight,
    up_bias,
    down_weight,
    down_bias,
    second_gain,
    second_shift,
    pool_weight,
    pool_bias,
    class_weight,
    class_bias,
    lengths,
    labels,
    cotangent,
):
    gathered = (
        lax.all_gather(in_weight, "fsdp", axis=0, tiled=True),
        lax.all_gather(in_bias, "fsdp", axis=0, tiled=True),
        lax.all_gather(mix_weight, "fsdp", axis=0, tiled=True),
        lax.all_gather(mix_bias, "fsdp", axis=0, tiled=True),
        lax.all_gather(first_gain, "fsdp", axis=0, tiled=True),
        lax.all_gather(first_shift, "fsdp", axis=0, tiled=True),
        lax.all_gather(up_weight, "fsdp", axis=0, tiled=True),
        lax.all_gather(up_bias, "fsdp", axis=0, tiled=True),
        lax.all_gather(down_weight, "fsdp", axis=0, tiled=True),
        lax.all_gather(down_bias, "fsdp", axis=0, tiled=True),
        lax.all_gather(second_gain, "fsdp", axis=0, tiled=True),
        lax.all_gather(second_shift, "fsdp", axis=0, tiled=True),
        lax.all_gather(pool_weight, "fsdp", axis=0, tiled=True),
        lax.all_gather(pool_bias, "fsdp", axis=0, tiled=True),
        lax.all_gather(class_weight, "fsdp", axis=0, tiled=True),
    )
    (
        whole_in,
        bias_in,
        whole_mix,
        bias_mix,
        gain_one,
        shift_one,
        whole_up,
        bias_up,
        whole_down,
        bias_down,
        gain_two,
        shift_two,
        whole_pool,
        bias_pool,
        whole_class,
    ) = gathered
    token_rows = tokens.shape[0]
    seq_count = lengths.shape[0]
    seq_len = token_rows // seq_count
    model_width = whole_mix.shape[0]
    score_scale = 1.0 / math.sqrt(DH)
    positions = jnp.arange(seq_len)
    projected = jnp.dot(tokens, whole_in, preferred_element_type=jnp.float32)
    in_bias_f = bias_in.astype(jnp.float32)
    head_shape = (seq_count, seq_len, H, DH)
    queries = (
        (projected[:, :model_width] + in_bias_f[:model_width])
        .astype(jnp.bfloat16)
        .reshape(head_shape)
    )
    keys_all = projected[:, model_width : 2 * model_width].astype(jnp.bfloat16).reshape(head_shape)
    values_all = (
        (projected[:, 2 * model_width :] + in_bias_f[model_width:])
        .astype(jnp.bfloat16)
        .reshape(head_shape)
    )

    def scores_of(query_blk, key_blk, length):
        raw_scores = (
            jnp.einsum("qhd,khd->hqk", query_blk, key_blk, preferred_element_type=jnp.float32)
            * score_scale
        )
        return jnp.where(positions[None, None, :] < length, raw_scores, -1e30)

    def attend_fore(block_items):
        query_blk, key_blk, value_blk, length = block_items
        scores = scores_of(query_blk, key_blk, length)
        highest = jnp.max(scores, axis=-1, keepdims=True)
        raw_weights = jnp.exp(scores - highest)
        totals = jnp.sum(raw_weights, axis=-1, keepdims=True)
        softmaxed = (raw_weights / totals).astype(jnp.bfloat16)
        mixed_values = jnp.einsum(
            "hqk,khd->qhd", softmaxed, value_blk, preferred_element_type=jnp.float32
        )
        return (mixed_values, (highest + jnp.log(totals))[..., 0])

    attended, logsum = lax.map(attend_fore, (queries, keys_all, values_all, lengths))
    attn_low = attended.reshape(token_rows, model_width).astype(jnp.bfloat16)
    branch = jnp.dot(attn_low, whole_mix, preferred_element_type=jnp.float32) + bias_mix.astype(
        jnp.float32
    )
    first_norm, unit_one, inverse_one = norm_fore(
        tokens.astype(jnp.float32) + branch,
        gain_one.astype(jnp.float32),
        shift_one.astype(jnp.float32),
    )
    first_low = first_norm.astype(jnp.bfloat16)
    pre_act = jnp.dot(first_low, whole_up, preferred_element_type=jnp.float32) + bias_up.astype(
        jnp.float32
    )
    activated, gelu_pull = jax.vjp(partial(jax.nn.gelu, approximate=False), pre_act)
    act_low = activated.astype(jnp.bfloat16)
    ffn_out = jnp.dot(act_low, whole_down, preferred_element_type=jnp.float32) + bias_down.astype(
        jnp.float32
    )
    result, unit_two, inverse_two = norm_fore(
        first_norm + ffn_out, gain_two.astype(jnp.float32), shift_two.astype(jnp.float32)
    )
    head_rows = result.reshape(seq_count, seq_len, model_width)[:, 0, :].astype(jnp.bfloat16)
    pooled = jnp.tanh(
        jnp.dot(head_rows, whole_pool, preferred_element_type=jnp.float32)
        + bias_pool.astype(jnp.float32)
    )
    pooled_low = pooled.astype(jnp.bfloat16)
    logits = jnp.dot(
        pooled_low, whole_class, preferred_element_type=jnp.float32
    ) + class_bias.astype(jnp.float32)
    back_in, back_mix, back_gain_one, back_up, back_down, back_gain_two, back_pool, back_class = (
        lax.all_gather(in_weight, "fsdp", axis=0, tiled=True),
        lax.all_gather(mix_weight, "fsdp", axis=0, tiled=True),
        lax.all_gather(first_gain, "fsdp", axis=0, tiled=True),
        lax.all_gather(up_weight, "fsdp", axis=0, tiled=True),
        lax.all_gather(down_weight, "fsdp", axis=0, tiled=True),
        lax.all_gather(second_gain, "fsdp", axis=0, tiled=True),
        lax.all_gather(pool_weight, "fsdp", axis=0, tiled=True),
        lax.all_gather(class_weight, "fsdp", axis=0, tiled=True),
    )
    onehot = (labels[:, None] == jnp.arange(logits.shape[1])[None, :]).astype(jnp.float32)
    grad_logits = (jax.nn.softmax(logits, axis=-1) - onehot).astype(jnp.bfloat16)
    grad_class_weight = jnp.dot(pooled_low.T, grad_logits, preferred_element_type=jnp.float32)
    grad_class_bias = column_sums(grad_logits)
    grad_pool_pre = (
        jnp.dot(grad_logits, back_class.T, preferred_element_type=jnp.float32)
        * (1.0 - pooled * pooled)
    ).astype(jnp.bfloat16)
    grad_pool_weight = jnp.dot(head_rows.T, grad_pool_pre, preferred_element_type=jnp.float32)
    grad_pool_bias = column_sums(grad_pool_pre)
    grad_head_rows = jnp.dot(grad_pool_pre, back_pool.T, preferred_element_type=jnp.float32)
    live_mask = (positions[None, :] < lengths[:, None]).astype(jnp.float32)
    grad_result = (
        cotangent.astype(jnp.float32).reshape(seq_count, seq_len, model_width)
        * live_mask[:, :, None]
    )
    grad_result = grad_result.at[:, 0, :].add(grad_head_rows).reshape(token_rows, model_width)
    grad_sum_two, grad_second_gain, grad_second_shift = norm_back(
        grad_result, unit_two, inverse_two, back_gain_two.astype(jnp.float32)
    )
    grad_ffn = grad_sum_two.astype(jnp.bfloat16)
    grad_down_weight = jnp.dot(act_low.T, grad_ffn, preferred_element_type=jnp.float32)
    grad_down_bias = column_sums(grad_ffn)
    grad_pre = gelu_pull(jnp.dot(grad_ffn, back_down.T, preferred_element_type=jnp.float32))[
        0
    ].astype(jnp.bfloat16)
    grad_up_weight = jnp.dot(first_low.T, grad_pre, preferred_element_type=jnp.float32)
    grad_up_bias = column_sums(grad_pre)
    grad_first_norm = grad_sum_two + jnp.dot(
        grad_pre, back_up.T, preferred_element_type=jnp.float32
    )
    grad_sum_one, grad_first_gain, grad_first_shift = norm_back(
        grad_first_norm, unit_one, inverse_one, back_gain_one.astype(jnp.float32)
    )
    grad_branch = grad_sum_one.astype(jnp.bfloat16)
    grad_mix_weight = jnp.dot(attn_low.T, grad_branch, preferred_element_type=jnp.float32)
    grad_mix_bias = column_sums(grad_branch)
    grad_attended = (
        jnp.dot(grad_branch, back_mix.T, preferred_element_type=jnp.float32)
        .astype(jnp.bfloat16)
        .reshape(head_shape)
    )

    def attend_back(block_items):
        query_blk, key_blk, value_blk, length, lse_blk, grad_blk = block_items
        softmaxed = jnp.exp(scores_of(query_blk, key_blk, length) - lse_blk[..., None])
        grad_value = jnp.einsum(
            "hqk,qhd->khd",
            softmaxed.astype(jnp.bfloat16),
            grad_blk,
            preferred_element_type=jnp.float32,
        )
        grad_soft = jnp.einsum(
            "qhd,khd->hqk", grad_blk, value_blk, preferred_element_type=jnp.float32
        )
        grad_scores = (
            softmaxed * (grad_soft - jnp.sum(softmaxed * grad_soft, axis=-1, keepdims=True))
        ).astype(jnp.bfloat16)
        grad_query = (
            jnp.einsum("hqk,khd->qhd", grad_scores, key_blk, preferred_element_type=jnp.float32)
            * score_scale
        )
        grad_key = (
            jnp.einsum("hqk,qhd->khd", grad_scores, query_blk, preferred_element_type=jnp.float32)
            * score_scale
        )
        return (grad_query, grad_key, grad_value)

    grad_queries, grad_keys, grad_values = lax.map(
        attend_back, (queries, keys_all, values_all, lengths, logsum, grad_attended)
    )
    grad_proj = jnp.concatenate(
        [
            grad_queries.reshape(token_rows, model_width),
            grad_keys.reshape(token_rows, model_width),
            grad_values.reshape(token_rows, model_width),
        ],
        axis=1,
    ).astype(jnp.bfloat16)
    grad_in_weight = jnp.dot(tokens.T, grad_proj, preferred_element_type=jnp.float32)
    proj_sums = column_sums(grad_proj)
    grad_in_bias = jnp.concatenate([proj_sums[:model_width], proj_sums[2 * model_width :]])
    input_grad = grad_sum_one + jnp.dot(grad_proj, back_in.T, preferred_element_type=jnp.float32)
    gradients = (
        grad_in_weight,
        grad_in_bias,
        grad_mix_weight,
        grad_mix_bias,
        grad_first_gain,
        grad_first_shift,
        grad_up_weight,
        grad_up_bias,
        grad_down_weight,
        grad_down_bias,
        grad_second_gain,
        grad_second_shift,
        grad_pool_weight,
        grad_pool_bias,
        grad_class_weight,
    )
    shard_sums = (
        lax.psum_scatter(gradients[0], "fsdp", scatter_dimension=0, tiled=True),
        lax.psum_scatter(gradients[1], "fsdp", scatter_dimension=0, tiled=True),
        lax.psum_scatter(gradients[2], "fsdp", scatter_dimension=0, tiled=True),
        lax.psum_scatter(gradients[3], "fsdp", scatter_dimension=0, tiled=True),
        lax.psum_scatter(gradients[4], "fsdp", scatter_dimension=0, tiled=True),
        lax.psum_scatter(gradients[5], "fsdp", scatter_dimension=0, tiled=True),
        lax.psum_scatter(gradients[6], "fsdp", scatter_dimension=0, tiled=True),
        lax.psum_scatter(gradients[7], "fsdp", scatter_dimension=0, tiled=True),
        lax.psum_scatter(gradients[8], "fsdp", scatter_dimension=0, tiled=True),
        lax.psum_scatter(gradients[9], "fsdp", scatter_dimension=0, tiled=True),
        lax.psum_scatter(gradients[10], "fsdp", scatter_dimension=0, tiled=True),
        lax.psum_scatter(gradients[11], "fsdp", scatter_dimension=0, tiled=True),
        lax.psum_scatter(gradients[12], "fsdp", scatter_dimension=0, tiled=True),
        lax.psum_scatter(gradients[13], "fsdp", scatter_dimension=0, tiled=True),
        lax.psum_scatter(gradients[14], "fsdp", scatter_dimension=0, tiled=True),
    )
    summed = (
        lax.psum(shard_sums[0].astype(jnp.bfloat16), "dp").astype(jnp.float32),
        lax.psum(shard_sums[1].astype(jnp.bfloat16), "dp").astype(jnp.float32),
        lax.psum(shard_sums[2].astype(jnp.bfloat16), "dp").astype(jnp.float32),
        lax.psum(shard_sums[3].astype(jnp.bfloat16), "dp").astype(jnp.float32),
        lax.psum(shard_sums[4].astype(jnp.bfloat16), "dp").astype(jnp.float32),
        lax.psum(shard_sums[5].astype(jnp.bfloat16), "dp").astype(jnp.float32),
        lax.psum(shard_sums[6].astype(jnp.bfloat16), "dp").astype(jnp.float32),
        lax.psum(shard_sums[7].astype(jnp.bfloat16), "dp").astype(jnp.float32),
        lax.psum(shard_sums[8].astype(jnp.bfloat16), "dp").astype(jnp.float32),
        lax.psum(shard_sums[9].astype(jnp.bfloat16), "dp").astype(jnp.float32),
        lax.psum(shard_sums[10].astype(jnp.bfloat16), "dp").astype(jnp.float32),
        lax.psum(shard_sums[11].astype(jnp.bfloat16), "dp").astype(jnp.float32),
        lax.psum(shard_sums[12].astype(jnp.bfloat16), "dp").astype(jnp.float32),
        lax.psum(shard_sums[13].astype(jnp.bfloat16), "dp").astype(jnp.float32),
        lax.psum(shard_sums[14].astype(jnp.bfloat16), "dp").astype(jnp.float32),
    )
    bias_total = lax.psum(grad_class_bias, ("dp", "fsdp"))
    return (
        result.astype(jnp.bfloat16),
        input_grad,
        summed[0],
        summed[1],
        summed[2],
        summed[3],
        summed[4],
        summed[5],
        summed[6],
        summed[7],
        summed[8],
        summed[9],
        summed[10],
        summed[11],
        summed[12],
        summed[13],
        summed[14],
        bias_total,
    )


def solution(mesh):
    in_specs = (
        P(("dp", "fsdp"), None),
        P("fsdp", None),
        P("fsdp"),
        P("fsdp", None),
        P("fsdp"),
        P("fsdp"),
        P("fsdp"),
        P("fsdp", None),
        P("fsdp"),
        P("fsdp", None),
        P("fsdp"),
        P("fsdp"),
        P("fsdp"),
        P("fsdp", None),
        P("fsdp"),
        P("fsdp", None),
        P(),
        P(("dp", "fsdp")),
        P(("dp", "fsdp")),
        P(("dp", "fsdp"), None),
    )
    out_specs = (
        P(("dp", "fsdp"), None),
        P(("dp", "fsdp"), None),
        P("fsdp", None),
        P("fsdp"),
        P("fsdp", None),
        P("fsdp"),
        P("fsdp"),
        P("fsdp"),
        P("fsdp", None),
        P("fsdp"),
        P("fsdp", None),
        P("fsdp"),
        P("fsdp"),
        P("fsdp"),
        P("fsdp", None),
        P("fsdp"),
        P("fsdp", None),
        P(),
    )
    dp_size, fsdp_size = mesh.shape["dp"], mesh.shape["fsdp"]
    body = partial(kernel_body, fsdp_size) if (dp_size, fsdp_size) == (4, 8) else plain_body
    return jax.shard_map(body, mesh=mesh, in_specs=in_specs, out_specs=out_specs, check_vma=False)
```

```python
import functools
from functools import partial
import math

import jax
import jax.numpy as jnp
from jax import lax
from jax.experimental import pallas as pl
from jax.experimental.pallas import tpu as pltpu
from jax.sharding import PartitionSpec as P

H = 12
DH = 64


EPSILON = 1e-06


def norm_fore(vector, norm_gain, norm_shift):
    average = jnp.mean(vector, axis=-1, keepdims=True)
    centered = vector - average
    inverse = lax.rsqrt(jnp.mean(centered * centered, axis=-1, keepdims=True) + EPSILON)
    normed = centered * inverse
    return (normed * norm_gain + norm_shift, normed, inverse)


def norm_back(gradient, normed, inverse, norm_gain):
    scaled = gradient * norm_gain
    inner_mean = jnp.mean(scaled, axis=-1, keepdims=True)
    cross_mean = jnp.mean(scaled * normed, axis=-1, keepdims=True)
    input_part = inverse * (scaled - inner_mean - normed * cross_mean)
    return (input_part, jnp.sum(gradient * normed, axis=0), jnp.sum(gradient, axis=0))


def column_sums(matrix):
    return jnp.sum(matrix.astype(jnp.float32), axis=0)


MESH = pl.DeviceIdType.MESH


def remote(src, dst, send_sem, recv_sem, target):
    return pltpu.make_async_remote_copy(
        src_ref=src, dst_ref=dst, send_sem=send_sem, recv_sem=recv_sem, device_id=target, device_id_type=MESH
    )


class Place:
    def __init__(self, fsdp_size):
        self.dp = lax.axis_index("dp")
        self.shard = lax.axis_index("fsdp")
        self.line = fsdp_size // 2
        self.row_half, self.col_half = self.dp // 2, lax.rem(self.dp, 2)
        self.spot, self.core = self.shard // 2, lax.rem(self.shard, 2)
        across = 2 * self.row_half + (1 - self.col_half)
        along = 2 * (1 - self.row_half) + self.col_half
        self.first = jnp.where(self.core == 0, across, along)
        self.second = jnp.where(self.core == 0, along, across)

    def partner(self):
        return {"dp": self.dp, "fsdp": 2 * self.spot + 1 - self.core}

    def on_line(self, hop):
        return {"dp": self.dp, "fsdp": 2 * lax.rem(self.spot + hop, self.line) + self.core}

    def in_plane(self, dp):
        return {"dp": dp, "fsdp": self.shard}

    def source_spot(self, hop):
        return lax.rem(self.spot + self.line - hop, self.line)

    def peers(self):
        return (
            [self.partner()]
            + [self.on_line(hop) for hop in range(1, self.line)]
            + [self.in_plane(lax.rem(self.dp + step, 4)) for step in range(1, 4)]
        )

    def meet(self):
        barrier = pltpu.get_barrier_semaphore()
        peers = self.peers()
        for peer in peers:
            pl.semaphore_signal(barrier, inc=1, device_id=peer, device_id_type=MESH)
        pl.semaphore_wait(barrier, len(peers))


class Gather:
    def __init__(self, place, shard_ref, whole_ref, send_sems, recv_sems):
        self.place, self.shard_ref, self.whole = place, shard_ref, whole_ref
        self.send_sems, self.recv_sems = send_sems, recv_sems
        self.rows, self.cols = shard_ref.shape
        self.hops = place.line - 1
        self.started = []

    @staticmethod
    def sems(line):
        return 5 * (line - 1) + 2

    def block(self, shard):
        return self.whole.at[shard // 2, lax.rem(shard, 2)]

    def quarter(self, shard, row_half, col_half):
        half_rows, half_cols = self.rows // 2, self.cols // 2
        return self.whole.at[
            shard // 2,
            lax.rem(shard, 2),
            pl.ds(pl.multiple_of(row_half * half_rows, 16), half_rows),
            pl.ds(pl.multiple_of(col_half * half_cols, 128), half_cols),
        ]

    def go(self, index, src, dst, target):
        remote(src, dst, self.send_sems.at[index], self.recv_sems.at[index], target).start()
        self.started.append((index, dst.shape[-2:]))

    def arrived(self, index, dst):
        remote(dst, dst, self.send_sems.at[index], self.recv_sems.at[index], self.place.partner()).wait_recv()

    def begin(self):
        p = self.place
        half_rows, half_cols = self.rows // 2, self.cols // 2
        piece = self.shard_ref.at[
            pl.ds(pl.multiple_of(p.row_half * half_rows, 16), half_rows),
            pl.ds(pl.multiple_of(p.col_half * half_cols, 128), half_cols),
        ]
        for hop in range(1, p.line):
            self.go(hop - 1, piece, self.quarter(p.shard, p.row_half, p.col_half), p.on_line(hop))
        self.go(4 * self.hops, self.shard_ref, self.block(p.shard), p.partner())
        self.own().start()

    def own(self):
        return pltpu.make_async_copy(
            self.shard_ref, self.block(self.place.shard), self.recv_sems.at[5 * self.hops + 1]
        )

    def source(self, hop):
        return 2 * self.place.source_spot(hop) + self.place.core

    def spread(self, hop):
        p = self.place
        quarter = self.quarter(self.source(hop), p.row_half, p.col_half)
        self.arrived(hop - 1, quarter)
        self.go(self.hops + hop - 1, quarter, quarter, p.in_plane(p.first))
        self.go(2 * self.hops + hop - 1, quarter, quarter, p.in_plane(p.second))

    def relay(self, hop):
        p = self.place
        quarter = self.quarter(self.source(hop), p.first // 2, lax.rem(p.first, 2))
        self.arrived(self.hops + hop - 1, quarter)
        self.go(3 * self.hops + hop - 1, quarter, quarter, p.in_plane(p.second))

    def hand(self, hop):
        p = self.place
        self.arrived(2 * self.hops + hop - 1, self.quarter(self.source(hop), p.second // 2, lax.rem(p.second, 2)))
        self.arrived(3 * self.hops + hop - 1, self.quarter(self.source(hop), 1 - p.row_half, 1 - p.col_half))
        block = self.block(self.source(hop))
        self.go(4 * self.hops + hop, block, block, p.partner())

    def ready(self):
        p = self.place
        self.own().wait()
        self.arrived(4 * self.hops, self.block(p.shard + 1 - 2 * p.core))
        for hop in range(1, p.line):
            self.arrived(4 * self.hops + hop, self.block(2 * p.source_spot(hop) + 1 - p.core))

    def end(self):
        for index, (rows, cols) in self.started:
            like = self.whole.at[0, 0, pl.ds(0, rows), pl.ds(0, cols)]
            remote(like, like, self.send_sems.at[index], self.recv_sems.at[index], self.place.partner()).wait_send()


class SmallGather:
    def __init__(self, place, own_ref, all_ref, send_sems, recv_sems):
        self.place, self.own_ref, self.all = place, own_ref, all_ref
        self.send_sems, self.recv_sems = send_sems, recv_sems
        self.hops = place.line - 1
        self.started = []

    def at(self, shard):
        rows, cols = self.own_ref.shape
        return self.all.at[pl.ds(pl.multiple_of(shard * rows, rows), rows), pl.ds(0, cols)]

    @staticmethod
    def sems(line):
        return 2 * (line - 1) + 2

    def go(self, index, src, dst, target):
        copy = remote(src, dst, self.send_sems.at[index], self.recv_sems.at[index], target)
        copy.start()
        self.started.append(copy)

    def arrived(self, index, dst):
        remote(dst, dst, self.send_sems.at[index], self.recv_sems.at[index], self.place.partner()).wait_recv()

    def begin(self):
        p = self.place
        for hop in range(1, p.line):
            self.go(hop - 1, self.own_ref, self.at(p.shard), p.on_line(hop))
        self.go(2 * self.hops, self.own_ref, self.at(p.shard), p.partner())
        self.own = pltpu.make_async_copy(self.own_ref, self.at(p.shard), self.recv_sems.at[2 * self.hops + 1])
        self.own.start()

    def hand(self):
        p = self.place
        for hop in range(1, p.line):
            block = self.at(2 * p.source_spot(hop) + p.core)
            self.arrived(hop - 1, block)
            self.go(self.hops + hop - 1, block, block, p.partner())

    def ready(self):
        p = self.place
        self.own.wait()
        self.arrived(2 * self.hops, self.at(p.shard + 1 - 2 * p.core))
        for hop in range(1, p.line):
            self.arrived(self.hops + hop - 1, self.at(2 * p.source_spot(hop) + 1 - p.core))

    def end(self):
        for copy in self.started:
            copy.wait_send()


class Scatter:
    def __init__(self, place, grad, from_core, from_first, from_second, from_line, done, send_sems, recv_sems):
        self.place, self.grad = place, grad
        self.from_core, self.from_first, self.from_second = from_core, from_first, from_second
        self.from_line, self.done = from_line, done
        self.send_sems, self.recv_sems = send_sems, recv_sems
        self.line, _, self.rows, self.cols = grad.shape

    @staticmethod
    def sems(line):
        return 1 + 2 + 1 + (line - 1) + 3

    @staticmethod
    def scratch(line, rows, cols):
        half = (rows // 2, cols // 2)
        return [
            pltpu.VMEM((line, rows, cols), jnp.bfloat16),
            pltpu.VMEM((2, line) + half, jnp.bfloat16),
            pltpu.VMEM((line,) + half, jnp.bfloat16),
            pltpu.VMEM((line - 1,) + half, jnp.bfloat16),
            pltpu.VMEM((2, 2) + half, jnp.bfloat16),
        ]

    def go(self, index, src, dst, target):
        remote(src, dst, self.send_sems.at[index], self.recv_sems.at[index], target).start()

    def arrived(self, index, dst):
        remote(dst, dst, self.send_sems.at[index], self.recv_sems.at[index], self.place.partner()).wait_recv()

    def slices(self, row_half, col_half):
        half_rows, half_cols = self.rows // 2, self.cols // 2
        return (
            pl.ds(pl.multiple_of(row_half * half_rows, 16), half_rows),
            pl.ds(pl.multiple_of(col_half * half_cols, 128), half_cols),
        )

    def halves(self, side, which):
        p = self.place
        row_half = which * (1 - p.core) + side * p.core
        col_half = side * (1 - p.core) + which * p.core
        return self.slices(row_half, col_half)

    def swap(self):
        p = self.place
        self.go(0, self.grad.at[:, 1 - p.core], self.from_core, p.partner())

    def add(self, rows, cols, others, targets_spot=None):
        p = self.place
        half_rows, half_cols = self.rows // 2, self.cols // 2
        step = next(size for size in (64, 48, 32, 16) if half_rows % size == 0)
        steps = half_rows // step

        def one(index, carry):
            spot, part = index // steps, lax.rem(index, steps)
            at = pl.ds(pl.multiple_of(rows.start + part * step, 16), step)
            inner = pl.ds(pl.multiple_of(part * step, 16), step)
            total = self.grad[spot, p.core, at, cols].astype(jnp.float32) + self.from_core[spot, at, cols].astype(
                jnp.float32
            )
            for other in others:
                total = total + other[spot, inner, :].astype(jnp.float32)
            self.grad[spot, p.core, at, cols] = total.astype(jnp.bfloat16)
            return carry

        lax.fori_loop(0, self.line * steps, one, 0)

    def to_first(self):
        p = self.place
        self.arrived(0, self.from_core)
        keep = jnp.where(p.core == 0, p.col_half, p.row_half)
        for which in (0, 1):
            rows, cols = self.halves(1 - keep, which)
            self.add(rows, cols, [])
            self.go(1 + which, self.grad.at[:, p.core, rows, cols], self.from_first.at[which], p.in_plane(p.first))

    def to_second(self):
        p = self.place
        for which in (0, 1):
            self.arrived(1 + which, self.from_first.at[which])
        keep = jnp.where(p.core == 0, p.col_half, p.row_half)
        mine = jnp.where(p.core == 0, p.row_half, p.col_half)
        rows, cols = self.halves(keep, 1 - mine)
        self.add(rows, cols, [self.from_first.at[1 - mine]])
        self.go(3, self.grad.at[:, p.core, rows, cols], self.from_second, p.in_plane(p.second))

    def to_line(self):
        p = self.place
        self.arrived(3, self.from_second)
        mine = jnp.where(p.core == 0, p.row_half, p.col_half)
        rows, cols = self.slices(p.row_half, p.col_half)
        self.add(rows, cols, [self.from_first.at[mine], self.from_second])
        for hop in range(1, self.line):
            spot = lax.rem(p.spot + hop, self.line)
            self.go(3 + hop, self.grad.at[spot, p.core, rows, cols], self.from_line.at[hop - 1], p.on_line(hop))

    def to_plane(self):
        p = self.place
        for hop in range(1, self.line):
            self.arrived(3 + hop, self.from_line.at[hop - 1])
        half_rows = self.rows // 2
        rows, cols = self.slices(p.row_half, p.col_half)
        step = 16

        def one(part, carry):
            at = pl.ds(pl.multiple_of(rows.start + part * step, 16), step)
            inner = pl.ds(pl.multiple_of(part * step, 16), step)
            total = self.grad[p.spot, p.core, at, cols].astype(jnp.float32)
            for hop in range(1, self.line):
                total = total + self.from_line[hop - 1, inner, :].astype(jnp.float32)
            self.done[p.row_half, p.col_half, inner, :] = total.astype(jnp.bfloat16)
            return carry

        lax.fori_loop(0, half_rows // step, one, 0)
        own = self.done.at[p.row_half, p.col_half]
        for step in range(1, 4):
            self.go(2 + self.line + step, own, own, p.in_plane(lax.rem(p.dp + step, 4)))

    def finish(self):
        p = self.place
        for step in range(1, 4):
            other = lax.rem(p.dp + 4 - step, 4)
            self.arrived(2 + self.line + step, self.done.at[other // 2, lax.rem(other, 2)])

    def end(self):
        third = 2 + self.line
        landed = {0: self.from_core, 1: self.from_first.at[0], 2: self.from_first.at[0], 3: self.from_second}
        for hop in range(1, self.line):
            landed[3 + hop] = self.from_line.at[0]
        for step in range(1, 4):
            landed[third + step] = self.done.at[0, 0]
        for index, like in landed.items():
            remote(like, like, self.send_sems.at[index], self.recv_sems.at[index], self.place.partner()).wait_send()


class LineFirst(Scatter):
    def __init__(self, place, grad, from_core, from_line, from_plane, done, send_sems, recv_sems):
        self.place, self.grad = place, grad
        self.from_core, self.from_line, self.from_plane, self.done = from_core, from_line, from_plane, done
        self.send_sems, self.recv_sems = send_sems, recv_sems
        self.line, _, self.rows, self.cols = grad.shape

    @staticmethod
    def scratch(line, rows, cols):
        half = (rows // 2, cols // 2)
        return [
            pltpu.VMEM((line, rows, cols), jnp.bfloat16),
            pltpu.VMEM((line - 1, rows, cols), jnp.bfloat16),
            pltpu.VMEM((3,) + half, jnp.bfloat16),
            pltpu.VMEM((2, 2) + half, jnp.bfloat16),
        ]

    def quarter(self, dp):
        rows, cols = self.slices(dp // 2, lax.rem(dp, 2))
        return self.grad.at[self.place.spot, self.place.core, rows, cols]

    def to_first(self):
        p = self.place
        self.arrived(0, self.from_core)
        step = 32
        steps = self.rows // step

        def one(index, carry):
            spot, at = index // steps, pl.ds(pl.multiple_of(lax.rem(index, steps) * step, step), step)
            total = self.grad[spot, p.core, at, :].astype(jnp.float32) + self.from_core[spot, at, :].astype(jnp.float32)
            self.grad[spot, p.core, at, :] = total.astype(jnp.bfloat16)
            return carry

        lax.fori_loop(0, self.line * steps, one, 0)
        for hop in range(1, self.line):
            spot = lax.rem(p.spot + hop, self.line)
            self.go(hop, self.grad.at[spot, p.core], self.from_line.at[hop - 1], p.on_line(hop))

    def to_second(self):
        p = self.place
        for hop in range(1, self.line):
            self.arrived(hop, self.from_line.at[hop - 1])
        step = 32

        def one(part, carry):
            at = pl.ds(pl.multiple_of(part * step, step), step)
            total = self.grad[p.spot, p.core, at, :].astype(jnp.float32)
            for hop in range(1, self.line):
                total = total + self.from_line[hop - 1, at, :].astype(jnp.float32)
            self.grad[p.spot, p.core, at, :] = total.astype(jnp.bfloat16)
            return carry

        lax.fori_loop(0, self.rows // step, one, 0)
        for step in range(1, 4):
            other = lax.rem(p.dp + step, 4)
            self.go(self.line - 1 + step, self.quarter(other), self.from_plane.at[step - 1], p.in_plane(other))

    def to_line(self):
        p = self.place
        for step in range(1, 4):
            self.arrived(self.line - 1 + step, self.from_plane.at[step - 1])
        rows, cols = self.slices(p.row_half, p.col_half)
        size = 16

        def one(part, carry):
            at = pl.ds(pl.multiple_of(rows.start + part * size, 16), size)
            inner = pl.ds(pl.multiple_of(part * size, 16), size)
            total = self.grad[p.spot, p.core, at, cols].astype(jnp.float32)
            for step in range(3):
                total = total + self.from_plane[step, inner, :].astype(jnp.float32)
            self.done[p.row_half, p.col_half, inner, :] = total.astype(jnp.bfloat16)
            return carry

        lax.fori_loop(0, self.rows // 2 // size, one, 0)
        own = self.done.at[p.row_half, p.col_half]
        for step in range(1, 4):
            self.go(2 + self.line + step, own, own, p.in_plane(lax.rem(p.dp + step, 4)))

    def end(self):
        landed = {0: self.from_core}
        for hop in range(1, self.line):
            landed[hop] = self.from_line.at[0]
        for step in range(1, 4):
            landed[self.line - 1 + step] = self.from_plane.at[0]
            landed[2 + self.line + step] = self.done.at[0, 0]
        for index, like in landed.items():
            remote(like, like, self.send_sems.at[index], self.recv_sems.at[index], self.place.partner()).wait_send()


class SmallSum:
    def __init__(self, place, own, from_core, on_line, in_plane, send_sems, recv_sems):
        self.place, self.own, self.from_core, self.on_line, self.in_plane = place, own, from_core, on_line, in_plane
        self.send_sems, self.recv_sems = send_sems, recv_sems
        self.started = []

    @staticmethod
    def sems(line):
        return 1 + (line - 1) + 3

    @staticmethod
    def scratch(line, rows, cols):
        return [
            pltpu.VMEM((rows, cols), jnp.float32),
            pltpu.VMEM((rows, cols), jnp.float32),
            pltpu.VMEM((line, rows, cols), jnp.float32),
            pltpu.VMEM((4, rows, cols), jnp.float32),
        ]

    def go(self, index, src, dst, target):
        copy = remote(src, dst, self.send_sems.at[index], self.recv_sems.at[index], target)
        copy.start()
        self.started.append(copy)

    def arrived(self, index, dst):
        remote(dst, dst, self.send_sems.at[index], self.recv_sems.at[index], self.place.partner()).wait_recv()

    def swap(self):
        self.go(0, self.own, self.from_core, self.place.partner())

    def to_line(self):
        p = self.place
        self.arrived(0, self.from_core)
        self.on_line[p.spot] = self.own[...] + self.from_core[...]
        slot = self.on_line.at[p.spot]
        for hop in range(1, p.line):
            self.go(hop, slot, slot, p.on_line(hop))

    def to_plane(self):
        p = self.place
        for hop in range(1, p.line):
            self.arrived(hop, self.on_line.at[p.source_spot(hop)])
        total = self.on_line[0]
        for spot in range(1, p.line):
            total = total + self.on_line[spot]
        self.in_plane[p.dp] = total
        slot = self.in_plane.at[p.dp]
        for step in range(1, 4):
            self.go(p.line - 1 + step, slot, slot, p.in_plane(lax.rem(p.dp + step, 4)))

    def finish(self, out_ref):
        p = self.place
        for step in range(1, 4):
            self.arrived(p.line - 1 + step, self.in_plane.at[lax.rem(p.dp + 4 - step, 4)])
        out_ref[...] = (self.in_plane[0] + self.in_plane[1]) + (self.in_plane[2] + self.in_plane[3])

    def end(self):
        for copy in self.started:
            copy.wait_send()


class SequenceGather:
    def __init__(self, place, blocks, send_sems, recv_sems):
        self.place, self.blocks = place, blocks
        self.send_sems, self.recv_sems = send_sems, recv_sems
        self.started = []

    @staticmethod
    def sems(line):
        return 3 + (line - 1) + line

    def go(self, index, ref, target):
        remote(ref, ref, self.send_sems.at[index], self.recv_sems.at[index], target).start()
        self.started.append((index, len(ref.shape)))

    def arrived(self, index, dst):
        remote(dst, dst, self.send_sems.at[index], self.recv_sems.at[index], self.place.partner()).wait_recv()

    def begin(self):
        p = self.place
        for step in range(1, 4):
            self.go(step - 1, self.blocks.at[p.shard, p.dp], p.in_plane(lax.rem(p.dp + step, 4)))

    def to_line(self):
        p = self.place
        for step in range(1, 4):
            self.arrived(step - 1, self.blocks.at[p.shard, lax.rem(p.dp + 4 - step, 4)])
        own = self.blocks.at[p.shard]
        for hop in range(1, p.line):
            self.go(2 + hop, own, p.on_line(hop))
        self.go(2 + p.line, own, p.partner())

    def hand(self):
        p = self.place
        for hop in range(1, p.line):
            block = self.blocks.at[2 * p.source_spot(hop) + p.core]
            self.arrived(2 + hop, block)
            self.go(2 + p.line + hop, block, p.partner())

    def ready(self):
        p = self.place
        self.arrived(2 + p.line, self.blocks.at[p.shard + 1 - 2 * p.core])
        for hop in range(1, p.line):
            self.arrived(2 + p.line + hop, self.blocks.at[2 * p.source_spot(hop) + 1 - p.core])

    def end(self):
        for index, rank in self.started:
            like = self.blocks.at[0] if rank == 3 else self.blocks.at[0, 0]
            remote(like, like, self.send_sems.at[index], self.recv_sems.at[index], self.place.partner()).wait_send()
ANY = pl.BlockSpec(memory_space=pl.ANY)
WHOLE = pl.BlockSpec(memory_space=pltpu.VMEM)
SCALARS = pl.BlockSpec(memory_space=pltpu.SMEM)
VMEM_BYTES = 67_043_328
AHEAD = 4
BF16, F32 = jnp.bfloat16, jnp.float32


def nn(left, right):
    return lax.dot_general(left, right, (((1,), (0,)), ((), ())), preferred_element_type=F32)


def nt(left, right):
    return lax.dot_general(left, right, (((1,), (1,)), ((), ())), preferred_element_type=F32)


def tn(left, right):
    return lax.dot_general(left, right, (((0,), (0,)), ((), ())), preferred_element_type=F32)


def lanes(start, size):
    return pl.ds(pl.multiple_of(start, 128), size)


def loop(count, step):
    def one(index, carry):
        step(index)
        return carry

    lax.fori_loop(0, count, one, 0)


def gelu_parts(v):
    spread = 0.5 * (1.0 + lax.erf(v * (1.0 / math.sqrt(2.0))))
    bell = jnp.exp(-0.5 * v * v) * (1.0 / math.sqrt(2.0 * math.pi))
    return v * spread, spread + v * bell


def place_vectors(shard, vectors, class_rows, short, out):
    in_bias, mix_bias, gain_one, shift_one, up_bias, down_bias, gain_two, shift_two, pool_bias = vectors
    short[...] = jnp.zeros(short.shape, F32)
    rows = [in_bias, in_bias, mix_bias, gain_one, shift_one, up_bias, up_bias, up_bias, up_bias]
    rows += [down_bias, gain_two, shift_two, pool_bias]
    for row, vector in enumerate(rows):
        size = vector.shape[0]
        short[row : row + 1, 0:size] = vector[...].astype(F32).reshape(1, size)
    size = class_rows.shape[1]
    short[13 : 13 + class_rows.shape[0], 0:size] = class_rows[...].astype(F32)
    values = short[...].astype(BF16)
    span, width = short.shape[1], out.shape[1]
    lane = lax.broadcasted_iota(jnp.int32, (span, width), 0)
    column = lax.broadcasted_iota(jnp.int32, (span, width), 1)
    row_at = lax.broadcasted_iota(jnp.int32, (16, 1), 0)

    def placed(size):
        per_row = width // size
        spread = jnp.where((column - lax.rem(shard, per_row) * size == lane) & (lane < size), 1.0, 0.0)
        return nn(values, spread.astype(BF16)), shard // per_row

    one_row, _ = placed(mix_bias.shape[0])
    of_in, in_row = placed(in_bias.shape[0])
    of_up, up_row = placed(up_bias.shape[0])
    is_in, is_up = row_at < 2, (row_at >= 5) & (row_at < 9)
    result = jnp.where(is_in, jnp.where(row_at == in_row, of_in, 0.0), one_row)
    result = jnp.where(is_up, jnp.where(row_at == 5 + up_row, of_up, 0.0), result)
    out[...] = result.astype(BF16)


def own_sums(shard, parts, total_ref, out, classes):
    total = total_ref[...]
    width = total.shape[1]
    size = width // parts
    own, own_in, own_up = (jnp.zeros(shape, F32) for shape in ((24, size), (1, 2 * size), (1, 4 * size)))
    for place in range(parts):
        here = shard == place
        own = jnp.where(here, total[:, place * size : (place + 1) * size], own)
        row, at = divmod(2 * size * place, width)
        own_in = jnp.where(here, total[row : row + 1, at : at + 2 * size], own_in)
        row, at = divmod(4 * size * place, width)
        own_up = jnp.where(here, total[5 + row : 6 + row, at : at + 4 * size], own_up)
    out[...] = jnp.zeros(out.shape, F32)
    out[0:24, 0:size] = own
    out[24:25, 0 : 2 * size] = own_in
    out[25:26, 0 : 4 * size] = own_up
    out[26:27, 0:classes] = total[16:17, 13 : 13 + classes]


def layer_kernel(fsdp_size, *refs):
    refs = list(refs)

    def take(count):
        out = refs[:count]
        del refs[:count]
        return out

    lengths, labels, class_bias, tokens_in, cot_in = take(5)
    shards = take(5)
    vectors, class_rows = take(9), take(1)[0]
    layer_out, input_grad, down_out, up_out, mix_out, in_out, pool_out, sums_out = take(8)
    w_in, w_mix, w_up, w_down, w_pool = take(5)
    g_down, g_up = take(2)
    recv = [take(4)] + [take(5) for _ in range(6)]
    recv.append([recv[1][0].at[:, pl.ds(0, shards[0].shape[0]), :]] + take(4))
    sum_refs = take(4)
    (blocks,) = take(1)
    tok, tok_t, cot, att, att_t, first, first_t = take(7)
    qkv, act, slope = take(3)
    unit_one, unit_two, grad = take(3)
    inv_one, inv_two, key_mask, lse, vec = take(5)
    short, small_in, bias_row = take(3)
    g_send, g_recv, s_send, s_recv, q_send, q_recv, v_send, v_recv, b_send, b_recv, local = take(11)
    seq, width = tok.shape
    hidden = act.shape[1]
    pairs = width // 128
    parts = hidden // width
    line = fsdp_size // 2
    rows_of = pl.ds

    loads = [
        pltpu.make_async_copy(tokens_in, tok, local.at[0]),
        pltpu.make_async_copy(cot_in, cot, local.at[1]),
    ]
    for load in loads:
        load.start()
    place = Place(fsdp_size)
    place_vectors(place.shard, vectors, class_rows, short, small_in)
    bias_row[...] = jnp.zeros(bias_row.shape, F32)
    classes = class_bias.shape[0]
    bias_row[0:1, 13 : 13 + classes] = class_bias[...].astype(F32).reshape(1, classes)
    place.meet()
    everything, all_rows = [], shards[0].shape[0]
    for shard, whole in zip(shards, (w_in, w_mix, w_up, w_down, w_pool)):
        for row in range(0, shard.shape[0], all_rows):
            for col in range(0, shard.shape[1], width):
                rows, cols = pl.ds(row, all_rows), pl.ds(col, width)
                everything.append((shard.at[rows, cols], whole.at[:, :, rows, cols]))
    gathers = [Gather(place, *pair, g_send.at[i], g_recv.at[i]) for i, pair in enumerate(everything)]
    little = SmallGather(place, small_in, slope, v_send, v_recv)
    hops = range(1, line)
    first_mix, first_up, first_down, first_pool = 3, 4, 4 + parts, 4 + 2 * parts

    def tick(count):
        if count + AHEAD < len(gathers):
            gathers[count + AHEAD].begin()
        if 0 <= count - 3 < len(gathers):
            for hop in hops:
                gathers[count - 3].hand(hop)
        if count < len(gathers):
            for hop in hops:
                gathers[count].spread(hop)
        if 0 <= count - 1 < len(gathers):
            for hop in hops:
                gathers[count - 1].relay(hop)

    gathers[0].begin()
    little.begin()
    for one in gathers[1:AHEAD]:
        one.begin()
    length = lengths[0]
    label = labels[0]

    for load in loads:
        load.wait()
    tok_t[...] = tok[...].T
    key_at = lax.broadcasted_iota(jnp.int32, (seq, 128), 0)
    key_mask[...] = jnp.where(key_at < length, 0.0, -1e30).astype(F32)

    def mask_cot(index):
        rows = rows_of(pl.multiple_of(index * 128, 128), 128)
        live = (key_mask[rows, :] == 0.0).astype(F32)
        grad[rows, :] = cot[rows, :].astype(F32) * jnp.concatenate([live] * (width // 128), axis=1)

    loop(seq // 128, mask_cot)
    grad_low = cot

    tick(0)
    little.hand()
    tick(1)
    tick(2)
    little.ready()
    vec[...] = jnp.sum(slope[0 : 16 * fsdp_size, 0:width].reshape(fsdp_size, 16, width).astype(F32), axis=0)

    score_scale = 1.0 / math.sqrt(DH)
    for part in range(3):
        tick(3 + part)
        gathers[part].ready()

        def project(index, part=part):
            inner = lanes(index * 256, 256)
            cols = lanes(part * width + index * 256, 256)
            out = nn(tok[...], w_in[:, :, :, cols].reshape(width, 256))
            if part != 1:
                row = 0 if part == 0 else 1
                out = out + vec[row : row + 1, inner]
            out = out.astype(BF16)
            if part == 0:
                out = out * jnp.asarray(score_scale, BF16)
            qkv[:, cols] = out

        loop(width // 256, project)

    low_lanes = lax.broadcasted_iota(jnp.int32, (1, 128), 1) < 64
    zero_low = jnp.zeros((), BF16)

    def head_lanes(value, half):
        return jnp.where(low_lanes if half == 0 else jnp.logical_not(low_lanes), value, zero_low)

    def masked_scores(keys, queries):
        mask = key_mask[...]
        return nt(keys, queries) + jnp.concatenate([mask] * (seq // 128), axis=1)

    def attend(pair):
        queries, keys, values = (qkv[:, lanes(part * width + pair * 128, 128)] for part in range(3))
        values_t = values.T
        mixed = []
        for half in (0, 1):
            scores = masked_scores(keys, head_lanes(queries, half))
            highest = jnp.max(scores, axis=0, keepdims=True)
            raw = jnp.exp(scores - highest)
            total = jnp.sum(raw, axis=0, keepdims=True)
            lse[pair, half : half + 1, :] = highest + jnp.log(total)
            soft = (raw * (1.0 / total)).astype(BF16)
            mixed.append(nn(values_t, soft)[64 * half : 64 * half + 64, :])
        both = jnp.concatenate(mixed, axis=0)
        att_t[rows_of(pl.multiple_of(pair * 128, 128), 128), :] = both.astype(BF16)
        att[:, lanes(pair * 128, 128)] = both.T.astype(BF16)

    def attend_on(pair):
        attend(pair)
        for one in range(pairs):

            @pl.when(pair == one)
            def _(one=one):
                tick(6 + one)

    loop(pairs, attend_on)
    gathers[first_mix].ready()

    little.end()

    gain_one, shift_one = vec[3:4, :], vec[4:5, :]

    def mean_of(value):
        return jnp.sum(value, axis=1, keepdims=True) * (1.0 / width)

    def norm_one(index):
        rows = rows_of(pl.multiple_of(index * 256, 256), 256)
        total = nn(att[rows, :], w_mix[...].reshape(width, width)) + vec[2:3, :] + tok[rows, :].astype(F32)
        centered = total - mean_of(total)
        inverse = lax.rsqrt(mean_of(centered * centered) + EPSILON)
        unit = centered * inverse
        unit_one[rows, :] = unit
        inv_one[rows, :] = jnp.broadcast_to(inverse, (256, 128))
        first[rows, :] = (unit * gain_one + shift_one).astype(BF16)

    loop(seq // 256, norm_one)
    first_t[...] = first[...].T
    tick(6 + pairs)

    for part in range(parts):
        gathers[first_up + part].ready()

        def raise_up(index, part=part):
            inner = lanes(index * 384, 384)
            cols = lanes(part * width + index * 384, 384)
            pre = nn(first[...], w_up[:, :, :, cols].reshape(width, 384)) + vec[5 + part : 6 + part, inner]
            value, derivative = gelu_parts(pre)
            act[:, cols] = value.astype(BF16)
            slope[:, cols] = derivative.astype(BF16)

        loop(width // 384, raise_up)
        if part < 3:
            tick(7 + pairs + part)
    for one in gathers[first_down:first_pool]:
        one.ready()
    gain_two, shift_two = vec[10:11, :], vec[11:12, :]

    def norm_two(index):
        rows = rows_of(pl.multiple_of(index * 256, 256), 256)
        total = nn(act[rows, :], w_down[...].reshape(hidden, width)) + vec[9:10, :]
        total = total + (unit_one[rows, :] * gain_one + shift_one)
        centered = total - mean_of(total)
        inverse = lax.rsqrt(mean_of(centered * centered) + EPSILON)
        unit = centered * inverse
        unit_two[rows, :] = unit
        inv_two[rows, :] = jnp.broadcast_to(inverse, (256, 128))
        att[rows, :] = (unit * gain_two + shift_two).astype(BF16)

    loop(seq // 256, norm_two)
    stores = [pltpu.make_async_copy(att, layer_out, local.at[2])]
    stores[0].start()

    gathers[first_pool].ready()
    top = lax.broadcasted_iota(jnp.int32, (16, 1), 0) == 0
    head = att[0:16, :]
    vec_low = vec[...].astype(BF16)
    pooled = jnp.tanh(nn(head, w_pool[...].reshape(width, width)) + vec[12:13, :])
    pooled_low = pooled.astype(BF16)
    logits = nt(pooled_low, vec_low) + bias_row[0:1, 0:16]
    class_at = lax.broadcasted_iota(jnp.int32, (16, 16), 1) - 13
    logits = jnp.where(class_at >= 0, logits, -1e30)
    raised = jnp.exp(logits - jnp.max(logits, axis=1, keepdims=True))
    soft_logits = raised / jnp.sum(raised, axis=1, keepdims=True)
    onehot = (class_at == label).astype(F32)
    grad_logits = jnp.where(top, soft_logits - onehot, 0.0).astype(BF16)
    sums = sum_refs[0]
    sums[0:16, :] = tn(grad_logits, pooled_low)
    sums[16:24, :] = jnp.zeros((8, width), F32)
    sums[16:17, 0:16] = grad_logits[0:1, :].astype(F32)
    grad_pool_pre = (nn(grad_logits, vec_low) * (1.0 - pooled * pooled)).astype(BF16)
    sums[12:13, :] = grad_pool_pre[0:1, :].astype(F32)
    block = jnp.where(top, head.astype(F32), 0.0)
    second_row = lax.broadcasted_iota(jnp.int32, (16, 1), 0) == 1
    block = jnp.where(second_row, jnp.broadcast_to(grad_pool_pre[0:1, :].astype(F32), (16, width)), block)
    blocks[place.shard, place.dp] = block.astype(BF16)
    sequences = SequenceGather(place, blocks, q_send, q_recv)
    sequences.begin()
    grad[0:16, :] += nt(grad_pool_pre, w_pool[...].reshape(width, width))

    def norm_back(unit_ref, inv_ref, gain, gain_row, shift_row, bias_row, size):
        def one(index, carry):
            by_gain, by_shift, by_bias = carry
            rows = rows_of(pl.multiple_of(index * size, size), size)
            incoming = grad[rows, :]
            unit = unit_ref[rows, :]
            scaled = incoming * gain
            inverse = jnp.concatenate([inv_ref[rows, :]] * (width // 128), axis=1)
            back = inverse * (scaled - mean_of(scaled) - unit * mean_of(scaled * unit))
            low = back.astype(BF16)
            grad[rows, :] = back
            grad_low[rows, :] = low
            return (
                by_gain + jnp.sum(incoming * unit, axis=0, keepdims=True),
                by_shift + jnp.sum(incoming, axis=0, keepdims=True),
                by_bias + jnp.sum(low.astype(F32), axis=0, keepdims=True),
            )

        zero = jnp.zeros((1, width), F32)
        by_gain, by_shift, by_bias = lax.fori_loop(0, seq // size, one, (zero, zero, zero))
        sums[gain_row : gain_row + 1, :] = by_gain
        sums[shift_row : shift_row + 1, :] = by_shift
        sums[bias_row : bias_row + 1, :] = by_bias

    norm_back(unit_two, inv_two, gain_two, 10, 11, 9, 128)

    rows_down = hidden // fsdp_size
    few = 128
    many = rows_down - few
    pieces = [g_down.at[:, :, pl.ds(many, few), :], g_down.at[:, :, pl.ds(0, many), :]]
    pieces += [g_up.at[:, :, :, pl.ds(half * 2 * width, 2 * width)] for half in (0, 1)]
    pieces += [w_up.at[:, :, :, pl.ds(at * width, width)] for at in (3, 0, 1, 2)]
    scatters = [
        (LineFirst if i == 0 else Scatter)(place, ref, *recv[i], s_send.at[i], s_recv.at[i])
        for i, ref in enumerate(pieces)
    ]
    down_a, down_b, up_a, up_b, of_mix, in_a, in_b, in_c = scatters

    for first_row, count, one in ((many, few, down_a), (0, many, down_b)):

        def down_gradient(index, first_row=first_row, count=count):
            cols = lanes(index * rows_down + first_row, count)
            out = tn(act[:, cols], grad_low[...]).astype(BF16)
            g_down[index // 2, lax.rem(index, 2), pl.ds(first_row, count), :] = out

        loop(fsdp_size, down_gradient)
        one.swap()
    sequences.to_line()

    for part in range(parts):

        def through_down(index, part=part):
            owner = part * 2 + index
            inner = lanes(index * rows_down, rows_down)
            cols = lanes(owner * rows_down, rows_down)
            low = (nt(grad_low[...], w_down[part, index]) * slope[:, cols].astype(F32)).astype(BF16)
            slope[:, cols] = low
            sums[5 + part : 6 + part, inner] = jnp.sum(low.astype(F32), axis=0, keepdims=True)

        loop(2, through_down)

        def up_gradient(index, part=part):
            cols = lanes(part * width + index * 256, 256)
            out = nn(first_t[...], slope[:, cols]).astype(BF16)
            g_up[:, :, :, cols] = out.reshape(line, 2, width // fsdp_size, 256)

        loop(width // 256, up_gradient)
        if part == 0:
            down_a.to_first()
        if part == 1:
            up_a.swap()
            down_b.to_first()
        if part == 2:
            up_a.to_first()
        if part == 3:
            up_b.swap()
            down_b.to_second()
            sequences.hand()

    half_line = line // 2
    half_width = width // 2

    def through_up(index):
        cols = lanes(index * half_width, half_width)
        weight = w_up[rows_of(index * half_line, half_line)].reshape(half_width, hidden)
        grad[:, cols] += nt(slope[...], weight)
        for one in (0, 1):

            @pl.when(index == one)
            def _(one=one):
                if one == 0:
                    up_b.to_first()
                    down_b.to_line()
                else:
                    up_a.to_second()
                    down_a.to_second()

    loop(2, through_up)
    norm_back(unit_one, inv_one, gain_one, 3, 4, 2, 128)
    for one in gathers:
        one.end()

    def mix_gradient(index):
        out = nn(att_t[...], grad_low[:, lanes(index * 256, 256)]).astype(BF16)
        w_up[:, :, :, lanes(3 * width + index * 256, 256)] = out.reshape(line, 2, width // fsdp_size, 256)

    loop(width // 256, mix_gradient)
    of_mix.swap()
    up_b.to_second()

    def through_mix(index):
        cols = lanes(index * half_width, half_width)
        weight = w_mix[rows_of(index * half_line, half_line)].reshape(half_width, width)
        first[:, cols] = nt(grad_low[...], weight).astype(BF16)

    loop(2, through_mix)
    of_mix.to_first()
    up_a.to_line()

    def attend_back(pair):
        at = [lanes(part * width + pair * 128, 128) for part in range(3)]
        queries, keys, values = (qkv[:, cols] for cols in at)
        rows = rows_of(pl.multiple_of(pair * 128, 128), 128)
        out_grad = first[:, lanes(pair * 128, 128)]
        keys_t = keys.T
        products = out_grad.astype(F32).T * att_t[rows, :].astype(F32)
        by_query, by_key, by_value = [], None, None
        for half in (0, 1):
            own_queries, own_grad = head_lanes(queries, half), head_lanes(out_grad, half)
            soft = jnp.exp(masked_scores(keys, own_queries) - lse[pair, half : half + 1, :])
            row_sum = jnp.sum(products[64 * half : 64 * half + 64, :], axis=0, keepdims=True)
            score_grad = (soft * (nt(values, own_grad) - row_sum)).astype(BF16)
            value_part = nn(soft.astype(BF16), own_grad)
            key_part = nn(score_grad, own_queries)
            by_value = value_part if by_value is None else by_value + value_part
            by_key = key_part if by_key is None else by_key + key_part
            by_query.append(nn(keys_t, score_grad)[64 * half : 64 * half + 64, :])
        qkv[:, at[0]] = (jnp.concatenate(by_query, axis=0).T * score_scale).astype(BF16)
        qkv[:, at[1]] = by_key.astype(BF16)
        qkv[:, at[2]] = by_value.astype(BF16)

    after_pair = {
        0: [down_b.to_plane, down_a.to_line],
        1: [up_b.to_line, of_mix.to_second],
        2: [in_a.to_first, up_a.to_plane],
        3: [of_mix.to_line, in_a.to_second],
        4: [in_b.to_first, up_b.to_plane],
        5: [in_a.to_line, of_mix.to_plane, in_b.to_second],
    }

    def attend_back_on(pair):
        attend_back(pair)
        for one in range(pairs):

            @pl.when(pair == one)
            def _(one=one):
                for step in after_pair[one]:
                    step()

    def in_gradient(chunk):
        for part in range(3):
            inner = lanes(chunk * 256, 256)
            incoming = qkv[:, lanes(part * width + chunk * 256, 256)]
            out = nn(tok_t[...], incoming).astype(BF16).reshape(line, 2, width // fsdp_size, 256)
            w_up[:, :, :, lanes(chunk * width + part * 256, 256)] = out
            if part != 1:
                row = 0 if part == 0 else 1
                sums[row : row + 1, inner] = jnp.sum(incoming.astype(F32), axis=0, keepdims=True)

    def attend_chunk(chunk):
        lax.fori_loop(2 * chunk, 2 * chunk + 2, lambda pair, carry: (attend_back_on(pair), carry)[1], 0)
        in_gradient(chunk)
        for at, one in enumerate((in_a, in_b, in_c)):

            @pl.when(chunk == at)
            def _(one=one):
                one.swap()

    loop(pairs // 2, attend_chunk)
    sequences.ready()
    total = SmallSum(place, *sum_refs, b_send, b_recv)
    total.swap()

    def through_in(index):
        cols = lanes(index * half_width, half_width)
        weight = w_in[rows_of(index * half_line, half_line)].reshape(half_width, 3 * width)
        grad[:, cols] += nt(qkv[...], weight)
        for one in (0, 1):

            @pl.when(index == one)
            def _(one=one):
                if one == 0:
                    in_c.to_first()
                    in_b.to_line()
                else:
                    in_a.to_plane()

    loop(2, through_in)
    store = pltpu.make_async_copy(grad, input_grad, local.at[3])
    store.start()
    stores.append(store)
    in_c.to_second()
    total.to_line()
    in_b.to_plane()

    every = blocks[...].reshape(fsdp_size * 4 * 16, width)
    count = fsdp_size * 4 * 16
    row_at = lax.broadcasted_iota(jnp.int32, (count, count), 0)
    col_at = lax.broadcasted_iota(jnp.int32, (count, count), 1)
    shift = jnp.where((lax.rem(row_at, 16) == 0) & (col_at == row_at + 1), 1.0, 0.0).astype(BF16)
    paired = nn(shift, every).astype(BF16)
    own_rows_at = lax.broadcasted_iota(jnp.int32, (128, width), 0) + place.shard * (width // fsdp_size)
    pick = jnp.where(own_rows_at == lax.broadcasted_iota(jnp.int32, (128, width), 1), 1.0, 0.0).astype(BF16)
    own_part = nt(pick, every).astype(BF16)
    pool_out[...] = nn(own_part, paired)[0 : width // fsdp_size, :]

    in_c.to_line()
    total.to_plane()

    wide = 256
    kept = [
        (down_a, down_out, many, [(0, 0, width)]),
        (down_b, down_out, 0, [(0, 0, width)]),
        (up_a, up_out, 0, [(0, 0, 2 * width)]),
        (up_b, up_out, 0, [(0, 2 * width, 2 * width)]),
        (of_mix, mix_out, 0, [(0, 0, width)]),
    ]
    for chunk, one in enumerate((in_a, in_b, in_c)):
        kept.append((one, in_out, 0, [(part * wide, part * width + chunk * wide, wide) for part in range(3)]))

    def keep(one, out, first_row, spans):
        one.finish()
        half_rows, half_cols = one.rows // 2, one.cols // 2
        for row_half in (0, 1):
            rows = pl.ds(first_row + row_half * half_rows, half_rows)
            for col_half in (0, 1):
                begin, end = col_half * half_cols, (col_half + 1) * half_cols
                for here, there, count in spans:
                    low, high = max(here, begin), min(here + count, end)
                    if low < high:
                        source = one.done.at[row_half, col_half, :, pl.ds(low - begin, high - low)]
                        target = out.at[rows, pl.ds(there + low - here, high - low)]
                        store = pltpu.make_async_copy(source, target, local.at[len(stores) + 2])
                        store.start()
                        stores.append(store)

    for item in kept[:-1]:
        keep(*item)
    total.finish(total.from_core)
    own_sums(place.shard, fsdp_size, total.from_core, sums_out, classes)
    in_c.to_plane()
    keep(*kept[-1])
    for store in stores:
        store.wait()
    for one in scatters + [sequences, total]:
        one.end()


def run_layer(fsdp_size, lengths, labels, class_bias, tokens, cotangent, shards, vectors, class_rows):
    line = fsdp_size // 2
    seq, width = tokens.shape
    in_shard, mix_shard, up_shard, down_shard, pool_shard = shards
    hidden = up_shard.shape[1]
    vmem, dma = pltpu.VMEM, pltpu.SemaphoreType.DMA
    reduced = (down_shard, up_shard, mix_shard, in_shard)
    block = width // fsdp_size
    few = 128
    sizes = [(few, width), (down_shard.shape[0] - few, width)] + [(block, 2 * width)] * 2 + [(block, width)] * 4
    scratch = [vmem((line, 2) + s.shape, BF16) for s in shards]
    scratch += [vmem((line, 2) + s.shape, BF16) for s in (down_shard, up_shard)]
    for i, size in enumerate(sizes):
        scratch += (LineFirst if i == 0 else Scatter).scratch(line, *size)
    del scratch[-5]
    scratch += SmallSum.scratch(line, 24, width)
    scratch += [vmem((fsdp_size, 4, 16, width), BF16)]
    rows, turned = vmem((seq, width), BF16), vmem((width, seq), BF16)
    scratch += [rows, turned, rows, rows, turned, rows, turned]
    scratch += [vmem((seq, 3 * width), BF16), vmem((seq, hidden), BF16), vmem((seq, hidden), BF16)]
    scratch += [vmem((seq, width), F32)] * 3
    scratch += [vmem((seq, 128), F32)] * 3 + [vmem((width // 128, 8, seq), F32), vmem((16, width), F32)]
    span = hidden // fsdp_size
    scratch += [vmem((16, span), F32), vmem((16, width), BF16), vmem((8, 128), F32)]
    for count in (
        (sum(s.shape[0] * s.shape[1] for s in shards) // (block * width), Gather.sems(line)),
        (len(sizes), Scatter.sems(line)),
        (SequenceGather.sems(line),),
        (SmallGather.sems(line),),
        (SmallSum.sems(line),),
    ):
        scratch += [dma(count), dma(count)]
    scratch += [dma((64,))]
    out_shape = [jax.ShapeDtypeStruct((seq, width), BF16), jax.ShapeDtypeStruct((seq, width), F32)]
    out_shape += [jax.ShapeDtypeStruct(s.shape, BF16) for s in reduced]
    out_shape += [jax.ShapeDtypeStruct((width // fsdp_size, width), F32), jax.ShapeDtypeStruct((32, span), F32)]
    return pl.pallas_call(
        functools.partial(layer_kernel, fsdp_size),
        out_shape=out_shape,
        in_specs=[SCALARS, SCALARS, WHOLE] + [ANY] * 7 + [WHOLE] * 10,
        out_specs=[ANY] * 6 + [WHOLE] * 2,
        scratch_shapes=scratch,
        compiler_params=pltpu.CompilerParams(collective_id=0, has_side_effects=True, vmem_limit_bytes=VMEM_BYTES),
        name="layer",
    )(lengths, labels, class_bias, tokens, cotangent, *shards, *vectors, class_rows)


def outputs_kernel(as_is, rounded, sizes, classes, size, *refs):
    count = as_is + rounded
    inputs, sums = refs[:count], refs[count]
    refs = refs[count + 1 :]
    outs, small = refs[:count], refs[count : count + len(sizes) + 2]
    refs = refs[count + len(sizes) + 2 :]
    held, wide, (load_sems, store_sems) = refs[:count], refs[count : count + rounded], refs[count + rounded :]
    order = list(range(as_is, count)) + list(range(as_is))
    loads = {i: pltpu.make_async_copy(inputs[i], held[i], load_sems.at[i]) for i in order}
    for load in loads.values():
        load.start()
    for (row, length), out in zip(sizes.items(), small):
        out[...] = sums[row : row + 1, 0:length].reshape(length)
    small[-2][...] = sums[13 : 13 + classes, 0:size]
    small[-1][...] = sums[26:27, 0:classes].reshape(classes)
    stores = []
    for i in order:
        loads[i].wait()
        source = held[i]
        if i >= as_is:
            source = wide[i - as_is]
            step = 32

            def widen(index, narrow=held[i], source=source):
                rows = pl.ds(pl.multiple_of(index * step, step), step)
                source[rows, :] = narrow[rows, :].astype(F32)

            loop(source.shape[0] // step, widen)
        stores.append(pltpu.make_async_copy(source, outs[i], store_sems.at[i]))
        stores[-1].start()
    for store in stores:
        store.wait()


def run_outputs(as_is, rounded, sums, sizes, classes, size):
    arrays = as_is + rounded
    out_shape = [jax.ShapeDtypeStruct(a.shape, a.dtype) for a in as_is]
    out_shape += [jax.ShapeDtypeStruct(a.shape, F32) for a in rounded]
    out_shape += [jax.ShapeDtypeStruct((length,), F32) for length in sizes.values()]
    out_shape += [jax.ShapeDtypeStruct((classes, size), F32), jax.ShapeDtypeStruct((classes,), F32)]
    scratch = [pltpu.VMEM(a.shape, a.dtype) for a in arrays] + [pltpu.VMEM(a.shape, F32) for a in rounded]
    scratch += [pltpu.SemaphoreType.DMA((len(arrays),))] * 2
    return pl.pallas_call(
        functools.partial(outputs_kernel, len(as_is), len(rounded), sizes, classes, size),
        out_shape=out_shape,
        in_specs=[ANY] * len(arrays) + [WHOLE],
        out_specs=[ANY] * len(arrays) + [WHOLE] * (len(sizes) + 2),
        scratch_shapes=scratch,
        compiler_params=pltpu.CompilerParams(vmem_limit_bytes=VMEM_BYTES),
        name="outputs",
    )(*arrays, sums)


def kernel_body(
    fsdp_size,
    tokens,
    in_weight,
    in_bias,
    mix_weight,
    mix_bias,
    first_gain,
    first_shift,
    up_weight,
    up_bias,
    down_weight,
    down_bias,
    second_gain,
    second_shift,
    pool_weight,
    pool_bias,
    class_weight,
    class_bias,
    lengths,
    labels,
    cotangent,
):
    layer_out, input_grad, down_grad, up_grad, mix_grad, in_grad, pool_grad, sums = run_layer(
        fsdp_size,
        lengths,
        labels,
        class_bias,
        tokens,
        cotangent,
        (in_weight, mix_weight, up_weight, down_weight, pool_weight),
        (in_bias, mix_bias, first_gain, first_shift, up_bias, down_bias, second_gain, second_shift, pool_bias),
        class_weight.T,
    )
    size = mix_bias.shape[0]
    sizes = {24: 2 * size, 2: size, 3: size, 4: size, 25: 4 * size, 9: size, 10: size, 11: size, 12: size}
    outs = run_outputs(
        (layer_out, input_grad, pool_grad),
        (in_grad, mix_grad, up_grad, down_grad),
        sums,
        sizes,
        class_bias.shape[0],
        size,
    )
    layer_out, input_grad, pool_grad, in_grad, mix_grad, up_grad, down_grad = outs[:7]
    of_in, of_mix, of_gain_one, of_shift_one, of_up, of_down, of_gain_two, of_shift_two, of_pool = outs[7:16]
    class_grad, class_bias_grad = outs[16:]
    return (
        layer_out,
        input_grad,
        in_grad,
        of_in,
        mix_grad,
        of_mix,
        of_gain_one,
        of_shift_one,
        up_grad,
        of_up,
        down_grad,
        of_down,
        of_gain_two,
        of_shift_two,
        pool_grad,
        of_pool,
        class_grad.T,
        class_bias_grad,
    )


def plain_body(
    tokens,
    in_weight,
    in_bias,
    mix_weight,
    mix_bias,
    first_gain,
    first_shift,
    up_weight,
    up_bias,
    down_weight,
    down_bias,
    second_gain,
    second_shift,
    pool_weight,
    pool_bias,
    class_weight,
    class_bias,
    lengths,
    labels,
    cotangent,
):
    gathered = (
        lax.all_gather(in_weight, "fsdp", axis=0, tiled=True),
        lax.all_gather(in_bias, "fsdp", axis=0, tiled=True),
        lax.all_gather(mix_weight, "fsdp", axis=0, tiled=True),
        lax.all_gather(mix_bias, "fsdp", axis=0, tiled=True),
        lax.all_gather(first_gain, "fsdp", axis=0, tiled=True),
        lax.all_gather(first_shift, "fsdp", axis=0, tiled=True),
        lax.all_gather(up_weight, "fsdp", axis=0, tiled=True),
        lax.all_gather(up_bias, "fsdp", axis=0, tiled=True),
        lax.all_gather(down_weight, "fsdp", axis=0, tiled=True),
        lax.all_gather(down_bias, "fsdp", axis=0, tiled=True),
        lax.all_gather(second_gain, "fsdp", axis=0, tiled=True),
        lax.all_gather(second_shift, "fsdp", axis=0, tiled=True),
        lax.all_gather(pool_weight, "fsdp", axis=0, tiled=True),
        lax.all_gather(pool_bias, "fsdp", axis=0, tiled=True),
        lax.all_gather(class_weight, "fsdp", axis=0, tiled=True),
    )
    (
        whole_in,
        bias_in,
        whole_mix,
        bias_mix,
        gain_one,
        shift_one,
        whole_up,
        bias_up,
        whole_down,
        bias_down,
        gain_two,
        shift_two,
        whole_pool,
        bias_pool,
        whole_class,
    ) = gathered
    token_rows = tokens.shape[0]
    seq_count = lengths.shape[0]
    seq_len = token_rows // seq_count
    model_width = whole_mix.shape[0]
    score_scale = 1.0 / math.sqrt(DH)
    positions = jnp.arange(seq_len)
    projected = jnp.dot(tokens, whole_in, preferred_element_type=jnp.float32)
    in_bias_f = bias_in.astype(jnp.float32)
    head_shape = (seq_count, seq_len, H, DH)
    queries = (
        (projected[:, :model_width] + in_bias_f[:model_width])
        .astype(jnp.bfloat16)
        .reshape(head_shape)
    )
    keys_all = projected[:, model_width : 2 * model_width].astype(jnp.bfloat16).reshape(head_shape)
    values_all = (
        (projected[:, 2 * model_width :] + in_bias_f[model_width:])
        .astype(jnp.bfloat16)
        .reshape(head_shape)
    )

    def scores_of(query_blk, key_blk, length):
        raw_scores = (
            jnp.einsum("qhd,khd->hqk", query_blk, key_blk, preferred_element_type=jnp.float32)
            * score_scale
        )
        return jnp.where(positions[None, None, :] < length, raw_scores, -1e30)

    def attend_fore(block_items):
        query_blk, key_blk, value_blk, length = block_items
        scores = scores_of(query_blk, key_blk, length)
        highest = jnp.max(scores, axis=-1, keepdims=True)
        raw_weights = jnp.exp(scores - highest)
        totals = jnp.sum(raw_weights, axis=-1, keepdims=True)
        softmaxed = (raw_weights / totals).astype(jnp.bfloat16)
        mixed_values = jnp.einsum(
            "hqk,khd->qhd", softmaxed, value_blk, preferred_element_type=jnp.float32
        )
        return (mixed_values, (highest + jnp.log(totals))[..., 0])

    attended, logsum = lax.map(attend_fore, (queries, keys_all, values_all, lengths))
    attn_low = attended.reshape(token_rows, model_width).astype(jnp.bfloat16)
    branch = jnp.dot(attn_low, whole_mix, preferred_element_type=jnp.float32) + bias_mix.astype(
        jnp.float32
    )
    first_norm, unit_one, inverse_one = norm_fore(
        tokens.astype(jnp.float32) + branch,
        gain_one.astype(jnp.float32),
        shift_one.astype(jnp.float32),
    )
    first_low = first_norm.astype(jnp.bfloat16)
    pre_act = jnp.dot(first_low, whole_up, preferred_element_type=jnp.float32) + bias_up.astype(
        jnp.float32
    )
    activated, gelu_pull = jax.vjp(partial(jax.nn.gelu, approximate=False), pre_act)
    act_low = activated.astype(jnp.bfloat16)
    ffn_out = jnp.dot(act_low, whole_down, preferred_element_type=jnp.float32) + bias_down.astype(
        jnp.float32
    )
    result, unit_two, inverse_two = norm_fore(
        first_norm + ffn_out, gain_two.astype(jnp.float32), shift_two.astype(jnp.float32)
    )
    head_rows = result.reshape(seq_count, seq_len, model_width)[:, 0, :].astype(jnp.bfloat16)
    pooled = jnp.tanh(
        jnp.dot(head_rows, whole_pool, preferred_element_type=jnp.float32)
        + bias_pool.astype(jnp.float32)
    )
    pooled_low = pooled.astype(jnp.bfloat16)
    logits = jnp.dot(
        pooled_low, whole_class, preferred_element_type=jnp.float32
    ) + class_bias.astype(jnp.float32)
    back_in, back_mix, back_gain_one, back_up, back_down, back_gain_two, back_pool, back_class = (
        lax.all_gather(in_weight, "fsdp", axis=0, tiled=True),
        lax.all_gather(mix_weight, "fsdp", axis=0, tiled=True),
        lax.all_gather(first_gain, "fsdp", axis=0, tiled=True),
        lax.all_gather(up_weight, "fsdp", axis=0, tiled=True),
        lax.all_gather(down_weight, "fsdp", axis=0, tiled=True),
        lax.all_gather(second_gain, "fsdp", axis=0, tiled=True),
        lax.all_gather(pool_weight, "fsdp", axis=0, tiled=True),
        lax.all_gather(class_weight, "fsdp", axis=0, tiled=True),
    )
    onehot = (labels[:, None] == jnp.arange(logits.shape[1])[None, :]).astype(jnp.float32)
    grad_logits = (jax.nn.softmax(logits, axis=-1) - onehot).astype(jnp.bfloat16)
    grad_class_weight = jnp.dot(pooled_low.T, grad_logits, preferred_element_type=jnp.float32)
    grad_class_bias = column_sums(grad_logits)
    grad_pool_pre = (
        jnp.dot(grad_logits, back_class.T, preferred_element_type=jnp.float32)
        * (1.0 - pooled * pooled)
    ).astype(jnp.bfloat16)
    grad_pool_weight = jnp.dot(head_rows.T, grad_pool_pre, preferred_element_type=jnp.float32)
    grad_pool_bias = column_sums(grad_pool_pre)
    grad_head_rows = jnp.dot(grad_pool_pre, back_pool.T, preferred_element_type=jnp.float32)
    live_mask = (positions[None, :] < lengths[:, None]).astype(jnp.float32)
    grad_result = (
        cotangent.astype(jnp.float32).reshape(seq_count, seq_len, model_width)
        * live_mask[:, :, None]
    )
    grad_result = grad_result.at[:, 0, :].add(grad_head_rows).reshape(token_rows, model_width)
    grad_sum_two, grad_second_gain, grad_second_shift = norm_back(
        grad_result, unit_two, inverse_two, back_gain_two.astype(jnp.float32)
    )
    grad_ffn = grad_sum_two.astype(jnp.bfloat16)
    grad_down_weight = jnp.dot(act_low.T, grad_ffn, preferred_element_type=jnp.float32)
    grad_down_bias = column_sums(grad_ffn)
    grad_pre = gelu_pull(jnp.dot(grad_ffn, back_down.T, preferred_element_type=jnp.float32))[
        0
    ].astype(jnp.bfloat16)
    grad_up_weight = jnp.dot(first_low.T, grad_pre, preferred_element_type=jnp.float32)
    grad_up_bias = column_sums(grad_pre)
    grad_first_norm = grad_sum_two + jnp.dot(
        grad_pre, back_up.T, preferred_element_type=jnp.float32
    )
    grad_sum_one, grad_first_gain, grad_first_shift = norm_back(
        grad_first_norm, unit_one, inverse_one, back_gain_one.astype(jnp.float32)
    )
    grad_branch = grad_sum_one.astype(jnp.bfloat16)
    grad_mix_weight = jnp.dot(attn_low.T, grad_branch, preferred_element_type=jnp.float32)
    grad_mix_bias = column_sums(grad_branch)
    grad_attended = (
        jnp.dot(grad_branch, back_mix.T, preferred_element_type=jnp.float32)
        .astype(jnp.bfloat16)
        .reshape(head_shape)
    )

    def attend_back(block_items):
        query_blk, key_blk, value_blk, length, lse_blk, grad_blk = block_items
        softmaxed = jnp.exp(scores_of(query_blk, key_blk, length) - lse_blk[..., None])
        grad_value = jnp.einsum(
            "hqk,qhd->khd",
            softmaxed.astype(jnp.bfloat16),
            grad_blk,
            preferred_element_type=jnp.float32,
        )
        grad_soft = jnp.einsum(
            "qhd,khd->hqk", grad_blk, value_blk, preferred_element_type=jnp.float32
        )
        grad_scores = (
            softmaxed * (grad_soft - jnp.sum(softmaxed * grad_soft, axis=-1, keepdims=True))
        ).astype(jnp.bfloat16)
        grad_query = (
            jnp.einsum("hqk,khd->qhd", grad_scores, key_blk, preferred_element_type=jnp.float32)
            * score_scale
        )
        grad_key = (
            jnp.einsum("hqk,qhd->khd", grad_scores, query_blk, preferred_element_type=jnp.float32)
            * score_scale
        )
        return (grad_query, grad_key, grad_value)

    grad_queries, grad_keys, grad_values = lax.map(
        attend_back, (queries, keys_all, values_all, lengths, logsum, grad_attended)
    )
    grad_proj = jnp.concatenate(
        [
            grad_queries.reshape(token_rows, model_width),
            grad_keys.reshape(token_rows, model_width),
            grad_values.reshape(token_rows, model_width),
        ],
        axis=1,
    ).astype(jnp.bfloat16)
    grad_in_weight = jnp.dot(tokens.T, grad_proj, preferred_element_type=jnp.float32)
    proj_sums = column_sums(grad_proj)
    grad_in_bias = jnp.concatenate([proj_sums[:model_width], proj_sums[2 * model_width :]])
    input_grad = grad_sum_one + jnp.dot(grad_proj, back_in.T, preferred_element_type=jnp.float32)
    gradients = (
        grad_in_weight,
        grad_in_bias,
        grad_mix_weight,
        grad_mix_bias,
        grad_first_gain,
        grad_first_shift,
        grad_up_weight,
        grad_up_bias,
        grad_down_weight,
        grad_down_bias,
        grad_second_gain,
        grad_second_shift,
        grad_pool_weight,
        grad_pool_bias,
        grad_class_weight,
    )
    shard_sums = (
        lax.psum_scatter(gradients[0], "fsdp", scatter_dimension=0, tiled=True),
        lax.psum_scatter(gradients[1], "fsdp", scatter_dimension=0, tiled=True),
        lax.psum_scatter(gradients[2], "fsdp", scatter_dimension=0, tiled=True),
        lax.psum_scatter(gradients[3], "fsdp", scatter_dimension=0, tiled=True),
        lax.psum_scatter(gradients[4], "fsdp", scatter_dimension=0, tiled=True),
        lax.psum_scatter(gradients[5], "fsdp", scatter_dimension=0, tiled=True),
        lax.psum_scatter(gradients[6], "fsdp", scatter_dimension=0, tiled=True),
        lax.psum_scatter(gradients[7], "fsdp", scatter_dimension=0, tiled=True),
        lax.psum_scatter(gradients[8], "fsdp", scatter_dimension=0, tiled=True),
        lax.psum_scatter(gradients[9], "fsdp", scatter_dimension=0, tiled=True),
        lax.psum_scatter(gradients[10], "fsdp", scatter_dimension=0, tiled=True),
        lax.psum_scatter(gradients[11], "fsdp", scatter_dimension=0, tiled=True),
        lax.psum_scatter(gradients[12], "fsdp", scatter_dimension=0, tiled=True),
        lax.psum_scatter(gradients[13], "fsdp", scatter_dimension=0, tiled=True),
        lax.psum_scatter(gradients[14], "fsdp", scatter_dimension=0, tiled=True),
    )
    summed = (
        lax.psum(shard_sums[0].astype(jnp.bfloat16), "dp").astype(jnp.float32),
        lax.psum(shard_sums[1].astype(jnp.bfloat16), "dp").astype(jnp.float32),
        lax.psum(shard_sums[2].astype(jnp.bfloat16), "dp").astype(jnp.float32),
        lax.psum(shard_sums[3].astype(jnp.bfloat16), "dp").astype(jnp.float32),
        lax.psum(shard_sums[4].astype(jnp.bfloat16), "dp").astype(jnp.float32),
        lax.psum(shard_sums[5].astype(jnp.bfloat16), "dp").astype(jnp.float32),
        lax.psum(shard_sums[6].astype(jnp.bfloat16), "dp").astype(jnp.float32),
        lax.psum(shard_sums[7].astype(jnp.bfloat16), "dp").astype(jnp.float32),
        lax.psum(shard_sums[8].astype(jnp.bfloat16), "dp").astype(jnp.float32),
        lax.psum(shard_sums[9].astype(jnp.bfloat16), "dp").astype(jnp.float32),
        lax.psum(shard_sums[10].astype(jnp.bfloat16), "dp").astype(jnp.float32),
        lax.psum(shard_sums[11].astype(jnp.bfloat16), "dp").astype(jnp.float32),
        lax.psum(shard_sums[12].astype(jnp.bfloat16), "dp").astype(jnp.float32),
        lax.psum(shard_sums[13].astype(jnp.bfloat16), "dp").astype(jnp.float32),
        lax.psum(shard_sums[14].astype(jnp.bfloat16), "dp").astype(jnp.float32),
    )
    bias_total = lax.psum(grad_class_bias, ("dp", "fsdp"))
    return (
        result.astype(jnp.bfloat16),
        input_grad,
        summed[0],
        summed[1],
        summed[2],
        summed[3],
        summed[4],
        summed[5],
        summed[6],
        summed[7],
        summed[8],
        summed[9],
        summed[10],
        summed[11],
        summed[12],
        summed[13],
        summed[14],
        bias_total,
    )


def solution(mesh):
    in_specs = (
        P(("dp", "fsdp"), None),
        P("fsdp", None),
        P("fsdp"),
        P("fsdp", None),
        P("fsdp"),
        P("fsdp"),
        P("fsdp"),
        P("fsdp", None),
        P("fsdp"),
        P("fsdp", None),
        P("fsdp"),
        P("fsdp"),
        P("fsdp"),
        P("fsdp", None),
        P("fsdp"),
        P("fsdp", None),
        P(),
        P(("dp", "fsdp")),
        P(("dp", "fsdp")),
        P(("dp", "fsdp"), None),
    )
    out_specs = (
        P(("dp", "fsdp"), None),
        P(("dp", "fsdp"), None),
        P("fsdp", None),
        P("fsdp"),
        P("fsdp", None),
        P("fsdp"),
        P("fsdp"),
        P("fsdp"),
        P("fsdp", None),
        P("fsdp"),
        P("fsdp", None),
        P("fsdp"),
        P("fsdp"),
        P("fsdp"),
        P("fsdp", None),
        P("fsdp"),
        P("fsdp", None),
        P(),
    )
    dp_size, fsdp_size = mesh.shape["dp"], mesh.shape["fsdp"]
    body = partial(kernel_body, fsdp_size) if (dp_size, fsdp_size) == (4, 8) else plain_body
    return jax.shard_map(body, mesh=mesh, in_specs=in_specs, out_specs=out_specs, check_vma=False)
```

```python
import functools
from functools import partial
import math

import jax
import jax.numpy as jnp
from jax import lax
from jax.experimental import pallas as pl
from jax.experimental.pallas import tpu as pltpu
from jax.sharding import PartitionSpec as P

H = 12
DH = 64


EPSILON = 1e-06


def norm_fore(vector, norm_gain, norm_shift):
    average = jnp.mean(vector, axis=-1, keepdims=True)
    centered = vector - average
    inverse = lax.rsqrt(jnp.mean(centered * centered, axis=-1, keepdims=True) + EPSILON)
    normed = centered * inverse
    return (normed * norm_gain + norm_shift, normed, inverse)


def norm_back(gradient, normed, inverse, norm_gain):
    scaled = gradient * norm_gain
    inner_mean = jnp.mean(scaled, axis=-1, keepdims=True)
    cross_mean = jnp.mean(scaled * normed, axis=-1, keepdims=True)
    input_part = inverse * (scaled - inner_mean - normed * cross_mean)
    return (input_part, jnp.sum(gradient * normed, axis=0), jnp.sum(gradient, axis=0))


def column_sums(matrix):
    return jnp.sum(matrix.astype(jnp.float32), axis=0)


MESH = pl.DeviceIdType.MESH


def remote(src, dst, send_sem, recv_sem, target):
    return pltpu.make_async_remote_copy(
        src_ref=src, dst_ref=dst, send_sem=send_sem, recv_sem=recv_sem, device_id=target, device_id_type=MESH
    )


class Place:
    def __init__(self, fsdp_size):
        self.dp = lax.axis_index("dp")
        self.shard = lax.axis_index("fsdp")
        self.line = fsdp_size // 2
        self.row_half, self.col_half = self.dp // 2, lax.rem(self.dp, 2)
        self.spot, self.core = self.shard // 2, lax.rem(self.shard, 2)
        across = 2 * self.row_half + (1 - self.col_half)
        along = 2 * (1 - self.row_half) + self.col_half
        self.first = jnp.where(self.core == 0, across, along)
        self.second = jnp.where(self.core == 0, along, across)

    def partner(self):
        return {"dp": self.dp, "fsdp": 2 * self.spot + 1 - self.core}

    def on_line(self, hop):
        return {"dp": self.dp, "fsdp": 2 * lax.rem(self.spot + hop, self.line) + self.core}

    def in_plane(self, dp):
        return {"dp": dp, "fsdp": self.shard}

    def source_spot(self, hop):
        return lax.rem(self.spot + self.line - hop, self.line)

    def peers(self):
        return (
            [self.partner()]
            + [self.on_line(hop) for hop in range(1, self.line)]
            + [self.in_plane(lax.rem(self.dp + step, 4)) for step in range(1, 4)]
        )

    def meet(self):
        barrier = pltpu.get_barrier_semaphore()
        peers = self.peers()
        for peer in peers:
            pl.semaphore_signal(barrier, inc=1, device_id=peer, device_id_type=MESH)
        pl.semaphore_wait(barrier, len(peers))


class Gather:
    def __init__(self, place, shard_ref, whole_ref, send_sems, recv_sems):
        self.place, self.shard_ref, self.whole = place, shard_ref, whole_ref
        self.send_sems, self.recv_sems = send_sems, recv_sems
        self.rows, self.cols = shard_ref.shape
        self.hops = place.line - 1
        self.started = []

    @staticmethod
    def sems(line):
        return 5 * (line - 1) + 2

    def block(self, shard):
        return self.whole.at[shard // 2, lax.rem(shard, 2)]

    def quarter(self, shard, row_half, col_half):
        half_rows, half_cols = self.rows // 2, self.cols // 2
        return self.whole.at[
            shard // 2,
            lax.rem(shard, 2),
            pl.ds(pl.multiple_of(row_half * half_rows, 16), half_rows),
            pl.ds(pl.multiple_of(col_half * half_cols, 128), half_cols),
        ]

    def go(self, index, src, dst, target):
        remote(src, dst, self.send_sems.at[index], self.recv_sems.at[index], target).start()
        self.started.append((index, dst.shape[-2:]))

    def arrived(self, index, dst):
        remote(dst, dst, self.send_sems.at[index], self.recv_sems.at[index], self.place.partner()).wait_recv()

    def begin(self):
        p = self.place
        half_rows, half_cols = self.rows // 2, self.cols // 2
        piece = self.shard_ref.at[
            pl.ds(pl.multiple_of(p.row_half * half_rows, 16), half_rows),
            pl.ds(pl.multiple_of(p.col_half * half_cols, 128), half_cols),
        ]
        for hop in range(1, p.line):
            self.go(hop - 1, piece, self.quarter(p.shard, p.row_half, p.col_half), p.on_line(hop))
        self.go(4 * self.hops, self.shard_ref, self.block(p.shard), p.partner())
        self.own().start()

    def own(self):
        return pltpu.make_async_copy(
            self.shard_ref, self.block(self.place.shard), self.recv_sems.at[5 * self.hops + 1]
        )

    def source(self, hop):
        return 2 * self.place.source_spot(hop) + self.place.core

    def spread(self, hop):
        p = self.place
        quarter = self.quarter(self.source(hop), p.row_half, p.col_half)
        self.arrived(hop - 1, quarter)
        self.go(self.hops + hop - 1, quarter, quarter, p.in_plane(p.first))
        self.go(2 * self.hops + hop - 1, quarter, quarter, p.in_plane(p.second))

    def relay(self, hop):
        p = self.place
        quarter = self.quarter(self.source(hop), p.first // 2, lax.rem(p.first, 2))
        self.arrived(self.hops + hop - 1, quarter)
        self.go(3 * self.hops + hop - 1, quarter, quarter, p.in_plane(p.second))

    def hand(self, hop):
        p = self.place
        self.arrived(2 * self.hops + hop - 1, self.quarter(self.source(hop), p.second // 2, lax.rem(p.second, 2)))
        self.arrived(3 * self.hops + hop - 1, self.quarter(self.source(hop), 1 - p.row_half, 1 - p.col_half))
        block = self.block(self.source(hop))
        self.go(4 * self.hops + hop, block, block, p.partner())

    def ready(self):
        p = self.place
        self.own().wait()
        self.arrived(4 * self.hops, self.block(p.shard + 1 - 2 * p.core))
        for hop in range(1, p.line):
            self.arrived(4 * self.hops + hop, self.block(2 * p.source_spot(hop) + 1 - p.core))

    def end(self):
        for index, (rows, cols) in self.started:
            like = self.whole.at[0, 0, pl.ds(0, rows), pl.ds(0, cols)]
            remote(like, like, self.send_sems.at[index], self.recv_sems.at[index], self.place.partner()).wait_send()


class SmallGather:
    def __init__(self, place, own_ref, all_ref, send_sems, recv_sems):
        self.place, self.own_ref, self.all = place, own_ref, all_ref
        self.send_sems, self.recv_sems = send_sems, recv_sems
        self.hops = place.line - 1
        self.started = []

    def at(self, shard):
        rows, cols = self.own_ref.shape
        return self.all.at[pl.ds(pl.multiple_of(shard * rows, rows), rows), pl.ds(0, cols)]

    @staticmethod
    def sems(line):
        return 2 * (line - 1) + 2

    def go(self, index, src, dst, target):
        copy = remote(src, dst, self.send_sems.at[index], self.recv_sems.at[index], target)
        copy.start()
        self.started.append(copy)

    def arrived(self, index, dst):
        remote(dst, dst, self.send_sems.at[index], self.recv_sems.at[index], self.place.partner()).wait_recv()

    def begin(self):
        p = self.place
        for hop in range(1, p.line):
            self.go(hop - 1, self.own_ref, self.at(p.shard), p.on_line(hop))
        self.go(2 * self.hops, self.own_ref, self.at(p.shard), p.partner())
        self.own = pltpu.make_async_copy(self.own_ref, self.at(p.shard), self.recv_sems.at[2 * self.hops + 1])
        self.own.start()

    def hand(self):
        p = self.place
        for hop in range(1, p.line):
            block = self.at(2 * p.source_spot(hop) + p.core)
            self.arrived(hop - 1, block)
            self.go(self.hops + hop - 1, block, block, p.partner())

    def ready(self):
        p = self.place
        self.own.wait()
        self.arrived(2 * self.hops, self.at(p.shard + 1 - 2 * p.core))
        for hop in range(1, p.line):
            self.arrived(self.hops + hop - 1, self.at(2 * p.source_spot(hop) + 1 - p.core))

    def end(self):
        for copy in self.started:
            copy.wait_send()


class Scatter:
    def __init__(self, place, grad, from_core, from_first, from_second, from_line, done, send_sems, recv_sems):
        self.place, self.grad = place, grad
        self.from_core, self.from_first, self.from_second = from_core, from_first, from_second
        self.from_line, self.done = from_line, done
        self.send_sems, self.recv_sems = send_sems, recv_sems
        self.line, _, self.rows, self.cols = grad.shape

    @staticmethod
    def sems(line):
        return 1 + 2 + 1 + (line - 1) + 3

    @staticmethod
    def scratch(line, rows, cols):
        half = (rows // 2, cols // 2)
        return [
            pltpu.VMEM((line, rows, cols), jnp.bfloat16),
            pltpu.VMEM((2, line) + half, jnp.bfloat16),
            pltpu.VMEM((line,) + half, jnp.bfloat16),
            pltpu.VMEM((line - 1,) + half, jnp.bfloat16),
            pltpu.VMEM((2, 2) + half, jnp.bfloat16),
        ]

    def go(self, index, src, dst, target):
        remote(src, dst, self.send_sems.at[index], self.recv_sems.at[index], target).start()

    def arrived(self, index, dst):
        remote(dst, dst, self.send_sems.at[index], self.recv_sems.at[index], self.place.partner()).wait_recv()

    def slices(self, row_half, col_half):
        half_rows, half_cols = self.rows // 2, self.cols // 2
        return (
            pl.ds(pl.multiple_of(row_half * half_rows, 16), half_rows),
            pl.ds(pl.multiple_of(col_half * half_cols, 128), half_cols),
        )

    def halves(self, side, which):
        p = self.place
        row_half = which * (1 - p.core) + side * p.core
        col_half = side * (1 - p.core) + which * p.core
        return self.slices(row_half, col_half)

    def swap(self):
        p = self.place
        self.go(0, self.grad.at[:, 1 - p.core], self.from_core, p.partner())

    def add(self, rows, cols, others, targets_spot=None):
        p = self.place
        half_rows, half_cols = self.rows // 2, self.cols // 2
        step = next(size for size in (64, 48, 32, 16) if half_rows % size == 0)
        steps = half_rows // step

        def one(index, carry):
            spot, part = index // steps, lax.rem(index, steps)
            at = pl.ds(pl.multiple_of(rows.start + part * step, 16), step)
            inner = pl.ds(pl.multiple_of(part * step, 16), step)
            total = self.grad[spot, p.core, at, cols].astype(jnp.float32) + self.from_core[spot, at, cols].astype(
                jnp.float32
            )
            for other in others:
                total = total + other[spot, inner, :].astype(jnp.float32)
            self.grad[spot, p.core, at, cols] = total.astype(jnp.bfloat16)
            return carry

        lax.fori_loop(0, self.line * steps, one, 0)

    def to_first(self):
        p = self.place
        self.arrived(0, self.from_core)
        keep = jnp.where(p.core == 0, p.col_half, p.row_half)
        for which in (0, 1):
            rows, cols = self.halves(1 - keep, which)
            self.add(rows, cols, [])
            self.go(1 + which, self.grad.at[:, p.core, rows, cols], self.from_first.at[which], p.in_plane(p.first))

    def to_second(self):
        p = self.place
        for which in (0, 1):
            self.arrived(1 + which, self.from_first.at[which])
        keep = jnp.where(p.core == 0, p.col_half, p.row_half)
        mine = jnp.where(p.core == 0, p.row_half, p.col_half)
        rows, cols = self.halves(keep, 1 - mine)
        self.add(rows, cols, [self.from_first.at[1 - mine]])
        self.go(3, self.grad.at[:, p.core, rows, cols], self.from_second, p.in_plane(p.second))

    def to_line(self):
        p = self.place
        self.arrived(3, self.from_second)
        mine = jnp.where(p.core == 0, p.row_half, p.col_half)
        rows, cols = self.slices(p.row_half, p.col_half)
        self.add(rows, cols, [self.from_first.at[mine], self.from_second])
        for hop in range(1, self.line):
            spot = lax.rem(p.spot + hop, self.line)
            self.go(3 + hop, self.grad.at[spot, p.core, rows, cols], self.from_line.at[hop - 1], p.on_line(hop))

    def to_plane(self):
        p = self.place
        for hop in range(1, self.line):
            self.arrived(3 + hop, self.from_line.at[hop - 1])
        half_rows = self.rows // 2
        rows, cols = self.slices(p.row_half, p.col_half)
        step = 16

        def one(part, carry):
            at = pl.ds(pl.multiple_of(rows.start + part * step, 16), step)
            inner = pl.ds(pl.multiple_of(part * step, 16), step)
            total = self.grad[p.spot, p.core, at, cols].astype(jnp.float32)
            for hop in range(1, self.line):
                total = total + self.from_line[hop - 1, inner, :].astype(jnp.float32)
            self.done[p.row_half, p.col_half, inner, :] = total.astype(jnp.bfloat16)
            return carry

        lax.fori_loop(0, half_rows // step, one, 0)
        own = self.done.at[p.row_half, p.col_half]
        for step in range(1, 4):
            self.go(2 + self.line + step, own, own, p.in_plane(lax.rem(p.dp + step, 4)))

    def finish(self):
        p = self.place
        for step in range(1, 4):
            other = lax.rem(p.dp + 4 - step, 4)
            self.arrived(2 + self.line + step, self.done.at[other // 2, lax.rem(other, 2)])

    def end(self):
        third = 2 + self.line
        landed = {0: self.from_core, 1: self.from_first.at[0], 2: self.from_first.at[0], 3: self.from_second}
        for hop in range(1, self.line):
            landed[3 + hop] = self.from_line.at[0]
        for step in range(1, 4):
            landed[third + step] = self.done.at[0, 0]
        for index, like in landed.items():
            remote(like, like, self.send_sems.at[index], self.recv_sems.at[index], self.place.partner()).wait_send()


class LineFirst(Scatter):
    def __init__(self, place, grad, from_core, from_line, from_plane, done, send_sems, recv_sems):
        self.place, self.grad = place, grad
        self.from_core, self.from_line, self.from_plane, self.done = from_core, from_line, from_plane, done
        self.send_sems, self.recv_sems = send_sems, recv_sems
        self.line, _, self.rows, self.cols = grad.shape

    @staticmethod
    def scratch(line, rows, cols):
        half = (rows // 2, cols // 2)
        return [
            pltpu.VMEM((line, rows, cols), jnp.bfloat16),
            pltpu.VMEM((line - 1, rows, cols), jnp.bfloat16),
            pltpu.VMEM((3,) + half, jnp.bfloat16),
            pltpu.VMEM((2, 2) + half, jnp.bfloat16),
        ]

    def quarter(self, dp):
        rows, cols = self.slices(dp // 2, lax.rem(dp, 2))
        return self.grad.at[self.place.spot, self.place.core, rows, cols]

    def to_first(self):
        p = self.place
        self.arrived(0, self.from_core)
        step = 32
        steps = self.rows // step

        def one(index, carry):
            spot, at = index // steps, pl.ds(pl.multiple_of(lax.rem(index, steps) * step, step), step)
            total = self.grad[spot, p.core, at, :].astype(jnp.float32) + self.from_core[spot, at, :].astype(jnp.float32)
            self.grad[spot, p.core, at, :] = total.astype(jnp.bfloat16)
            return carry

        lax.fori_loop(0, self.line * steps, one, 0)
        for hop in range(1, self.line):
            spot = lax.rem(p.spot + hop, self.line)
            self.go(hop, self.grad.at[spot, p.core], self.from_line.at[hop - 1], p.on_line(hop))

    def to_second(self):
        p = self.place
        for hop in range(1, self.line):
            self.arrived(hop, self.from_line.at[hop - 1])
        step = 32

        def one(part, carry):
            at = pl.ds(pl.multiple_of(part * step, step), step)
            total = self.grad[p.spot, p.core, at, :].astype(jnp.float32)
            for hop in range(1, self.line):
                total = total + self.from_line[hop - 1, at, :].astype(jnp.float32)
            self.grad[p.spot, p.core, at, :] = total.astype(jnp.bfloat16)
            return carry

        lax.fori_loop(0, self.rows // step, one, 0)
        for step in range(1, 4):
            other = lax.rem(p.dp + step, 4)
            self.go(self.line - 1 + step, self.quarter(other), self.from_plane.at[step - 1], p.in_plane(other))

    def to_line(self):
        p = self.place
        for step in range(1, 4):
            self.arrived(self.line - 1 + step, self.from_plane.at[step - 1])
        rows, cols = self.slices(p.row_half, p.col_half)
        size = 16

        def one(part, carry):
            at = pl.ds(pl.multiple_of(rows.start + part * size, 16), size)
            inner = pl.ds(pl.multiple_of(part * size, 16), size)
            total = self.grad[p.spot, p.core, at, cols].astype(jnp.float32)
            for step in range(3):
                total = total + self.from_plane[step, inner, :].astype(jnp.float32)
            self.done[p.row_half, p.col_half, inner, :] = total.astype(jnp.bfloat16)
            return carry

        lax.fori_loop(0, self.rows // 2 // size, one, 0)
        own = self.done.at[p.row_half, p.col_half]
        for step in range(1, 4):
            self.go(2 + self.line + step, own, own, p.in_plane(lax.rem(p.dp + step, 4)))

    def end(self):
        landed = {0: self.from_core}
        for hop in range(1, self.line):
            landed[hop] = self.from_line.at[0]
        for step in range(1, 4):
            landed[self.line - 1 + step] = self.from_plane.at[0]
            landed[2 + self.line + step] = self.done.at[0, 0]
        for index, like in landed.items():
            remote(like, like, self.send_sems.at[index], self.recv_sems.at[index], self.place.partner()).wait_send()


class SmallSum:
    def __init__(self, place, own, from_core, on_line, in_plane, send_sems, recv_sems):
        self.place, self.own, self.from_core, self.on_line, self.in_plane = place, own, from_core, on_line, in_plane
        self.send_sems, self.recv_sems = send_sems, recv_sems
        self.started = []

    @staticmethod
    def sems(line):
        return 1 + (line - 1) + 3

    @staticmethod
    def scratch(line, rows, cols):
        return [
            pltpu.VMEM((rows, cols), jnp.float32),
            pltpu.VMEM((rows, cols), jnp.float32),
            pltpu.VMEM((line, rows, cols), jnp.float32),
            pltpu.VMEM((4, rows, cols), jnp.float32),
        ]

    def go(self, index, src, dst, target):
        copy = remote(src, dst, self.send_sems.at[index], self.recv_sems.at[index], target)
        copy.start()
        self.started.append(copy)

    def arrived(self, index, dst):
        remote(dst, dst, self.send_sems.at[index], self.recv_sems.at[index], self.place.partner()).wait_recv()

    def swap(self):
        self.go(0, self.own, self.from_core, self.place.partner())

    def to_line(self):
        p = self.place
        self.arrived(0, self.from_core)
        self.on_line[p.spot] = self.own[...] + self.from_core[...]
        slot = self.on_line.at[p.spot]
        for hop in range(1, p.line):
            self.go(hop, slot, slot, p.on_line(hop))

    def to_plane(self):
        p = self.place
        for hop in range(1, p.line):
            self.arrived(hop, self.on_line.at[p.source_spot(hop)])
        total = self.on_line[0]
        for spot in range(1, p.line):
            total = total + self.on_line[spot]
        self.in_plane[p.dp] = total
        slot = self.in_plane.at[p.dp]
        for step in range(1, 4):
            self.go(p.line - 1 + step, slot, slot, p.in_plane(lax.rem(p.dp + step, 4)))

    def finish(self, out_ref):
        p = self.place
        for step in range(1, 4):
            self.arrived(p.line - 1 + step, self.in_plane.at[lax.rem(p.dp + 4 - step, 4)])
        out_ref[...] = (self.in_plane[0] + self.in_plane[1]) + (self.in_plane[2] + self.in_plane[3])

    def end(self):
        for copy in self.started:
            copy.wait_send()


class SequenceGather:
    def __init__(self, place, blocks, send_sems, recv_sems):
        self.place, self.blocks = place, blocks
        self.send_sems, self.recv_sems = send_sems, recv_sems
        self.started = []

    @staticmethod
    def sems(line):
        return 3 + (line - 1) + line

    def go(self, index, ref, target):
        remote(ref, ref, self.send_sems.at[index], self.recv_sems.at[index], target).start()
        self.started.append((index, len(ref.shape)))

    def arrived(self, index, dst):
        remote(dst, dst, self.send_sems.at[index], self.recv_sems.at[index], self.place.partner()).wait_recv()

    def begin(self):
        p = self.place
        for step in range(1, 4):
            self.go(step - 1, self.blocks.at[p.shard, p.dp], p.in_plane(lax.rem(p.dp + step, 4)))

    def to_line(self):
        p = self.place
        for step in range(1, 4):
            self.arrived(step - 1, self.blocks.at[p.shard, lax.rem(p.dp + 4 - step, 4)])
        own = self.blocks.at[p.shard]
        for hop in range(1, p.line):
            self.go(2 + hop, own, p.on_line(hop))
        self.go(2 + p.line, own, p.partner())

    def hand(self):
        p = self.place
        for hop in range(1, p.line):
            block = self.blocks.at[2 * p.source_spot(hop) + p.core]
            self.arrived(2 + hop, block)
            self.go(2 + p.line + hop, block, p.partner())

    def ready(self):
        p = self.place
        self.arrived(2 + p.line, self.blocks.at[p.shard + 1 - 2 * p.core])
        for hop in range(1, p.line):
            self.arrived(2 + p.line + hop, self.blocks.at[2 * p.source_spot(hop) + 1 - p.core])

    def end(self):
        for index, rank in self.started:
            like = self.blocks.at[0] if rank == 3 else self.blocks.at[0, 0]
            remote(like, like, self.send_sems.at[index], self.recv_sems.at[index], self.place.partner()).wait_send()
ANY = pl.BlockSpec(memory_space=pl.ANY)
WHOLE = pl.BlockSpec(memory_space=pltpu.VMEM)
SCALARS = pl.BlockSpec(memory_space=pltpu.SMEM)
VMEM_BYTES = 67_043_328
AHEAD = 2
BF16, F32 = jnp.bfloat16, jnp.float32


def nn(left, right):
    return lax.dot_general(left, right, (((1,), (0,)), ((), ())), preferred_element_type=F32)


def nt(left, right):
    return lax.dot_general(left, right, (((1,), (1,)), ((), ())), preferred_element_type=F32)


def tn(left, right):
    return lax.dot_general(left, right, (((0,), (0,)), ((), ())), preferred_element_type=F32)


def lanes(start, size):
    return pl.ds(pl.multiple_of(start, 128), size)


def loop(count, step):
    def one(index, carry):
        step(index)
        return carry

    lax.fori_loop(0, count, one, 0)


def gelu_parts(v):
    spread = 0.5 * (1.0 + lax.erf(v * (1.0 / math.sqrt(2.0))))
    bell = jnp.exp(-0.5 * v * v) * (1.0 / math.sqrt(2.0 * math.pi))
    return v * spread, spread + v * bell


def place_vectors(shard, vectors, class_rows, short, out):
    in_bias, mix_bias, gain_one, shift_one, up_bias, down_bias, gain_two, shift_two, pool_bias = vectors
    short[...] = jnp.zeros(short.shape, F32)
    rows = [in_bias, in_bias, mix_bias, gain_one, shift_one, up_bias, up_bias, up_bias, up_bias]
    rows += [down_bias, gain_two, shift_two, pool_bias]
    for row, vector in enumerate(rows):
        size = vector.shape[0]
        short[row : row + 1, 0:size] = vector[...].astype(F32).reshape(1, size)
    size = class_rows.shape[1]
    short[13 : 13 + class_rows.shape[0], 0:size] = class_rows[...].astype(F32)
    values = short[...].astype(BF16)
    span, width = short.shape[1], out.shape[1]
    lane = lax.broadcasted_iota(jnp.int32, (span, width), 0)
    column = lax.broadcasted_iota(jnp.int32, (span, width), 1)
    row_at = lax.broadcasted_iota(jnp.int32, (16, 1), 0)

    def placed(size):
        per_row = width // size
        spread = jnp.where((column - lax.rem(shard, per_row) * size == lane) & (lane < size), 1.0, 0.0)
        return nn(values, spread.astype(BF16)), shard // per_row

    one_row, _ = placed(mix_bias.shape[0])
    of_in, in_row = placed(in_bias.shape[0])
    of_up, up_row = placed(up_bias.shape[0])
    is_in, is_up = row_at < 2, (row_at >= 5) & (row_at < 9)
    result = jnp.where(is_in, jnp.where(row_at == in_row, of_in, 0.0), one_row)
    result = jnp.where(is_up, jnp.where(row_at == 5 + up_row, of_up, 0.0), result)
    out[...] = result.astype(BF16)


def own_sums(shard, parts, total_ref, out, classes):
    total = total_ref[...]
    width = total.shape[1]
    size = width // parts
    own, own_in, own_up = (jnp.zeros(shape, F32) for shape in ((24, size), (1, 2 * size), (1, 4 * size)))
    for place in range(parts):
        here = shard == place
        own = jnp.where(here, total[:, place * size : (place + 1) * size], own)
        row, at = divmod(2 * size * place, width)
        own_in = jnp.where(here, total[row : row + 1, at : at + 2 * size], own_in)
        row, at = divmod(4 * size * place, width)
        own_up = jnp.where(here, total[5 + row : 6 + row, at : at + 4 * size], own_up)
    out[...] = jnp.zeros(out.shape, F32)
    out[0:24, 0:size] = own
    out[24:25, 0 : 2 * size] = own_in
    out[25:26, 0 : 4 * size] = own_up
    out[26:27, 0:classes] = total[16:17, 13 : 13 + classes]


def layer_kernel(fsdp_size, *refs):
    refs = list(refs)

    def take(count):
        out = refs[:count]
        del refs[:count]
        return out

    lengths, labels, class_bias, tokens_in, cot_in = take(5)
    shards = take(5)
    vectors, class_rows = take(9), take(1)[0]
    layer_out, input_grad, down_out, up_out, mix_out, in_out, pool_out, sums_out = take(8)
    w_in, w_mix, w_up, w_down, w_pool = take(5)
    g_down, g_up = take(2)
    recv = [take(4)] + [take(5) for _ in range(6)]
    recv.append([recv[1][0].at[:, pl.ds(0, shards[0].shape[0]), :]] + take(4))
    sum_refs = take(4)
    (blocks,) = take(1)
    tok, tok_t, cot, att, att_t, first, first_t = take(7)
    qkv, act, slope = take(3)
    unit_one, unit_two, grad = take(3)
    inv_one, inv_two, key_mask, lse, vec = take(5)
    short, small_in, bias_row = take(3)
    g_send, g_recv, s_send, s_recv, q_send, q_recv, v_send, v_recv, b_send, b_recv, local = take(11)
    seq, width = tok.shape
    hidden = act.shape[1]
    pairs = width // 128
    parts = hidden // width
    line = fsdp_size // 2
    rows_of = pl.ds

    loads = [
        pltpu.make_async_copy(tokens_in, tok, local.at[0]),
        pltpu.make_async_copy(cot_in, cot, local.at[1]),
    ]
    for load in loads:
        load.start()
    place = Place(fsdp_size)
    place_vectors(place.shard, vectors, class_rows, short, small_in)
    bias_row[...] = jnp.zeros(bias_row.shape, F32)
    classes = class_bias.shape[0]
    bias_row[0:1, 13 : 13 + classes] = class_bias[...].astype(F32).reshape(1, classes)
    place.meet()
    everything, all_rows = [], shards[0].shape[0]
    for shard, whole in zip(shards, (w_in, w_mix, w_up, w_down, w_pool)):
        for row in range(0, shard.shape[0], all_rows):
            for col in range(0, shard.shape[1], width):
                rows, cols = pl.ds(row, all_rows), pl.ds(col, width)
                everything.append((shard.at[rows, cols], whole.at[:, :, rows, cols]))
    gathers = [Gather(place, *pair, g_send.at[i], g_recv.at[i]) for i, pair in enumerate(everything)]
    little = SmallGather(place, small_in, slope, v_send, v_recv)
    hops = range(1, line)
    first_mix, first_up, first_down, first_pool = 3, 4, 4 + parts, 4 + 2 * parts

    def tick(count):
        if count + AHEAD < len(gathers):
            gathers[count + AHEAD].begin()
        if 0 <= count - 3 < len(gathers):
            for hop in hops:
                gathers[count - 3].hand(hop)
        if count < len(gathers):
            for hop in hops:
                gathers[count].spread(hop)
        if 0 <= count - 1 < len(gathers):
            for hop in hops:
                gathers[count - 1].relay(hop)

    gathers[0].begin()
    little.begin()
    for one in gathers[1:AHEAD]:
        one.begin()
    length = lengths[0]
    label = labels[0]

    for load in loads:
        load.wait()
    tok_t[...] = tok[...].T
    key_at = lax.broadcasted_iota(jnp.int32, (seq, 128), 0)
    key_mask[...] = jnp.where(key_at < length, 0.0, -1e30).astype(F32)

    def mask_cot(index):
        rows = rows_of(pl.multiple_of(index * 128, 128), 128)
        live = (key_mask[rows, :] == 0.0).astype(F32)
        grad[rows, :] = cot[rows, :].astype(F32) * jnp.concatenate([live] * (width // 128), axis=1)

    loop(seq // 128, mask_cot)
    grad_low = cot

    tick(0)
    little.hand()
    tick(1)
    tick(2)
    little.ready()
    vec[...] = jnp.sum(slope[0 : 16 * fsdp_size, 0:width].reshape(fsdp_size, 16, width).astype(F32), axis=0)

    score_scale = 1.0 / math.sqrt(DH)
    for part in range(3):
        tick(3 + part)
        gathers[part].ready()

        def project(index, part=part):
            inner = lanes(index * 256, 256)
            cols = lanes(part * width + index * 256, 256)
            out = nn(tok[...], w_in[:, :, :, cols].reshape(width, 256))
            if part != 1:
                row = 0 if part == 0 else 1
                out = out + vec[row : row + 1, inner]
            out = out.astype(BF16)
            if part == 0:
                out = out * jnp.asarray(score_scale, BF16)
            qkv[:, cols] = out

        loop(width // 256, project)

    low_lanes = lax.broadcasted_iota(jnp.int32, (1, 128), 1) < 64
    zero_low = jnp.zeros((), BF16)

    def head_lanes(value, half):
        return jnp.where(low_lanes if half == 0 else jnp.logical_not(low_lanes), value, zero_low)

    def masked_scores(keys, queries):
        mask = key_mask[...]
        return nt(keys, queries) + jnp.concatenate([mask] * (seq // 128), axis=1)

    def attend(pair):
        queries, keys, values = (qkv[:, lanes(part * width + pair * 128, 128)] for part in range(3))
        values_t = values.T
        mixed = []
        for half in (0, 1):
            scores = masked_scores(keys, head_lanes(queries, half))
            highest = jnp.max(scores, axis=0, keepdims=True)
            raw = jnp.exp(scores - highest)
            total = jnp.sum(raw, axis=0, keepdims=True)
            lse[pair, half : half + 1, :] = highest + jnp.log(total)
            soft = (raw * (1.0 / total)).astype(BF16)
            mixed.append(nn(values_t, soft)[64 * half : 64 * half + 64, :])
        both = jnp.concatenate(mixed, axis=0)
        att_t[rows_of(pl.multiple_of(pair * 128, 128), 128), :] = both.astype(BF16)
        att[:, lanes(pair * 128, 128)] = both.T.astype(BF16)

    def attend_on(pair):
        attend(pair)
        for one in range(pairs):

            @pl.when(pair == one)
            def _(one=one):
                tick(6 + one)

    loop(pairs, attend_on)
    gathers[first_mix].ready()

    little.end()

    gain_one, shift_one = vec[3:4, :], vec[4:5, :]

    def mean_of(value):
        return jnp.sum(value, axis=1, keepdims=True) * (1.0 / width)

    def norm_one(index):
        rows = rows_of(pl.multiple_of(index * 256, 256), 256)
        total = nn(att[rows, :], w_mix[...].reshape(width, width)) + vec[2:3, :] + tok[rows, :].astype(F32)
        centered = total - mean_of(total)
        inverse = lax.rsqrt(mean_of(centered * centered) + EPSILON)
        unit = centered * inverse
        unit_one[rows, :] = unit
        inv_one[rows, :] = jnp.broadcast_to(inverse, (256, 128))
        first[rows, :] = (unit * gain_one + shift_one).astype(BF16)

    loop(seq // 256, norm_one)
    first_t[...] = first[...].T
    tick(6 + pairs)

    for part in range(parts):
        gathers[first_up + part].ready()

        def raise_up(index, part=part):
            inner = lanes(index * 384, 384)
            cols = lanes(part * width + index * 384, 384)
            pre = nn(first[...], w_up[:, :, :, cols].reshape(width, 384)) + vec[5 + part : 6 + part, inner]
            value, derivative = gelu_parts(pre)
            act[:, cols] = value.astype(BF16)
            slope[:, cols] = derivative.astype(BF16)

        loop(width // 384, raise_up)
        if part < 3:
            tick(7 + pairs + part)
    for one in gathers[first_down:first_pool]:
        one.ready()
    gain_two, shift_two = vec[10:11, :], vec[11:12, :]

    def norm_two(index):
        rows = rows_of(pl.multiple_of(index * 256, 256), 256)
        total = nn(act[rows, :], w_down[...].reshape(hidden, width)) + vec[9:10, :]
        total = total + (unit_one[rows, :] * gain_one + shift_one)
        centered = total - mean_of(total)
        inverse = lax.rsqrt(mean_of(centered * centered) + EPSILON)
        unit = centered * inverse
        unit_two[rows, :] = unit
        inv_two[rows, :] = jnp.broadcast_to(inverse, (256, 128))
        att[rows, :] = (unit * gain_two + shift_two).astype(BF16)

    loop(seq // 256, norm_two)
    stores = [pltpu.make_async_copy(att, layer_out, local.at[2])]
    stores[0].start()

    gathers[first_pool].ready()
    top = lax.broadcasted_iota(jnp.int32, (16, 1), 0) == 0
    head = att[0:16, :]
    vec_low = vec[...].astype(BF16)
    pooled = jnp.tanh(nn(head, w_pool[...].reshape(width, width)) + vec[12:13, :])
    pooled_low = pooled.astype(BF16)
    logits = nt(pooled_low, vec_low) + bias_row[0:1, 0:16]
    class_at = lax.broadcasted_iota(jnp.int32, (16, 16), 1) - 13
    logits = jnp.where(class_at >= 0, logits, -1e30)
    raised = jnp.exp(logits - jnp.max(logits, axis=1, keepdims=True))
    soft_logits = raised / jnp.sum(raised, axis=1, keepdims=True)
    onehot = (class_at == label).astype(F32)
    grad_logits = jnp.where(top, soft_logits - onehot, 0.0).astype(BF16)
    sums = sum_refs[0]
    sums[0:16, :] = tn(grad_logits, pooled_low)
    sums[16:24, :] = jnp.zeros((8, width), F32)
    sums[16:17, 0:16] = grad_logits[0:1, :].astype(F32)
    grad_pool_pre = (nn(grad_logits, vec_low) * (1.0 - pooled * pooled)).astype(BF16)
    sums[12:13, :] = grad_pool_pre[0:1, :].astype(F32)
    block = jnp.where(top, head.astype(F32), 0.0)
    second_row = lax.broadcasted_iota(jnp.int32, (16, 1), 0) == 1
    block = jnp.where(second_row, jnp.broadcast_to(grad_pool_pre[0:1, :].astype(F32), (16, width)), block)
    blocks[place.shard, place.dp] = block.astype(BF16)
    sequences = SequenceGather(place, blocks, q_send, q_recv)
    sequences.begin()
    grad[0:16, :] += nt(grad_pool_pre, w_pool[...].reshape(width, width))

    def norm_back(unit_ref, inv_ref, gain, gain_row, shift_row, bias_row, size):
        def one(index, carry):
            by_gain, by_shift, by_bias = carry
            rows = rows_of(pl.multiple_of(index * size, size), size)
            incoming = grad[rows, :]
            unit = unit_ref[rows, :]
            scaled = incoming * gain
            inverse = jnp.concatenate([inv_ref[rows, :]] * (width // 128), axis=1)
            back = inverse * (scaled - mean_of(scaled) - unit * mean_of(scaled * unit))
            low = back.astype(BF16)
            grad[rows, :] = back
            grad_low[rows, :] = low
            return (
                by_gain + jnp.sum(incoming * unit, axis=0, keepdims=True),
                by_shift + jnp.sum(incoming, axis=0, keepdims=True),
                by_bias + jnp.sum(low.astype(F32), axis=0, keepdims=True),
            )

        zero = jnp.zeros((1, width), F32)
        by_gain, by_shift, by_bias = lax.fori_loop(0, seq // size, one, (zero, zero, zero))
        sums[gain_row : gain_row + 1, :] = by_gain
        sums[shift_row : shift_row + 1, :] = by_shift
        sums[bias_row : bias_row + 1, :] = by_bias

    norm_back(unit_two, inv_two, gain_two, 10, 11, 9, 128)

    rows_down = hidden // fsdp_size
    few = 128
    many = rows_down - few
    pieces = [g_down.at[:, :, pl.ds(many, few), :], g_down.at[:, :, pl.ds(0, many), :]]
    pieces += [g_up.at[:, :, :, pl.ds(half * 2 * width, 2 * width)] for half in (0, 1)]
    pieces += [w_up.at[:, :, :, pl.ds(at * width, width)] for at in (3, 0, 1, 2)]
    scatters = [
        (LineFirst if i == 0 else Scatter)(place, ref, *recv[i], s_send.at[i], s_recv.at[i])
        for i, ref in enumerate(pieces)
    ]
    down_a, down_b, up_a, up_b, of_mix, in_a, in_b, in_c = scatters

    for first_row, count, one in ((many, few, down_a), (0, many, down_b)):

        def down_gradient(index, first_row=first_row, count=count):
            cols = lanes(index * rows_down + first_row, count)
            out = tn(act[:, cols], grad_low[...]).astype(BF16)
            g_down[index // 2, lax.rem(index, 2), pl.ds(first_row, count), :] = out

        loop(fsdp_size, down_gradient)
        one.swap()
    sequences.to_line()

    for part in range(parts):

        def through_down(index, part=part):
            owner = part * 2 + index
            inner = lanes(index * rows_down, rows_down)
            cols = lanes(owner * rows_down, rows_down)
            low = (nt(grad_low[...], w_down[part, index]) * slope[:, cols].astype(F32)).astype(BF16)
            slope[:, cols] = low
            sums[5 + part : 6 + part, inner] = jnp.sum(low.astype(F32), axis=0, keepdims=True)

        loop(2, through_down)

        def up_gradient(index, part=part):
            cols = lanes(part * width + index * 256, 256)
            out = nn(first_t[...], slope[:, cols]).astype(BF16)
            g_up[:, :, :, cols] = out.reshape(line, 2, width // fsdp_size, 256)

        loop(width // 256, up_gradient)
        if part == 0:
            down_a.to_first()
        if part == 1:
            up_a.swap()
            down_b.to_first()
        if part == 2:
            up_a.to_first()
        if part == 3:
            up_b.swap()
            down_b.to_second()
            sequences.hand()

    half_line = line // 2
    half_width = width // 2

    def through_up(index):
        cols = lanes(index * half_width, half_width)
        weight = w_up[rows_of(index * half_line, half_line)].reshape(half_width, hidden)
        grad[:, cols] += nt(slope[...], weight)
        for one in (0, 1):

            @pl.when(index == one)
            def _(one=one):
                if one == 0:
                    up_b.to_first()
                    down_b.to_line()
                else:
                    up_a.to_second()
                    down_a.to_second()

    loop(2, through_up)
    norm_back(unit_one, inv_one, gain_one, 3, 4, 2, 128)
    for one in gathers:
        one.end()

    def mix_gradient(index):
        out = nn(att_t[...], grad_low[:, lanes(index * 256, 256)]).astype(BF16)
        w_up[:, :, :, lanes(3 * width + index * 256, 256)] = out.reshape(line, 2, width // fsdp_size, 256)

    loop(width // 256, mix_gradient)
    of_mix.swap()
    up_b.to_second()

    def through_mix(index):
        cols = lanes(index * half_width, half_width)
        weight = w_mix[rows_of(index * half_line, half_line)].reshape(half_width, width)
        first[:, cols] = nt(grad_low[...], weight).astype(BF16)

    loop(2, through_mix)
    of_mix.to_first()
    up_a.to_line()

    def attend_back(pair):
        at = [lanes(part * width + pair * 128, 128) for part in range(3)]
        queries, keys, values = (qkv[:, cols] for cols in at)
        rows = rows_of(pl.multiple_of(pair * 128, 128), 128)
        out_grad = first[:, lanes(pair * 128, 128)]
        keys_t = keys.T
        products = out_grad.astype(F32).T * att_t[rows, :].astype(F32)
        by_query, by_key, by_value = [], None, None
        for half in (0, 1):
            own_queries, own_grad = head_lanes(queries, half), head_lanes(out_grad, half)
            soft = jnp.exp(masked_scores(keys, own_queries) - lse[pair, half : half + 1, :])
            row_sum = jnp.sum(products[64 * half : 64 * half + 64, :], axis=0, keepdims=True)
            score_grad = (soft * (nt(values, own_grad) - row_sum)).astype(BF16)
            value_part = nn(soft.astype(BF16), own_grad)
            key_part = nn(score_grad, own_queries)
            by_value = value_part if by_value is None else by_value + value_part
            by_key = key_part if by_key is None else by_key + key_part
            by_query.append(nn(keys_t, score_grad)[64 * half : 64 * half + 64, :])
        qkv[:, at[0]] = (jnp.concatenate(by_query, axis=0).T * score_scale).astype(BF16)
        qkv[:, at[1]] = by_key.astype(BF16)
        qkv[:, at[2]] = by_value.astype(BF16)

    after_pair = {
        0: [down_b.to_plane, down_a.to_line],
        1: [up_b.to_line, of_mix.to_second],
        2: [in_a.to_first, up_a.to_plane],
        3: [of_mix.to_line, in_a.to_second],
        4: [in_b.to_first, up_b.to_plane],
        5: [in_a.to_line, of_mix.to_plane, in_b.to_second],
    }

    def attend_back_on(pair):
        attend_back(pair)
        for one in range(pairs):

            @pl.when(pair == one)
            def _(one=one):
                for step in after_pair[one]:
                    step()

    def in_gradient(chunk):
        for part in range(3):
            inner = lanes(chunk * 256, 256)
            incoming = qkv[:, lanes(part * width + chunk * 256, 256)]
            out = nn(tok_t[...], incoming).astype(BF16).reshape(line, 2, width // fsdp_size, 256)
            w_up[:, :, :, lanes(chunk * width + part * 256, 256)] = out
            if part != 1:
                row = 0 if part == 0 else 1
                sums[row : row + 1, inner] = jnp.sum(incoming.astype(F32), axis=0, keepdims=True)

    def attend_chunk(chunk):
        lax.fori_loop(2 * chunk, 2 * chunk + 2, lambda pair, carry: (attend_back_on(pair), carry)[1], 0)
        in_gradient(chunk)
        for at, one in enumerate((in_a, in_b, in_c)):

            @pl.when(chunk == at)
            def _(one=one):
                one.swap()

    loop(pairs // 2, attend_chunk)
    sequences.ready()
    total = SmallSum(place, *sum_refs, b_send, b_recv)
    total.swap()

    def through_in(index):
        cols = lanes(index * half_width, half_width)
        weight = w_in[rows_of(index * half_line, half_line)].reshape(half_width, 3 * width)
        grad[:, cols] += nt(qkv[...], weight)
        for one in (0, 1):

            @pl.when(index == one)
            def _(one=one):
                if one == 0:
                    in_c.to_first()
                    in_b.to_line()
                else:
                    in_a.to_plane()

    loop(2, through_in)
    store = pltpu.make_async_copy(grad, input_grad, local.at[3])
    store.start()
    stores.append(store)
    in_c.to_second()
    total.to_line()
    in_b.to_plane()

    every = blocks[...].reshape(fsdp_size * 4 * 16, width)
    count = fsdp_size * 4 * 16
    row_at = lax.broadcasted_iota(jnp.int32, (count, count), 0)
    col_at = lax.broadcasted_iota(jnp.int32, (count, count), 1)
    shift = jnp.where((lax.rem(row_at, 16) == 0) & (col_at == row_at + 1), 1.0, 0.0).astype(BF16)
    paired = nn(shift, every).astype(BF16)
    own_rows_at = lax.broadcasted_iota(jnp.int32, (128, width), 0) + place.shard * (width // fsdp_size)
    pick = jnp.where(own_rows_at == lax.broadcasted_iota(jnp.int32, (128, width), 1), 1.0, 0.0).astype(BF16)
    own_part = nt(pick, every).astype(BF16)
    pool_out[...] = nn(own_part, paired)[0 : width // fsdp_size, :]

    in_c.to_line()
    total.to_plane()

    wide = 256
    kept = [
        (down_a, down_out, many, [(0, 0, width)]),
        (down_b, down_out, 0, [(0, 0, width)]),
        (up_a, up_out, 0, [(0, 0, 2 * width)]),
        (up_b, up_out, 0, [(0, 2 * width, 2 * width)]),
        (of_mix, mix_out, 0, [(0, 0, width)]),
    ]
    for chunk, one in enumerate((in_a, in_b, in_c)):
        kept.append((one, in_out, 0, [(part * wide, part * width + chunk * wide, wide) for part in range(3)]))

    def keep(one, out, first_row, spans):
        one.finish()
        half_rows, half_cols = one.rows // 2, one.cols // 2
        for row_half in (0, 1):
            rows = pl.ds(first_row + row_half * half_rows, half_rows)
            for col_half in (0, 1):
                begin, end = col_half * half_cols, (col_half + 1) * half_cols
                for here, there, count in spans:
                    low, high = max(here, begin), min(here + count, end)
                    if low < high:
                        source = one.done.at[row_half, col_half, :, pl.ds(low - begin, high - low)]
                        target = out.at[rows, pl.ds(there + low - here, high - low)]
                        store = pltpu.make_async_copy(source, target, local.at[len(stores) + 2])
                        store.start()
                        stores.append(store)

    for item in kept[:-1]:
        keep(*item)
    total.finish(total.from_core)
    own_sums(place.shard, fsdp_size, total.from_core, sums_out, classes)
    in_c.to_plane()
    keep(*kept[-1])
    for store in stores:
        store.wait()
    for one in scatters + [sequences, total]:
        one.end()


def run_layer(fsdp_size, lengths, labels, class_bias, tokens, cotangent, shards, vectors, class_rows):
    line = fsdp_size // 2
    seq, width = tokens.shape
    in_shard, mix_shard, up_shard, down_shard, pool_shard = shards
    hidden = up_shard.shape[1]
    vmem, dma = pltpu.VMEM, pltpu.SemaphoreType.DMA
    reduced = (down_shard, up_shard, mix_shard, in_shard)
    block = width // fsdp_size
    few = 128
    sizes = [(few, width), (down_shard.shape[0] - few, width)] + [(block, 2 * width)] * 2 + [(block, width)] * 4
    scratch = [vmem((line, 2) + s.shape, BF16) for s in shards]
    scratch += [vmem((line, 2) + s.shape, BF16) for s in (down_shard, up_shard)]
    for i, size in enumerate(sizes):
        scratch += (LineFirst if i == 0 else Scatter).scratch(line, *size)
    del scratch[-5]
    scratch += SmallSum.scratch(line, 24, width)
    scratch += [vmem((fsdp_size, 4, 16, width), BF16)]
    rows, turned = vmem((seq, width), BF16), vmem((width, seq), BF16)
    scratch += [rows, turned, rows, rows, turned, rows, turned]
    scratch += [vmem((seq, 3 * width), BF16), vmem((seq, hidden), BF16), vmem((seq, hidden), BF16)]
    scratch += [vmem((seq, width), F32)] * 3
    scratch += [vmem((seq, 128), F32)] * 3 + [vmem((width // 128, 8, seq), F32), vmem((16, width), F32)]
    span = hidden // fsdp_size
    scratch += [vmem((16, span), F32), vmem((16, width), BF16), vmem((8, 128), F32)]
    for count in (
        (sum(s.shape[0] * s.shape[1] for s in shards) // (block * width), Gather.sems(line)),
        (len(sizes), Scatter.sems(line)),
        (SequenceGather.sems(line),),
        (SmallGather.sems(line),),
        (SmallSum.sems(line),),
    ):
        scratch += [dma(count), dma(count)]
    scratch += [dma((64,))]
    out_shape = [jax.ShapeDtypeStruct((seq, width), BF16), jax.ShapeDtypeStruct((seq, width), F32)]
    out_shape += [jax.ShapeDtypeStruct(s.shape, BF16) for s in reduced]
    out_shape += [jax.ShapeDtypeStruct((width // fsdp_size, width), F32), jax.ShapeDtypeStruct((32, span), F32)]
    return pl.pallas_call(
        functools.partial(layer_kernel, fsdp_size),
        out_shape=out_shape,
        in_specs=[SCALARS, SCALARS, WHOLE] + [ANY] * 7 + [WHOLE] * 10,
        out_specs=[ANY] * 6 + [WHOLE] * 2,
        scratch_shapes=scratch,
        compiler_params=pltpu.CompilerParams(collective_id=0, has_side_effects=True, vmem_limit_bytes=VMEM_BYTES),
        name="layer",
    )(lengths, labels, class_bias, tokens, cotangent, *shards, *vectors, class_rows)


def outputs_kernel(as_is, rounded, sizes, classes, size, *refs):
    count = as_is + rounded
    inputs, sums = refs[:count], refs[count]
    refs = refs[count + 1 :]
    outs, small = refs[:count], refs[count : count + len(sizes) + 2]
    refs = refs[count + len(sizes) + 2 :]
    held, wide, (load_sems, store_sems) = refs[:count], refs[count : count + rounded], refs[count + rounded :]
    order = list(range(as_is, count)) + list(range(as_is))
    loads = {i: pltpu.make_async_copy(inputs[i], held[i], load_sems.at[i]) for i in order}
    for load in loads.values():
        load.start()
    for (row, length), out in zip(sizes.items(), small):
        out[...] = sums[row : row + 1, 0:length].reshape(length)
    small[-2][...] = sums[13 : 13 + classes, 0:size]
    small[-1][...] = sums[26:27, 0:classes].reshape(classes)
    stores = []
    for i in order:
        loads[i].wait()
        source = held[i]
        if i >= as_is:
            source = wide[i - as_is]
            step = 32

            def widen(index, narrow=held[i], source=source):
                rows = pl.ds(pl.multiple_of(index * step, step), step)
                source[rows, :] = narrow[rows, :].astype(F32)

            loop(source.shape[0] // step, widen)
        stores.append(pltpu.make_async_copy(source, outs[i], store_sems.at[i]))
        stores[-1].start()
    for store in stores:
        store.wait()


def run_outputs(as_is, rounded, sums, sizes, classes, size):
    arrays = as_is + rounded
    out_shape = [jax.ShapeDtypeStruct(a.shape, a.dtype) for a in as_is]
    out_shape += [jax.ShapeDtypeStruct(a.shape, F32) for a in rounded]
    out_shape += [jax.ShapeDtypeStruct((length,), F32) for length in sizes.values()]
    out_shape += [jax.ShapeDtypeStruct((classes, size), F32), jax.ShapeDtypeStruct((classes,), F32)]
    scratch = [pltpu.VMEM(a.shape, a.dtype) for a in arrays] + [pltpu.VMEM(a.shape, F32) for a in rounded]
    scratch += [pltpu.SemaphoreType.DMA((len(arrays),))] * 2
    return pl.pallas_call(
        functools.partial(outputs_kernel, len(as_is), len(rounded), sizes, classes, size),
        out_shape=out_shape,
        in_specs=[ANY] * len(arrays) + [WHOLE],
        out_specs=[ANY] * len(arrays) + [WHOLE] * (len(sizes) + 2),
        scratch_shapes=scratch,
        compiler_params=pltpu.CompilerParams(vmem_limit_bytes=VMEM_BYTES),
        name="outputs",
    )(*arrays, sums)


def kernel_body(
    fsdp_size,
    tokens,
    in_weight,
    in_bias,
    mix_weight,
    mix_bias,
    first_gain,
    first_shift,
    up_weight,
    up_bias,
    down_weight,
    down_bias,
    second_gain,
    second_shift,
    pool_weight,
    pool_bias,
    class_weight,
    class_bias,
    lengths,
    labels,
    cotangent,
):
    layer_out, input_grad, down_grad, up_grad, mix_grad, in_grad, pool_grad, sums = run_layer(
        fsdp_size,
        lengths,
        labels,
        class_bias,
        tokens,
        cotangent,
        (in_weight, mix_weight, up_weight, down_weight, pool_weight),
        (in_bias, mix_bias, first_gain, first_shift, up_bias, down_bias, second_gain, second_shift, pool_bias),
        class_weight.T,
    )
    size = mix_bias.shape[0]
    sizes = {24: 2 * size, 2: size, 3: size, 4: size, 25: 4 * size, 9: size, 10: size, 11: size, 12: size}
    outs = run_outputs(
        (layer_out, input_grad, pool_grad),
        (in_grad, mix_grad, up_grad, down_grad),
        sums,
        sizes,
        class_bias.shape[0],
        size,
    )
    layer_out, input_grad, pool_grad, in_grad, mix_grad, up_grad, down_grad = outs[:7]
    of_in, of_mix, of_gain_one, of_shift_one, of_up, of_down, of_gain_two, of_shift_two, of_pool = outs[7:16]
    class_grad, class_bias_grad = outs[16:]
    return (
        layer_out,
        input_grad,
        in_grad,
        of_in,
        mix_grad,
        of_mix,
        of_gain_one,
        of_shift_one,
        up_grad,
        of_up,
        down_grad,
        of_down,
        of_gain_two,
        of_shift_two,
        pool_grad,
        of_pool,
        class_grad.T,
        class_bias_grad,
    )


def plain_body(
    tokens,
    in_weight,
    in_bias,
    mix_weight,
    mix_bias,
    first_gain,
    first_shift,
    up_weight,
    up_bias,
    down_weight,
    down_bias,
    second_gain,
    second_shift,
    pool_weight,
    pool_bias,
    class_weight,
    class_bias,
    lengths,
    labels,
    cotangent,
):
    gathered = (
        lax.all_gather(in_weight, "fsdp", axis=0, tiled=True),
        lax.all_gather(in_bias, "fsdp", axis=0, tiled=True),
        lax.all_gather(mix_weight, "fsdp", axis=0, tiled=True),
        lax.all_gather(mix_bias, "fsdp", axis=0, tiled=True),
        lax.all_gather(first_gain, "fsdp", axis=0, tiled=True),
        lax.all_gather(first_shift, "fsdp", axis=0, tiled=True),
        lax.all_gather(up_weight, "fsdp", axis=0, tiled=True),
        lax.all_gather(up_bias, "fsdp", axis=0, tiled=True),
        lax.all_gather(down_weight, "fsdp", axis=0, tiled=True),
        lax.all_gather(down_bias, "fsdp", axis=0, tiled=True),
        lax.all_gather(second_gain, "fsdp", axis=0, tiled=True),
        lax.all_gather(second_shift, "fsdp", axis=0, tiled=True),
        lax.all_gather(pool_weight, "fsdp", axis=0, tiled=True),
        lax.all_gather(pool_bias, "fsdp", axis=0, tiled=True),
        lax.all_gather(class_weight, "fsdp", axis=0, tiled=True),
    )
    (
        whole_in,
        bias_in,
        whole_mix,
        bias_mix,
        gain_one,
        shift_one,
        whole_up,
        bias_up,
        whole_down,
        bias_down,
        gain_two,
        shift_two,
        whole_pool,
        bias_pool,
        whole_class,
    ) = gathered
    token_rows = tokens.shape[0]
    seq_count = lengths.shape[0]
    seq_len = token_rows // seq_count
    model_width = whole_mix.shape[0]
    score_scale = 1.0 / math.sqrt(DH)
    positions = jnp.arange(seq_len)
    projected = jnp.dot(tokens, whole_in, preferred_element_type=jnp.float32)
    in_bias_f = bias_in.astype(jnp.float32)
    head_shape = (seq_count, seq_len, H, DH)
    queries = (
        (projected[:, :model_width] + in_bias_f[:model_width])
        .astype(jnp.bfloat16)
        .reshape(head_shape)
    )
    keys_all = projected[:, model_width : 2 * model_width].astype(jnp.bfloat16).reshape(head_shape)
    values_all = (
        (projected[:, 2 * model_width :] + in_bias_f[model_width:])
        .astype(jnp.bfloat16)
        .reshape(head_shape)
    )

    def scores_of(query_blk, key_blk, length):
        raw_scores = (
            jnp.einsum("qhd,khd->hqk", query_blk, key_blk, preferred_element_type=jnp.float32)
            * score_scale
        )
        return jnp.where(positions[None, None, :] < length, raw_scores, -1e30)

    def attend_fore(block_items):
        query_blk, key_blk, value_blk, length = block_items
        scores = scores_of(query_blk, key_blk, length)
        highest = jnp.max(scores, axis=-1, keepdims=True)
        raw_weights = jnp.exp(scores - highest)
        totals = jnp.sum(raw_weights, axis=-1, keepdims=True)
        softmaxed = (raw_weights / totals).astype(jnp.bfloat16)
        mixed_values = jnp.einsum(
            "hqk,khd->qhd", softmaxed, value_blk, preferred_element_type=jnp.float32
        )
        return (mixed_values, (highest + jnp.log(totals))[..., 0])

    attended, logsum = lax.map(attend_fore, (queries, keys_all, values_all, lengths))
    attn_low = attended.reshape(token_rows, model_width).astype(jnp.bfloat16)
    branch = jnp.dot(attn_low, whole_mix, preferred_element_type=jnp.float32) + bias_mix.astype(
        jnp.float32
    )
    first_norm, unit_one, inverse_one = norm_fore(
        tokens.astype(jnp.float32) + branch,
        gain_one.astype(jnp.float32),
        shift_one.astype(jnp.float32),
    )
    first_low = first_norm.astype(jnp.bfloat16)
    pre_act = jnp.dot(first_low, whole_up, preferred_element_type=jnp.float32) + bias_up.astype(
        jnp.float32
    )
    activated, gelu_pull = jax.vjp(partial(jax.nn.gelu, approximate=False), pre_act)
    act_low = activated.astype(jnp.bfloat16)
    ffn_out = jnp.dot(act_low, whole_down, preferred_element_type=jnp.float32) + bias_down.astype(
        jnp.float32
    )
    result, unit_two, inverse_two = norm_fore(
        first_norm + ffn_out, gain_two.astype(jnp.float32), shift_two.astype(jnp.float32)
    )
    head_rows = result.reshape(seq_count, seq_len, model_width)[:, 0, :].astype(jnp.bfloat16)
    pooled = jnp.tanh(
        jnp.dot(head_rows, whole_pool, preferred_element_type=jnp.float32)
        + bias_pool.astype(jnp.float32)
    )
    pooled_low = pooled.astype(jnp.bfloat16)
    logits = jnp.dot(
        pooled_low, whole_class, preferred_element_type=jnp.float32
    ) + class_bias.astype(jnp.float32)
    back_in, back_mix, back_gain_one, back_up, back_down, back_gain_two, back_pool, back_class = (
        lax.all_gather(in_weight, "fsdp", axis=0, tiled=True),
        lax.all_gather(mix_weight, "fsdp", axis=0, tiled=True),
        lax.all_gather(first_gain, "fsdp", axis=0, tiled=True),
        lax.all_gather(up_weight, "fsdp", axis=0, tiled=True),
        lax.all_gather(down_weight, "fsdp", axis=0, tiled=True),
        lax.all_gather(second_gain, "fsdp", axis=0, tiled=True),
        lax.all_gather(pool_weight, "fsdp", axis=0, tiled=True),
        lax.all_gather(class_weight, "fsdp", axis=0, tiled=True),
    )
    onehot = (labels[:, None] == jnp.arange(logits.shape[1])[None, :]).astype(jnp.float32)
    grad_logits = (jax.nn.softmax(logits, axis=-1) - onehot).astype(jnp.bfloat16)
    grad_class_weight = jnp.dot(pooled_low.T, grad_logits, preferred_element_type=jnp.float32)
    grad_class_bias = column_sums(grad_logits)
    grad_pool_pre = (
        jnp.dot(grad_logits, back_class.T, preferred_element_type=jnp.float32)
        * (1.0 - pooled * pooled)
    ).astype(jnp.bfloat16)
    grad_pool_weight = jnp.dot(head_rows.T, grad_pool_pre, preferred_element_type=jnp.float32)
    grad_pool_bias = column_sums(grad_pool_pre)
    grad_head_rows = jnp.dot(grad_pool_pre, back_pool.T, preferred_element_type=jnp.float32)
    live_mask = (positions[None, :] < lengths[:, None]).astype(jnp.float32)
    grad_result = (
        cotangent.astype(jnp.float32).reshape(seq_count, seq_len, model_width)
        * live_mask[:, :, None]
    )
    grad_result = grad_result.at[:, 0, :].add(grad_head_rows).reshape(token_rows, model_width)
    grad_sum_two, grad_second_gain, grad_second_shift = norm_back(
        grad_result, unit_two, inverse_two, back_gain_two.astype(jnp.float32)
    )
    grad_ffn = grad_sum_two.astype(jnp.bfloat16)
    grad_down_weight = jnp.dot(act_low.T, grad_ffn, preferred_element_type=jnp.float32)
    grad_down_bias = column_sums(grad_ffn)
    grad_pre = gelu_pull(jnp.dot(grad_ffn, back_down.T, preferred_element_type=jnp.float32))[
        0
    ].astype(jnp.bfloat16)
    grad_up_weight = jnp.dot(first_low.T, grad_pre, preferred_element_type=jnp.float32)
    grad_up_bias = column_sums(grad_pre)
    grad_first_norm = grad_sum_two + jnp.dot(
        grad_pre, back_up.T, preferred_element_type=jnp.float32
    )
    grad_sum_one, grad_first_gain, grad_first_shift = norm_back(
        grad_first_norm, unit_one, inverse_one, back_gain_one.astype(jnp.float32)
    )
    grad_branch = grad_sum_one.astype(jnp.bfloat16)
    grad_mix_weight = jnp.dot(attn_low.T, grad_branch, preferred_element_type=jnp.float32)
    grad_mix_bias = column_sums(grad_branch)
    grad_attended = (
        jnp.dot(grad_branch, back_mix.T, preferred_element_type=jnp.float32)
        .astype(jnp.bfloat16)
        .reshape(head_shape)
    )

    def attend_back(block_items):
        query_blk, key_blk, value_blk, length, lse_blk, grad_blk = block_items
        softmaxed = jnp.exp(scores_of(query_blk, key_blk, length) - lse_blk[..., None])
        grad_value = jnp.einsum(
            "hqk,qhd->khd",
            softmaxed.astype(jnp.bfloat16),
            grad_blk,
            preferred_element_type=jnp.float32,
        )
        grad_soft = jnp.einsum(
            "qhd,khd->hqk", grad_blk, value_blk, preferred_element_type=jnp.float32
        )
        grad_scores = (
            softmaxed * (grad_soft - jnp.sum(softmaxed * grad_soft, axis=-1, keepdims=True))
        ).astype(jnp.bfloat16)
        grad_query = (
            jnp.einsum("hqk,khd->qhd", grad_scores, key_blk, preferred_element_type=jnp.float32)
            * score_scale
        )
        grad_key = (
            jnp.einsum("hqk,qhd->khd", grad_scores, query_blk, preferred_element_type=jnp.float32)
            * score_scale
        )
        return (grad_query, grad_key, grad_value)

    grad_queries, grad_keys, grad_values = lax.map(
        attend_back, (queries, keys_all, values_all, lengths, logsum, grad_attended)
    )
    grad_proj = jnp.concatenate(
        [
            grad_queries.reshape(token_rows, model_width),
            grad_keys.reshape(token_rows, model_width),
            grad_values.reshape(token_rows, model_width),
        ],
        axis=1,
    ).astype(jnp.bfloat16)
    grad_in_weight = jnp.dot(tokens.T, grad_proj, preferred_element_type=jnp.float32)
    proj_sums = column_sums(grad_proj)
    grad_in_bias = jnp.concatenate([proj_sums[:model_width], proj_sums[2 * model_width :]])
    input_grad = grad_sum_one + jnp.dot(grad_proj, back_in.T, preferred_element_type=jnp.float32)
    gradients = (
        grad_in_weight,
        grad_in_bias,
        grad_mix_weight,
        grad_mix_bias,
        grad_first_gain,
        grad_first_shift,
        grad_up_weight,
        grad_up_bias,
        grad_down_weight,
        grad_down_bias,
        grad_second_gain,
        grad_second_shift,
        grad_pool_weight,
        grad_pool_bias,
        grad_class_weight,
    )
    shard_sums = (
        lax.psum_scatter(gradients[0], "fsdp", scatter_dimension=0, tiled=True),
        lax.psum_scatter(gradients[1], "fsdp", scatter_dimension=0, tiled=True),
        lax.psum_scatter(gradients[2], "fsdp", scatter_dimension=0, tiled=True),
        lax.psum_scatter(gradients[3], "fsdp", scatter_dimension=0, tiled=True),
        lax.psum_scatter(gradients[4], "fsdp", scatter_dimension=0, tiled=True),
        lax.psum_scatter(gradients[5], "fsdp", scatter_dimension=0, tiled=True),
        lax.psum_scatter(gradients[6], "fsdp", scatter_dimension=0, tiled=True),
        lax.psum_scatter(gradients[7], "fsdp", scatter_dimension=0, tiled=True),
        lax.psum_scatter(gradients[8], "fsdp", scatter_dimension=0, tiled=True),
        lax.psum_scatter(gradients[9], "fsdp", scatter_dimension=0, tiled=True),
        lax.psum_scatter(gradients[10], "fsdp", scatter_dimension=0, tiled=True),
        lax.psum_scatter(gradients[11], "fsdp", scatter_dimension=0, tiled=True),
        lax.psum_scatter(gradients[12], "fsdp", scatter_dimension=0, tiled=True),
        lax.psum_scatter(gradients[13], "fsdp", scatter_dimension=0, tiled=True),
        lax.psum_scatter(gradients[14], "fsdp", scatter_dimension=0, tiled=True),
    )
    summed = (
        lax.psum(shard_sums[0].astype(jnp.bfloat16), "dp").astype(jnp.float32),
        lax.psum(shard_sums[1].astype(jnp.bfloat16), "dp").astype(jnp.float32),
        lax.psum(shard_sums[2].astype(jnp.bfloat16), "dp").astype(jnp.float32),
        lax.psum(shard_sums[3].astype(jnp.bfloat16), "dp").astype(jnp.float32),
        lax.psum(shard_sums[4].astype(jnp.bfloat16), "dp").astype(jnp.float32),
        lax.psum(shard_sums[5].astype(jnp.bfloat16), "dp").astype(jnp.float32),
        lax.psum(shard_sums[6].astype(jnp.bfloat16), "dp").astype(jnp.float32),
        lax.psum(shard_sums[7].astype(jnp.bfloat16), "dp").astype(jnp.float32),
        lax.psum(shard_sums[8].astype(jnp.bfloat16), "dp").astype(jnp.float32),
        lax.psum(shard_sums[9].astype(jnp.bfloat16), "dp").astype(jnp.float32),
        lax.psum(shard_sums[10].astype(jnp.bfloat16), "dp").astype(jnp.float32),
        lax.psum(shard_sums[11].astype(jnp.bfloat16), "dp").astype(jnp.float32),
        lax.psum(shard_sums[12].astype(jnp.bfloat16), "dp").astype(jnp.float32),
        lax.psum(shard_sums[13].astype(jnp.bfloat16), "dp").astype(jnp.float32),
        lax.psum(shard_sums[14].astype(jnp.bfloat16), "dp").astype(jnp.float32),
    )
    bias_total = lax.psum(grad_class_bias, ("dp", "fsdp"))
    return (
        result.astype(jnp.bfloat16),
        input_grad,
        summed[0],
        summed[1],
        summed[2],
        summed[3],
        summed[4],
        summed[5],
        summed[6],
        summed[7],
        summed[8],
        summed[9],
        summed[10],
        summed[11],
        summed[12],
        summed[13],
        summed[14],
        bias_total,
    )


def solution(mesh):
    in_specs = (
        P(("dp", "fsdp"), None),
        P("fsdp", None),
        P("fsdp"),
        P("fsdp", None),
        P("fsdp"),
        P("fsdp"),
        P("fsdp"),
        P("fsdp", None),
        P("fsdp"),
        P("fsdp", None),
        P("fsdp"),
        P("fsdp"),
        P("fsdp"),
        P("fsdp", None),
        P("fsdp"),
        P("fsdp", None),
        P(),
        P(("dp", "fsdp")),
        P(("dp", "fsdp")),
        P(("dp", "fsdp"), None),
    )
    out_specs = (
        P(("dp", "fsdp"), None),
        P(("dp", "fsdp"), None),
        P("fsdp", None),
        P("fsdp"),
        P("fsdp", None),
        P("fsdp"),
        P("fsdp"),
        P("fsdp"),
        P("fsdp", None),
        P("fsdp"),
        P("fsdp", None),
        P("fsdp"),
        P("fsdp"),
        P("fsdp"),
        P("fsdp", None),
        P("fsdp"),
        P("fsdp", None),
        P(),
    )
    dp_size, fsdp_size = mesh.shape["dp"], mesh.shape["fsdp"]
    body = partial(kernel_body, fsdp_size) if (dp_size, fsdp_size) == (4, 8) else plain_body
    return jax.shard_map(body, mesh=mesh, in_specs=in_specs, out_specs=out_specs, check_vma=False)
```
